256 devices in a mesh: seq: 32 (over y, x, core), expert: 8 (over z).
Axes of the slice: x: 4, y: 4, z: 8, core: 2. Of those that a mesh axis runs over, the one named last changes fastest.
Arguments:
- layer_input: bfloat16 [2048, 2, 4096], P(('seq', 'expert')), may hold values from -6 to 6
- x_branch: bfloat16 [2048, 2, 4096], P('seq', None, 'expert'), may hold values from -24 to 24
- gate_branch: bfloat16 [2048, 2, 4096], P('seq', None, 'expert'), may hold values from -6 to 6
- conv_weight: bfloat16 [4, 4096], P(None, 'expert'), may hold values from -3 to 3
- conv_bias: bfloat16 [4096], P('expert'), may hold values from -3 to 3
- x_proj: bfloat16 [4096, 288], P('expert'), may hold values from -0.09375 to 0.09375
- dt_proj: bfloat16 [256, 4096], P(None, 'expert'), may hold values from -0.375 to 0.375
- dt_bias: float32 [4096], P('expert'), may hold values from -5.5 to -2
- a_log: float32 [4096, 16], P('expert'), may hold values from -7 to 2.77
- d_skip: float32 [4096], P('expert'), may hold values from 0.5 to 1.5
- carry_state: float32 [2, 4096, 16], P(None, 'expert'), may hold values from -3 to 3
- carry_tail: bfloat16 [3, 2, 4096], P(None, None, 'expert'), may hold values from -6 to 6
- out_proj: bfloat16 [4096, 4096], P('expert'), may hold values from -0.09375 to 0.09375
- steering: bfloat16 [4096], replicated, may hold values from -6 to 6
- refusal: bfloat16 [4, 4096], replicated, may hold values from -6 to 6
- norm_gain: bfloat16 [4096], replicated, may hold values from 0.5 to 1.5
- router: bfloat16 [4096, 8], replicated, may hold values from -0.09375 to 0.09375
- specialist_switch_matrix: bfloat16 [8, 4096, 8192], P('expert', None, 'seq'), may hold values from -0.09375 to 0.09375
- w_up: bfloat16 [8, 4096, 8192], P('expert', None, 'seq'), may hold values from -0.09375 to 0.09375
- w_down: bfloat16 [8, 8192, 4096], P('expert', 'seq'), may hold values from -0.0625 to 0.0625
- expert_ids: int32 [2048, 2, 2], P('seq'), may hold values from 0 to 7, all different within a row; in each aligned block of 128 rows (0 to 127, 128 to 255, ..., all dimensions but the last counted through in order) at most 40 rows name the same one
Outputs:
- layer_out: float32 [2048, 2, 4096], P(('seq', 'expert'))
The draws below stay inside these ranges and needn't reach their ends.
Inputs may be any that keep to these rules, and one draw needn't show every extreme that they name: `expert_ids`: in every aligned block of 128 rows in position-major order (the tokens of one seq index), no expert is named by more than 40 tokens, and in some block an expert is named by exactly 40; the two experts of a token differ.
All inputs are finite; a program needn't handle non-finite values.
Results may differ from the reference program's by a relative error of at most 0.0044.
Values may be sent and summed in bfloat16 or wider, within the bound.
No kernel may reach another device: no remote copies, remote signals or barrier semaphores. Data moves between devices by JAX's collectives and lax.ppermute only.
A program may use at most 128 MiB of HBM per device.

```python
import math
import jax
import jax.numpy as jnp
import numpy as np
from jax import lax

D = 4096
ECH = 4096
NST = 16
KCONV = 4
RANK = 256
DIRS = 4
TOP = 2
FF_DEV = 256
PROMPTS = 2
TOK_SEQ = 64
EXPERTS = 8
FF = 8192
LEN = 2048
MOST = 40
N_SEQ = 32


def draw_x_branch(key, part):
    base_key, selection_key = jax.random.split(jax.random.fold_in(key, 11))
    specialist_choices = jax.random.randint(selection_key, (6,), 0, LEN)
    word_locations = jnp.arange(LEN)
    word_group_run = jnp.any(word_locations[:, None] == specialist_choices[None, :], axis=1)
    multiplier_value = jnp.where(word_group_run, 4.0, 1.0).astype(jnp.float32)
    base = jnp.clip(jax.random.normal(base_key, (LEN, PROMPTS, ECH), jnp.float32), -6.0, 6.0)
    return (base * multiplier_value[:, None, None]).astype(jnp.bfloat16)


def draw_dt_bias(key, part):
    uniform_draw = jax.random.uniform(jax.random.fold_in(key, 23), (ECH,), jnp.float32)
    lower, upper = (0.01, 0.1)
    initial = jnp.exp(jnp.log(lower) + uniform_draw * (jnp.log(upper) - jnp.log(lower)))
    return (initial + jnp.log(-jnp.expm1(-initial))).astype(jnp.float32)


def levels(own_key, dims, cuts, smallest, top_value):
    gain, own = 1.0, jax.random.fold_in(own_key, 6)
    for dim, blocks in cuts:
        draws = jnp.exp(jax.random.uniform(jax.random.fold_in(own, dim), (blocks,), jnp.float32, smallest / len(cuts), top_value / len(cuts)))
        gain = gain * jnp.repeat(draws, dims[dim] // blocks).reshape([-1 if axis == dim else 1 for axis in range(len(dims))])
    return gain


def assign_block(stream_key, own, number, rows, count, top, reach, slope):
    ranking = jax.random.permutation(stream_key, count)
    heavy_load, common = load_shares(count, rows * top, reach, slope, True), load_shares(count, rows * top, reach, slope, False)
    places = jnp.arange(count)

    def named(sizes, turn):
        used = int((sizes > 0).sum())
        fixed = max(1, used // 4)
        shifted = fixed + (places - fixed + turn * (used - fixed)) % max(1, count - fixed)
        return jnp.zeros((count,), jnp.int32).at[ranking[jnp.where(places < fixed, places, shifted)]].set(jnp.asarray(sizes, jnp.int32))

    sizes = jnp.where(number % 4 == 0, named(heavy_load, number // 4), named(common, number - number // 4 - 1))
    mixed = jax.random.permutation(jax.random.fold_in(own, 3), count)
    giver, taker = mixed[0:count // 2 * 2:2], mixed[1:count // 2 * 2:2]
    margin = jnp.minimum(sizes[giver] - 1, reach - sizes[taker]) // 2
    margin = jnp.where((giver == ranking[0]) | (taker == ranking[0]) | (sizes[taker] == 0), 0, jnp.maximum(margin, 0))
    shifted = jax.random.randint(jax.random.fold_in(own, 4), (count // 2,), 0, 1 << 20) % (margin + 1)
    sizes = sizes.at[giver].add(-shifted).at[taker].add(shifted)
    labels = jnp.searchsorted(jnp.cumsum(sizes), jnp.arange(rows * top), side="right").astype(jnp.int32)
    grid = labels.reshape(top, rows).T
    grid = grid[jax.random.permutation(jax.random.fold_in(own, 1), rows)]
    turn = jax.random.randint(jax.random.fold_in(own, 2), (rows, 1), 0, top)
    return jnp.take_along_axis(grid, (jnp.arange(top)[None, :] + turn) % top, axis=1)


def load_shares(count, total, bound, skew, full):
    portions = [(1 << 20) // math.isqrt(grade ** skew) + 1 for grade in range(1, count + 1)]
    largest = bound if full else min(bound, max(-(-total // count), total * portions[0] // sum(portions)))
    least = 1 if total - largest >= count - 1 else 0
    counts, surplus = [largest] + [least] * (count - 1), total - largest - least * (count - 1)
    while surplus > 0:
        candidates = [i for i in range(1, count) if counts[i] < largest] or [i for i in range(1, count) if counts[i] < bound]
        pool, budget = sum([portions[i] for i in candidates]), surplus
        for i in candidates:
            more = min(bound - counts[i], max(1, budget * portions[i] // pool), surplus)
            counts[i] = counts[i] + more
            surplus = surplus - more
    return np.array(counts)


def scatter_about(key, dims, spread, most, cuts=(), held_as=jnp.bfloat16):
    drawn = jax.random.normal(key, dims, jnp.float32) * spread
    if len(cuts) > 0:
        drawn = levels(key, dims, cuts, -0.22, 0.18) * drawn
    return jnp.clip(drawn, min=-most, max=most).astype(held_as)


def setup_inputs(seed: int = 0) -> dict:
    key_list = jax.random.split(jax.random.key(seed), 22)
    layer_input = scatter_about(key_list[0], (LEN, PROMPTS, D), 1.0, 6.0, ((0, 256),))
    x_branch = draw_x_branch(jax.random.fold_in(key_list[21], 71), 0)
    gate_branch = scatter_about(key_list[2], (LEN, PROMPTS, ECH), 1.0, 6.0, ((0, 32), (2, 8)))
    conv_weight = scatter_about(key_list[3], (KCONV, ECH), KCONV ** -0.5, 3.0, ((1, 8),))
    conv_bias = scatter_about(key_list[4], (ECH,), 0.5, 3.0, ((0, 8),))
    x_proj = scatter_about(key_list[5], (ECH, RANK + 2 * NST), ECH ** -0.5, 0.09375, ((0, 8),))
    dt_proj = scatter_about(key_list[6], (RANK, ECH), RANK ** -0.5, 0.375, ((1, 8),))
    dt_bias = draw_dt_bias(jax.random.fold_in(key_list[21], 71), 0)
    a_log = jnp.clip(-7.0 + 9.77 * jax.random.uniform(key_list[8], (ECH, NST), jnp.float32) ** levels(key_list[8], (ECH, NST), ((0, 8),), -0.2, 0.2), -7.0, 2.77)
    d_skip = jnp.clip(0.5 + 1.0 * jax.random.uniform(key_list[9], (ECH,), jnp.float32) ** levels(key_list[9], (ECH,), ((0, 8),), -0.2, 0.2), 0.5, 1.5)
    carry_state = scatter_about(key_list[10], (PROMPTS, ECH, NST), 0.5, 3.0, ((1, 8),), jnp.float32)
    carry_tail = scatter_about(key_list[11], (KCONV - 1, PROMPTS, ECH), 1.0, 6.0, ((2, 8),))
    out_proj = scatter_about(key_list[12], (ECH, D), ECH ** -0.5, 0.09375, ((0, 8),))
    steering = scatter_about(key_list[13], (D,), 1.0, 6.0)
    refusal = scatter_about(key_list[14], (DIRS, D), 1.0, 6.0)
    norm_gain = jnp.clip(1.0 + 0.1 * jax.random.normal(key_list[15], (D,), jnp.float32), 0.5, 1.5).astype(jnp.bfloat16)
    router = scatter_about(key_list[16], (D, EXPERTS), D ** -0.5, 0.09375)
    specialist_switch_matrix = scatter_about(key_list[17], (EXPERTS, D, FF), D ** -0.5, 0.09375, ((0, 8), (2, 32)))
    w_up = scatter_about(key_list[18], (EXPERTS, D, FF), D ** -0.5, 0.09375, ((0, 8), (2, 32)))
    w_down = scatter_about(key_list[19], (EXPERTS, FF, D), FF ** -0.5, 0.0625, ((0, 8), (1, 32)))
    expert_ids_keys = jax.random.split(jax.random.fold_in(key_list[20], 1), LEN * PROMPTS // (TOK_SEQ * PROMPTS))
    expert_ids_turns = jax.random.permutation(jax.random.fold_in(key_list[20], 3), LEN * PROMPTS // (TOK_SEQ * PROMPTS))
    expert_ids = jax.vmap(lambda own, number: assign_block(jax.random.fold_in(key_list[20], 2), own, number, TOK_SEQ * PROMPTS, EXPERTS, TOP, MOST, 1))(expert_ids_keys, expert_ids_turns).reshape((LEN, PROMPTS, TOP))
    return dict(layer_input=layer_input, x_branch=x_branch, gate_branch=gate_branch, conv_weight=conv_weight, conv_bias=conv_bias, x_proj=x_proj, dt_proj=dt_proj, dt_bias=dt_bias, a_log=a_log, d_skip=d_skip, carry_state=carry_state, carry_tail=carry_tail, out_proj=out_proj, steering=steering, refusal=refusal, norm_gain=norm_gain, router=router, specialist_switch_matrix=specialist_switch_matrix, w_up=w_up, w_down=w_down, expert_ids=expert_ids)


EPS = 1e-06

def remove_directions(steering, refusal):
    vector = steering.astype(jnp.float32)
    units = []
    for k in range(DIRS):
        r = refusal[k].astype(jnp.float32)
        for q in units:
            r = r - jnp.sum(q * r) * q
        r = r * lax.rsqrt(jnp.sum(r * r) + EPS)
        units.append(r)
    for q in units:
        vector = vector - jnp.sum(q * vector) * q
    return vector

def route_weights(normed, router, picked_indices):
    logits = jnp.dot(normed, router, preferred_element_type=jnp.float32)
    onehot = (picked_indices[:, :, None] == jnp.arange(EXPERTS, dtype=jnp.int32)[None, None, :]).astype(jnp.float32)
    picked = lax.optimization_barrier(jnp.sum(onehot * logits[:, None, :], axis=-1))
    leading = jax.nn.sigmoid(picked[:, 0] - picked[:, 1])
    shares = jnp.stack([leading, 1.0 - leading], axis=1)
    return lax.optimization_barrier(jnp.sum(onehot * shares[:, :, None], axis=1))

def reference(layer_input, x_branch, gate_branch, conv_weight, conv_bias, x_proj, dt_proj, dt_bias, a_log, d_skip, carry_state, carry_tail, out_proj, steering, refusal, norm_gain, router, specialist_switch_matrix, w_up, w_down, expert_ids):
    padded = jnp.concatenate([carry_tail, x_branch], axis=0).astype(jnp.float32)
    convolved = conv_bias.astype(jnp.float32)
    for k in range(KCONV):
        convolved = convolved + conv_weight[k].astype(jnp.float32) * padded[k:k + LEN]
    activated = jax.nn.silu(convolved)
    row_count = LEN * PROMPTS
    projected = jnp.dot(activated.astype(jnp.bfloat16).reshape(row_count, ECH), x_proj, preferred_element_type=jnp.float32)
    low = projected[:, :RANK].astype(jnp.bfloat16)
    input_matrix_b = projected[:, RANK:RANK + NST].reshape(LEN, PROMPTS, NST)
    c_output = projected[:, RANK + NST:].reshape(LEN, PROMPTS, NST)
    step_size = jax.nn.softplus(jnp.dot(low, dt_proj, preferred_element_type=jnp.float32) + dt_bias).reshape(LEN, PROMPTS, ECH)
    rate = -jnp.exp(a_log)

    def advance(carried, inputs):
        current_increment, act_now, b_now, c_now = inputs
        decays = jnp.exp(current_increment[:, :, None] * rate[None])
        carried = decays * carried + (current_increment * act_now)[:, :, None] * b_now[:, None, :]
        return (carried, lax.optimization_barrier(jnp.sum(carried * c_now[:, None, :], axis=-1)))
    _, scanned = lax.scan(advance, carry_state, (step_size, activated, input_matrix_b, c_output))
    output_y = scanned + d_skip * activated
    gated = (output_y * jax.nn.silu(gate_branch.astype(jnp.float32))).astype(jnp.bfloat16)
    mixed = jnp.dot(gated.reshape(row_count, ECH), out_proj, preferred_element_type=jnp.float32)
    steering_clean = remove_directions(steering, refusal)
    residual = layer_input.astype(jnp.float32).reshape(row_count, D) + mixed + steering_clean
    normed = (residual * lax.rsqrt(lax.optimization_barrier(jnp.mean(residual * residual, axis=-1, keepdims=True)) + EPS) * norm_gain.astype(jnp.float32)).astype(jnp.bfloat16)
    row_ids = expert_ids.reshape(row_count, TOP)
    weights = route_weights(normed, router, row_ids)
    capacity = N_SEQ * MOST

    def per_expert(total, items):
        expert_slot, gate_w, up_w, down_w = items
        member = jnp.any(row_ids == expert_slot, axis=1)
        count = jnp.sum(member.astype(jnp.int32))
        slot_index = jnp.nonzero(member, size=capacity, fill_value=0)[0].astype(jnp.int32)
        valid = (jnp.arange(capacity, dtype=jnp.int32) < count).astype(jnp.float32)
        inputs = normed[slot_index]
        gate = jnp.dot(inputs, gate_w, preferred_element_type=jnp.float32)
        upward = jnp.dot(inputs, up_w, preferred_element_type=jnp.float32)
        hidden = (jax.nn.silu(gate) * upward).astype(jnp.bfloat16)
        shards = hidden.reshape(capacity, N_SEQ, FF_DEV).transpose(1, 0, 2)
        downs = down_w.reshape(N_SEQ, FF_DEV, D)

        def add_shard(accum, pair):
            partial_out = jnp.dot(pair[0], pair[1], preferred_element_type=jnp.float32).astype(jnp.bfloat16)
            partial_out = lax.optimization_barrier(partial_out)
            return (accum + partial_out.astype(jnp.float32), None)
        expert_out, _ = lax.scan(add_shard, jnp.zeros((capacity, D), jnp.float32), (shards, downs))
        column = (jnp.arange(EXPERTS, dtype=jnp.int32) == expert_slot).astype(jnp.float32)
        share = lax.optimization_barrier(jnp.sum(weights[slot_index] * column[None, :], axis=1)) * valid
        total = total.at[slot_index].add(expert_out * share[:, None])
        return (total, None)
    moe_total, _ = lax.scan(per_expert, jnp.zeros((row_count, D), jnp.float32), (jnp.arange(EXPERTS, dtype=jnp.int32), specialist_switch_matrix, w_up, w_down))
    return (residual + moe_total).reshape(LEN, PROMPTS, D)
```

```python
import functools

import jax
import jax.numpy as jnp
from jax import lax
from jax.experimental import pallas as pl
from jax.experimental.pallas import tpu as pltpu
from jax.sharding import PartitionSpec as P

EPS = 1e-06
LOG2E = 1.4426950408889634
F32 = jnp.float32
BF16 = jnp.bfloat16
WIDE = pltpu.CompilerParams(vmem_limit_bytes=40 * 1024 * 1024)


def silu(v):
    return v * jax.nn.sigmoid(v)


def dot(a, b):
    return jnp.dot(a, b, preferred_element_type=F32)


def exchanged(blocks, axis, groups=None):
    return lax.all_to_all(blocks, axis, 0, 0, tiled=True, axis_index_groups=groups)


def conv_kernel(lead_ref, x_ref, got_ref, carry_ref, w_ref, b_ref, xp_ref, act_ref, part_ref, pad_ref):
    rows = x_ref.shape[0]
    taps = w_ref.shape[0]
    halo = got_ref.shape[0]
    step = halo // (taps - 1)
    first = lead_ref[0] == 0
    pad_ref[:halo, :] = jnp.where(first, carry_ref[...].astype(F32), got_ref[...].astype(F32))
    pad_ref[halo : halo + rows, :] = x_ref[...].astype(F32)
    total = b_ref[...].astype(F32)
    w = w_ref[...].astype(F32)
    for k in range(taps):
        total = total + w[k : k + 1, :] * pad_ref[k * step : k * step + rows, :]
    act = silu(total)
    act_ref[...] = act
    part_ref[...] = dot(act.astype(BF16), xp_ref[...])


def advance(state, rate, step, drive, b):
    return jnp.exp2(step * rate) * state + drive * b


def local_kernel(prompts, proj_ref, dtp_ref, dtb_ref, act_ref, bc_ref, alog_ref, step_ref, out_ref):
    rows, channels = act_ref.shape
    states = alog_ref.shape[0]
    rank = dtp_ref.shape[0]
    low = proj_ref[:, :rank].astype(BF16)
    step_ref[...] = jax.nn.softplus(dot(low, dtp_ref[...]) + dtb_ref[...])
    rate = -jnp.exp(alog_ref[...]) * LOG2E

    def body(i, carried):
        carried = list(carried)
        at = pl.multiple_of(i * 8, 8)
        step = step_ref[pl.ds(at, 8), :]
        drive = step * act_ref[pl.ds(at, 8), :]
        for r in range(8):
            p = r % prompts
            b = jnp.tile(bc_ref[at + r, :states, :], (1, channels // 128))
            carried[p] = advance(carried[p], rate, step[r : r + 1, :], drive[r : r + 1, :], b)
        return tuple(carried)

    zero = jnp.zeros((states, channels), F32)
    ends = lax.fori_loop(0, rows // 8, body, (zero,) * prompts)
    for p in range(prompts):
        out_ref[p * states : (p + 1) * states, :] = ends[p].astype(BF16)
    step = step_ref[...].reshape(rows // 8, 8, channels).sum(axis=0)
    sums = [sum(step[r : r + 1, :] for r in range(p, 8, prompts)) for p in range(prompts)]
    high = [s.astype(BF16).astype(F32) for s in sums]
    low_part = [(s - h) for s, h in zip(sums, high)]
    rest = jnp.zeros((8 - 2 * prompts, channels), F32)
    out_ref[prompts * states :, :] = jnp.concatenate(high + low_part + [rest], axis=0).astype(BF16)


def scan_kernel(
    prompts, ids_ref, all_ref, carry_ref, step_ref, act_ref, bc_ref, alog_ref, skip_ref, gate_ref, own_ref,
    outp_ref, mixed_ref, y_ref, w_ref, sem,
):
    rows, channels = act_ref.shape
    states = alog_ref.shape[0]
    copy = pltpu.make_async_copy(outp_ref, w_ref, sem)
    copy.start()
    rate = -jnp.exp(alog_ref[...]) * LOG2E

    def earlier(j, carried):
        block = all_ref[j].astype(F32)
        at = prompts * states
        out = []
        for p in range(prompts):
            total = block[at + p : at + p + 1, :] + block[at + prompts + p : at + prompts + p + 1, :]
            out.append(jnp.exp2(total * rate) * carried[p] + block[p * states : (p + 1) * states, :])
        return tuple(out)

    entering = lax.fori_loop(0, ids_ref[0], earlier, tuple(carry_ref[p] for p in range(prompts)))

    def body(i, carried):
        carried = list(carried)
        at = pl.multiple_of(i * 8, 8)
        step = step_ref[pl.ds(at, 8), :]
        drive = step * act_ref[pl.ds(at, 8), :]
        outs = []
        for r in range(8):
            p = r % prompts
            bc = bc_ref[at + r]
            b = jnp.tile(bc[:states], (1, channels // 128))
            c = jnp.tile(bc[states:], (1, channels // 128))
            carried[p] = advance(carried[p], rate, step[r : r + 1, :], drive[r : r + 1, :], b)
            outs.append(jnp.sum(carried[p] * c, axis=0, keepdims=True))
        y_ref[pl.ds(at, 8), :] = jnp.concatenate(outs, axis=0)
        return tuple(carried)

    lax.fori_loop(0, rows // 8, body, entering)
    y = y_ref[...] + skip_ref[...] * act_ref[...]
    gated = (y * silu(gate_ref[...].astype(F32))).astype(BF16)
    copy.wait()
    blocks, _, width = mixed_ref.shape
    own_rows = own_ref.shape[0]
    row_group = lax.broadcasted_iota(jnp.int32, (rows, width), 0) // own_rows
    mine = row_group == ids_ref[1]
    for j in range(blocks):
        part = dot(gated, w_ref[:, j * width : (j + 1) * width])
        own = jnp.tile(own_ref[:, j * width : (j + 1) * width].astype(F32), (rows // own_rows, 1))
        mixed_ref[j] = (part + jnp.where(mine, own, 0.0)).astype(BF16)


def clean_kernel(steer_ref, refusal_ref, out_ref):
    vector = steer_ref[...].astype(F32)
    units = []
    for k in range(refusal_ref.shape[0]):
        r = refusal_ref[k].astype(F32)
        for q in units:
            r = r - jnp.sum(q * r) * q
        r = r * lax.rsqrt(jnp.sum(r * r) + EPS)
        units.append(r)
    for q in units:
        vector = vector - jnp.sum(q * vector) * q
    out_ref[...] = vector


def dispatch_kernel(mixed_ref, clean_ref, gain_ref, lanes_ref, res_ref, send_ref, slots_ref):
    experts, capacity, rows = slots_ref.shape
    width = res_ref.shape[1]
    residual = clean_ref[...]
    for j in range(mixed_ref.shape[0]):
        residual = residual + mixed_ref[j].astype(F32)
    res_ref[...] = residual
    scaled = (residual * gain_ref[...].astype(F32)).astype(BF16)
    square = jnp.sum(residual * residual, axis=1, keepdims=True)
    high = square.astype(BF16).astype(F32)
    middle = (square - high).astype(BF16).astype(F32)
    low = square - high - middle
    lane = lax.broadcasted_iota(jnp.int32, (rows, 128), 1)
    extra = jnp.where(lane == 0, high, jnp.where(lane == 1, middle, jnp.where(lane == 2, low, 0.0)))
    payload = jnp.concatenate([scaled, extra.astype(BF16)], axis=1)
    label = lax.broadcasted_iota(jnp.int32, (experts, rows), 0)
    member = (lanes_ref[0:1, :] == label) | (lanes_ref[1:2, :] == label)
    upper = lax.broadcasted_iota(jnp.int32, (rows, rows), 0) <= lax.broadcasted_iota(jnp.int32, (rows, rows), 1)
    order = dot(member.astype(F32).astype(BF16), upper.astype(F32).astype(BF16))
    place = jnp.where(member, order - 1.0, -1.0)
    slot = lax.broadcasted_iota(jnp.int32, (capacity, rows), 0).astype(F32)
    for e in range(experts):
        chosen = (place[e : e + 1, :] == slot).astype(F32).astype(BF16)
        slots_ref[e] = chosen
        send_ref[e] = dot(chosen, payload).astype(BF16)


def normed_kernel(features, got_ref, out_ref):
    width = out_ref.shape[1] // got_ref.shape[0]
    total = jnp.zeros((out_ref.shape[0], 128), F32)
    for j in range(got_ref.shape[0]):
        total = total + got_ref[j, :, width:].astype(F32)
    scale = lax.rsqrt(jnp.sum(total, axis=1, keepdims=True) / features + EPS)
    for j in range(got_ref.shape[0]):
        out_ref[:, j * width : (j + 1) * width] = (got_ref[j, :, :width].astype(F32) * scale).astype(BF16)


def share_kernel(owner_ref, x_ref, router_ref, slots_ref, rows_ref, out_ref):
    logits = lax.dot_general(x_ref[...], router_ref[...], (((1,), (1,)), ((), ())), preferred_element_type=F32)
    experts = router_ref.shape[0]
    rows = rows_ref.shape[0]
    label = lax.broadcasted_iota(jnp.int32, (rows, experts), 1)
    member = (rows_ref[:, 0:1] == label) | (rows_ref[:, 1:2] == label)
    both = dot(slots_ref[owner_ref[0]], member.astype(F32).astype(BF16))
    own = (lax.broadcasted_iota(jnp.int32, both.shape, 1) == owner_ref[0]).astype(F32) * both
    gap = jnp.sum(logits * (2.0 * own - both), axis=1, keepdims=True)
    out_ref[...] = jnp.broadcast_to(jax.nn.sigmoid(gap), out_ref.shape)


def weigh_kernel(got_ref, share_ref, out_ref):
    total = got_ref[0].astype(F32)
    for i in range(1, got_ref.shape[0]):
        total = total + got_ref[i].astype(F32)
    out_ref[0] = (total * share_ref[:, :1]).astype(BF16)


def combine_kernel(res_ref, got_ref, slots_ref, out_ref):
    total = res_ref[...]
    for e in range(got_ref.shape[0]):
        total = total + lax.dot_general(
            slots_ref[e], got_ref[e], (((0,), (0,)), ((), ())), preferred_element_type=F32
        )
    out_ref[...] = total


def shape(dims, dtype=F32):
    return jax.ShapeDtypeStruct(dims, dtype)


SCALAR = pl.BlockSpec(memory_space=pltpu.SMEM)
VM = pl.BlockSpec(memory_space=pltpu.VMEM)


def call(kernel, outs, specs, scratch=(), name=None):
    return pl.pallas_call(
        kernel, out_shape=outs, in_specs=specs, scratch_shapes=list(scratch), compiler_params=WIDE, name=name
    )


def shards(
    layer_input, x_branch, gate_branch, conv_weight, conv_bias, x_proj, dt_proj, dt_bias, a_log, d_skip, carry_state,
    carry_tail, out_proj, steering, refusal, norm_gain, router, specialist_switch_matrix, w_up, w_down, expert_ids,
):
    taps = conv_weight.shape[0]
    length, prompts, channels = x_branch.shape
    rows = length * prompts
    states = a_log.shape[1]
    rank = dt_proj.shape[0]
    d_model = out_proj.shape[1]
    experts = router.shape[1]
    top_count = expert_ids.shape[-1]
    capacity = rows * top_count * 5 // (4 * experts)
    n_seq = lax.axis_size("seq")
    groups = lax.axis_size("expert")
    width = d_model // groups
    own_rows = rows // groups
    place = lax.axis_index("seq").astype(jnp.int32)
    owner = lax.axis_index("expert").astype(jnp.int32)

    swap = [(i, i ^ 1) for i in range(n_seq)]
    gate_w, up_w, down_w = specialist_switch_matrix[0], w_up[0], w_down[0]
    gate_o, up_o, down_o = (lax.ppermute(w, "seq", swap) for w in (gate_w, up_w, down_w))

    halo = (taps - 1) * prompts
    x_rows = x_branch.reshape(rows, channels)
    received = lax.ppermute(x_rows[rows - halo :], "seq", [(i, i + 1) for i in range(n_seq - 1)])
    activated, part = call(
        conv_kernel,
        (shape((rows, channels)), shape((rows, x_proj.shape[1]))),
        [SCALAR] + [VM] * 6,
        [pltpu.VMEM((rows + 8, channels), F32)],
        name="conv",
    )(place[None], x_rows, received, carry_tail.reshape(halo, channels), conv_weight, conv_bias[None], x_proj)
    summed = exchanged(part, "expert").reshape(groups, own_rows, part.shape[1]).sum(axis=0)
    projected = exchanged(jnp.tile(summed, (groups, 1)), "expert")
    bc = jnp.broadcast_to(projected[:, rank:, None], (rows, 2 * states, 128))
    a_log_t = a_log.T
    step, ends = call(
        functools.partial(local_kernel, prompts),
        (shape((rows, channels)), shape((prompts * states + 8, channels), BF16)),
        [VM] * 6,
        name="local",
    )(projected, dt_proj, dt_bias[None], activated, bc, a_log_t)
    every = exchanged(jnp.broadcast_to(ends[None], (n_seq,) + ends.shape), "seq")
    mixed = call(
        functools.partial(scan_kernel, prompts),
        shape((groups, rows, width), BF16),
        [SCALAR] + [VM] * 9 + [pl.BlockSpec(memory_space=pl.ANY)],
        [pltpu.VMEM((rows, channels), F32), pltpu.VMEM((channels, d_model), BF16), pltpu.SemaphoreType.DMA],
        name="scan",
    )(
        jnp.stack([place, owner]), every, carry_state.transpose(0, 2, 1), step, activated, bc, a_log_t, d_skip[None],
        gate_branch.reshape(rows, channels), layer_input.reshape(own_rows, d_model), out_proj,
    )
    mixed = exchanged(mixed, "expert")

    clean = call(clean_kernel, shape((d_model // 128, 128)), [VM] * 2, name="clean")(
        steering.reshape(-1, 128), refusal.reshape(refusal.shape[0], -1, 128)
    )
    start = owner * width
    ids = expert_ids.reshape(rows, top_count)
    residual, send, slots = call(
        dispatch_kernel,
        (
            shape((rows, width)),
            shape((experts, capacity, width + 128), BF16),
            shape((experts, capacity, rows), BF16),
        ),
        [VM] * 4,
        name="dispatch",
    )(
        mixed,
        lax.dynamic_slice_in_dim(clean.reshape(1, d_model), start, width, 1),
        lax.dynamic_slice_in_dim(norm_gain[None], start, width, 1),
        ids.T,
    )
    got = exchanged(send, "expert")
    normed = call(
        functools.partial(normed_kernel, float(d_model)), shape((capacity, d_model), BF16), [VM], name="normed"
    )(got)

    same_core = [[i for i in range(n_seq) if i % 2 == c] for c in range(2)]
    pieces = lax.all_gather(normed, "seq", axis=0, tiled=True, axis_index_groups=same_core)
    share = call(share_kernel, shape((capacity, 128)), [SCALAR] + [VM] * 4, name="share")(
        owner[None], normed, router.T, slots, ids
    )
    gate = dot(pieces, jnp.concatenate([gate_w, gate_o], axis=1))
    upward = dot(pieces, jnp.concatenate([up_w, up_o], axis=1))
    hidden = (jax.nn.silu(gate) * upward).astype(BF16)
    partial = dot(hidden, jnp.concatenate([down_w, down_o], axis=0)).astype(BF16)
    partial = exchanged(partial, "seq", same_core).reshape(n_seq // 2, capacity, d_model)
    weighted = pl.pallas_call(
        weigh_kernel,
        grid=(groups,),
        out_shape=shape((groups, capacity, width), BF16),
        in_specs=[
            pl.BlockSpec((n_seq // 2, capacity, width), lambda j: (0, 0, j)),
            pl.BlockSpec((capacity, 128), lambda j: (0, 0)),
        ],
        out_specs=pl.BlockSpec((1, capacity, width), lambda j: (j, 0, 0)),
        compiler_params=WIDE,
        name="weigh",
    )(partial, share)
    back = exchanged(weighted, "expert")
    total = call(combine_kernel, shape((rows, width)), [VM] * 3, name="combine")(residual, back, slots)
    out = exchanged(total, "expert").reshape(groups, own_rows, width)
    return out.transpose(1, 0, 2).reshape(own_rows // prompts, prompts, d_model)


def solution(mesh):
    return jax.shard_map(
        shards,
        mesh=mesh,
        in_specs=(
            P(("seq", "expert"), None, None),
            P("seq", None, "expert"),
            P("seq", None, "expert"),
            P(None, "expert"),
            P("expert"),
            P("expert", None),
            P(None, "expert"),
            P("expert"),
            P("expert", None),
            P("expert"),
            P(None, "expert", None),
            P(None, None, "expert"),
            P("expert", None),
            P(),
            P(),
            P(),
            P(),
            P("expert", None, "seq"),
            P("expert", None, "seq"),
            P("expert", "seq", None),
            P("seq", None, None),
        ),
        out_specs=P(("seq", "expert"), None, None),
        check_vma=False,
    )
```

```python
import functools

import jax
import jax.numpy as jnp
from jax import lax
from jax.experimental import pallas as pl
from jax.experimental.pallas import tpu as pltpu
from jax.sharding import PartitionSpec as P

EPS = 1e-06
LOG2E = 1.4426950408889634
F32 = jnp.float32
BF16 = jnp.bfloat16
WIDE = pltpu.CompilerParams(vmem_limit_bytes=40 * 1024 * 1024)


def silu(v):
    return v * jax.nn.sigmoid(v)


def dot(a, b):
    return jnp.dot(a, b, preferred_element_type=F32)


def fence(*values):
    return lax.optimization_barrier(values)


def exchanged(blocks, axis, groups=None):
    return lax.all_to_all(blocks, axis, 0, 0, tiled=True, axis_index_groups=groups)


def conv_kernel(lead_ref, x_ref, got_ref, carry_ref, w_ref, b_ref, xp_ref, act_ref, part_ref, pad_ref):
    rows = x_ref.shape[0]
    taps = w_ref.shape[0]
    halo = got_ref.shape[0]
    step = halo // (taps - 1)
    first = lead_ref[0] == 0
    pad_ref[:halo, :] = jnp.where(first, carry_ref[...].astype(F32), got_ref[...].astype(F32))
    pad_ref[halo : halo + rows, :] = x_ref[...].astype(F32)
    total = b_ref[...].astype(F32)
    w = w_ref[...].astype(F32)
    for k in range(taps):
        total = total + w[k : k + 1, :] * pad_ref[k * step : k * step + rows, :]
    act = silu(total)
    act_ref[...] = act
    part_ref[...] = lax.dot_general(act.astype(BF16), xp_ref[...], (((1,), (1,)), ((), ())), preferred_element_type=F32)


def advance(state, rate, step, drive, b):
    return jnp.exp2(step * rate) * state + drive * b


def local_kernel(prompts, proj_ref, dtp_ref, dtb_ref, act_ref, bc_ref, alog_ref, step_ref, out_ref):
    rows, channels = act_ref.shape
    states = alog_ref.shape[0]
    rank = dtp_ref.shape[0]
    low = proj_ref[:, :rank].astype(BF16)
    step_ref[...] = jax.nn.softplus(dot(low, dtp_ref[...]) + dtb_ref[...])
    rate = -jnp.exp(alog_ref[...]) * LOG2E

    def body(i, carried):
        carried = list(carried)
        at = pl.multiple_of(i * 8, 8)
        step = step_ref[pl.ds(at, 8), :]
        drive = step * act_ref[pl.ds(at, 8), :]
        for r in range(8):
            p = r % prompts
            b = jnp.tile(bc_ref[at + r, :states, :], (1, channels // 128))
            carried[p] = advance(carried[p], rate, step[r : r + 1, :], drive[r : r + 1, :], b)
        return tuple(carried)

    zero = jnp.zeros((states, channels), F32)
    ends = lax.fori_loop(0, rows // 8, body, (zero,) * prompts)
    for p in range(prompts):
        out_ref[p * states : (p + 1) * states, :] = ends[p].astype(BF16)
    step = step_ref[...].reshape(rows // 8, 8, channels).sum(axis=0)
    sums = [sum(step[r : r + 1, :] for r in range(p, 8, prompts)) for p in range(prompts)]
    high = [s.astype(BF16).astype(F32) for s in sums]
    low_part = [(s - h) for s, h in zip(sums, high)]
    rest = jnp.zeros((8 - 2 * prompts, channels), F32)
    out_ref[prompts * states :, :] = jnp.concatenate(high + low_part + [rest], axis=0).astype(BF16)


def scan_kernel(
    prompts, ids_ref, all_ref, carry_ref, step_ref, act_ref, bc_ref, alog_ref, skip_ref, gate_ref, own_ref,
    outp_ref, mixed_ref, y_ref, w_ref, sem,
):
    rows, channels = act_ref.shape
    states = alog_ref.shape[0]
    copy = pltpu.make_async_copy(outp_ref, w_ref, sem)
    copy.start()
    rate = -jnp.exp(alog_ref[...]) * LOG2E

    def earlier(j, carried):
        block = all_ref[j].astype(F32)
        at = prompts * states
        out = []
        for p in range(prompts):
            total = block[at + p : at + p + 1, :] + block[at + prompts + p : at + prompts + p + 1, :]
            out.append(jnp.exp2(total * rate) * carried[p] + block[p * states : (p + 1) * states, :])
        return tuple(out)

    entering = lax.fori_loop(0, ids_ref[0], earlier, tuple(carry_ref[p] for p in range(prompts)))

    def body(i, carried):
        carried = list(carried)
        at = pl.multiple_of(i * 8, 8)
        step = step_ref[pl.ds(at, 8), :]
        drive = step * act_ref[pl.ds(at, 8), :]
        outs = []
        for r in range(8):
            p = r % prompts
            bc = bc_ref[at + r]
            b = jnp.tile(bc[:states], (1, channels // 128))
            c = jnp.tile(bc[states:], (1, channels // 128))
            carried[p] = advance(carried[p], rate, step[r : r + 1, :], drive[r : r + 1, :], b)
            outs.append(jnp.sum(carried[p] * c, axis=0, keepdims=True))
        y_ref[pl.ds(at, 8), :] = jnp.concatenate(outs, axis=0)
        return tuple(carried)

    lax.fori_loop(0, rows // 8, body, entering)
    y = y_ref[...] + skip_ref[...] * act_ref[...]
    gated = (y * silu(gate_ref[...].astype(F32))).astype(BF16)
    copy.wait()
    blocks, _, width = mixed_ref.shape
    own_rows = own_ref.shape[0]
    row_group = lax.broadcasted_iota(jnp.int32, (rows, width), 0) // own_rows
    mine = row_group == ids_ref[1]
    for j in range(blocks):
        part = dot(gated, w_ref[:, j * width : (j + 1) * width])
        own = jnp.tile(own_ref[:, j * width : (j + 1) * width].astype(F32), (rows // own_rows, 1))
        mixed_ref[j] = (part + jnp.where(mine, own, 0.0)).astype(BF16)


def clean_kernel(steer_ref, refusal_ref, out_ref):
    vector = steer_ref[...].astype(F32)
    units = []
    for k in range(refusal_ref.shape[0]):
        r = refusal_ref[k].astype(F32)
        for q in units:
            r = r - jnp.sum(q * r) * q
        r = r * lax.rsqrt(jnp.sum(r * r) + EPS)
        units.append(r)
    for q in units:
        vector = vector - jnp.sum(q * vector) * q
    out_ref[...] = vector


def dispatch_kernel(mixed_ref, clean_ref, gain_ref, lanes_ref, res_ref, send_ref, slots_ref):
    experts, capacity, rows = slots_ref.shape
    width = res_ref.shape[1]
    residual = clean_ref[...]
    for j in range(mixed_ref.shape[0]):
        residual = residual + mixed_ref[j].astype(F32)
    res_ref[...] = residual
    scaled = (residual * gain_ref[...].astype(F32)).astype(BF16)
    square = jnp.sum(residual * residual, axis=1, keepdims=True)
    high = square.astype(BF16).astype(F32)
    middle = (square - high).astype(BF16).astype(F32)
    low = square - high - middle
    lane = lax.broadcasted_iota(jnp.int32, (rows, 128), 1)
    extra = jnp.where(lane == 0, high, jnp.where(lane == 1, middle, jnp.where(lane == 2, low, 0.0)))
    payload = jnp.concatenate([scaled, extra.astype(BF16)], axis=1)
    label = lax.broadcasted_iota(jnp.int32, (experts, rows), 0)
    member = (lanes_ref[0:1, :] == label) | (lanes_ref[1:2, :] == label)
    upper = lax.broadcasted_iota(jnp.int32, (rows, rows), 0) <= lax.broadcasted_iota(jnp.int32, (rows, rows), 1)
    order = dot(member.astype(F32).astype(BF16), upper.astype(F32).astype(BF16))
    place = jnp.where(member, order - 1.0, -1.0)
    slot = lax.broadcasted_iota(jnp.int32, (capacity, rows), 0).astype(F32)
    for e in range(experts):
        chosen = (place[e : e + 1, :] == slot).astype(F32).astype(BF16)
        slots_ref[e] = chosen
        send_ref[e] = dot(chosen, payload).astype(BF16)


def normed_kernel(features, got_ref, out_ref):
    width = out_ref.shape[1] // got_ref.shape[0]
    total = jnp.zeros((out_ref.shape[0], 128), F32)
    for j in range(got_ref.shape[0]):
        total = total + got_ref[j, :, width:].astype(F32)
    scale = lax.rsqrt(jnp.sum(total, axis=1, keepdims=True) / features + EPS)
    for j in range(got_ref.shape[0]):
        out_ref[:, j * width : (j + 1) * width] = (got_ref[j, :, :width].astype(F32) * scale).astype(BF16)


def share_kernel(owner_ref, x_ref, router_ref, slots_ref, rows_ref, out_ref):
    logits = lax.dot_general(x_ref[...], router_ref[...], (((1,), (1,)), ((), ())), preferred_element_type=F32)
    experts = router_ref.shape[0]
    rows = rows_ref.shape[0]
    label = lax.broadcasted_iota(jnp.int32, (rows, experts), 1)
    member = (rows_ref[:, 0:1] == label) | (rows_ref[:, 1:2] == label)
    both = dot(slots_ref[owner_ref[0]], member.astype(F32).astype(BF16))
    own = (lax.broadcasted_iota(jnp.int32, both.shape, 1) == owner_ref[0]).astype(F32) * both
    gap = jnp.sum(logits * (2.0 * own - both), axis=1, keepdims=True)
    out_ref[...] = jnp.broadcast_to(jax.nn.sigmoid(gap), out_ref.shape)


def fetched(sources, held, sem):
    copies = [pltpu.make_async_copy(a, b, sem.at[i]) for i, (a, b) in enumerate(zip(sources, held))]
    for copy in copies:
        copy.start()
    return copies


def hidden_kernel(half_ref, x_ref, g0_ref, u0_ref, g1_ref, u1_ref, out_ref, g0, u0, g1, u1, sem):
    copies = fetched((g0_ref, u0_ref, g1_ref, u1_ref), (g0, u0, g1, u1), sem)
    x = x_ref[...]
    width = g0.shape[1]
    for k, (g, u) in enumerate(((g0, u0), (g1, u1))):
        copies[2 * k].wait()
        gate = dot(x, g[...])
        copies[2 * k + 1].wait()
        out_ref[:, k * width : (k + 1) * width] = (silu(gate) * dot(x, u[...])).astype(BF16)


def down_kernel(own_ref, far_ref, d0_ref, d1_ref, d2_ref, d3_ref, out_ref, d0, d1, d2, d3, sem):
    copies = fetched((d0_ref, d1_ref, d2_ref, d3_ref), (d0, d1, d2, d3), sem)
    width = d0.shape[0]
    hidden = [ref[:, k * width : (k + 1) * width] for ref in (own_ref, far_ref) for k in range(2)]
    for copy in copies:
        copy.wait()
    for j in range(0, out_ref.shape[1], 512):
        total = dot(hidden[0], d0[:, j : j + 512])
        for h, d in zip(hidden[1:], (d1, d2, d3)):
            total = total + dot(h, d[:, j : j + 512])
        out_ref[:, j : j + 512] = total.astype(BF16)


def weigh_kernel(got_ref, share_ref, out_ref):
    total = got_ref[0].astype(F32)
    for i in range(1, got_ref.shape[0]):
        total = total + got_ref[i].astype(F32)
    out_ref[0] = (total * share_ref[:, :1]).astype(BF16)


def combine_kernel(res_ref, got_ref, slots_ref, out_ref):
    total = res_ref[...]
    for e in range(got_ref.shape[0]):
        total = total + lax.dot_general(
            slots_ref[e], got_ref[e], (((0,), (0,)), ((), ())), preferred_element_type=F32
        )
    out_ref[...] = total


def shape(dims, dtype=F32):
    return jax.ShapeDtypeStruct(dims, dtype)


SCALAR = pl.BlockSpec(memory_space=pltpu.SMEM)
VM = pl.BlockSpec(memory_space=pltpu.VMEM)


def call(kernel, outs, specs, scratch=(), name=None):
    return pl.pallas_call(
        kernel, out_shape=outs, in_specs=specs, scratch_shapes=list(scratch), compiler_params=WIDE, name=name
    )


def shards(
    layer_input, x_branch, gate_branch, conv_weight, conv_bias, x_proj, dt_proj, dt_bias, a_log, d_skip, carry_state,
    carry_tail, out_proj, steering, refusal, norm_gain, router, specialist_switch_matrix, w_up, w_down, expert_ids,
):
    taps = conv_weight.shape[0]
    length, prompts, channels = x_branch.shape
    rows = length * prompts
    states = a_log.shape[1]
    rank = dt_proj.shape[0]
    d_model = out_proj.shape[1]
    experts = router.shape[1]
    top_count = expert_ids.shape[-1]
    capacity = rows * top_count * 5 // (4 * experts)
    n_seq = lax.axis_size("seq")
    groups = lax.axis_size("expert")
    width = d_model // groups
    own_rows = rows // groups
    place = lax.axis_index("seq").astype(jnp.int32)
    owner = lax.axis_index("expert").astype(jnp.int32)

    near, across = ([(i, i ^ d) for i in range(n_seq)] for d in (1, 2))
    gate_w, up_w, down_w = specialist_switch_matrix[0], w_up[0], w_down[0]
    others = tuple(lax.ppermute(w, "seq", near) for w in (gate_w, up_w, down_w))
    down_far = lax.ppermute(down_w, "seq", across)

    halo = (taps - 1) * prompts
    x_rows = x_branch.reshape(rows, channels)
    received = lax.ppermute(x_rows[rows - halo :], "seq", [(i, i + 1) for i in range(n_seq - 1)])
    here = (
        a_log.T, carry_state.transpose(0, 2, 1), gate_branch.reshape(rows, channels),
        layer_input.reshape(own_rows, d_model), jnp.stack([place, owner]),
    )

    activated, part = call(
        conv_kernel,
        (shape((rows, channels)), shape((rows, x_proj.shape[1]))),
        [SCALAR] + [VM] * 6,
        [pltpu.VMEM((rows + 8, channels), F32)],
        name="conv",
    )(place[None], x_rows, received, carry_tail.reshape(halo, channels), conv_weight, conv_bias[None], x_proj.T)
    part, activated, *here = fence(part, activated, *here)
    summed = exchanged(part, "expert").reshape(groups, own_rows, part.shape[1]).sum(axis=0)
    summed, activated, *here = fence(summed, activated, *here)
    projected = exchanged(jnp.tile(summed, (groups, 1)), "expert")
    projected, activated, *rest = fence(projected, activated, *here, *others, down_far)
    (a_log_t, carry_t, gate_rows, own, spot), (gate_o, up_o, down_o, down_far) = rest[:-4], rest[-4:]
    down_corner = lax.ppermute(down_far, "seq", near)
    bc = jnp.broadcast_to(projected[:, rank:, None], (rows, 2 * states, 128))
    step, ends = call(
        functools.partial(local_kernel, prompts),
        (shape((rows, channels)), shape((prompts * states + 8, channels), BF16)),
        [VM] * 6,
        name="local",
    )(projected, dt_proj, dt_bias[None], activated, bc, a_log_t)
    ends, step, bc = fence(jnp.broadcast_to(ends[None], (n_seq,) + ends.shape), step, bc)
    every = exchanged(ends, "seq")
    every, step, bc, activated, a_log_t, carry_t, gate_rows, own = fence(
        every, step, bc, activated, a_log_t, carry_t, gate_rows, own
    )
    mixed = call(
        functools.partial(scan_kernel, prompts),
        shape((groups, rows, width), BF16),
        [SCALAR] + [VM] * 9 + [pl.BlockSpec(memory_space=pl.ANY)],
        [pltpu.VMEM((rows, channels), F32), pltpu.VMEM((channels, d_model), BF16), pltpu.SemaphoreType.DMA],
        name="scan",
    )(spot, every, carry_t, step, activated, bc, a_log_t, d_skip[None], gate_rows, own, out_proj)
    mixed, steering, refusal, norm_gain, expert_ids, down_corner = fence(
        mixed, steering, refusal, norm_gain, expert_ids, down_corner
    )
    mixed = exchanged(mixed, "expert")
    clean = call(clean_kernel, shape((d_model // 128, 128)), [VM] * 2, name="clean")(
        steering.reshape(-1, 128), refusal.reshape(refusal.shape[0], -1, 128)
    )
    start = owner * width
    clean = lax.dynamic_slice_in_dim(clean.reshape(1, d_model), start, width, 1)
    gain = lax.dynamic_slice_in_dim(norm_gain[None], start, width, 1)
    ids = expert_ids.reshape(rows, top_count)

    residual, send, slots = call(
        dispatch_kernel,
        (
            shape((rows, width)),
            shape((experts, capacity, width + 128), BF16),
            shape((experts, capacity, rows), BF16),
        ),
        [VM] * 4,
        name="dispatch",
    )(mixed, clean, gain, ids.T)
    got = exchanged(send, "expert")
    normed = call(
        functools.partial(normed_kernel, float(d_model)), shape((capacity, d_model), BF16), [VM], name="normed"
    )(got)

    kinds = [[i for i in range(n_seq) if i % 4 == k] for k in range(4)]
    pieces = lax.all_gather(normed, "seq", axis=0, tiled=True, axis_index_groups=[kinds[0] + kinds[2], kinds[1] + kinds[3]])
    share = call(share_kernel, shape((capacity, 128)), [SCALAR] + [VM] * 4, name="share")(
        owner[None], normed, router.T, slots, ids
    )
    half = pieces.shape[0] // 2
    big = pltpu.CompilerParams(vmem_limit_bytes=58 * 1024 * 1024)
    hbm = pl.BlockSpec(memory_space=pltpu.HBM)
    up_sources = (gate_w, up_w, gate_o, up_o)
    inner = 2 * up_w.shape[1]

    def hidden_of(which):
        return pl.pallas_call(
            hidden_kernel,
            grid_spec=pltpu.PrefetchScalarGridSpec(
                num_scalar_prefetch=1,
                grid=(1,),
                in_specs=[pl.BlockSpec((half, d_model), lambda i, which: (which[0], 0))] + [hbm] * 4,
                out_specs=pl.BlockSpec((half, inner), lambda i, which: (0, 0)),
                scratch_shapes=[pltpu.VMEM(w.shape, BF16) for w in up_sources] + [pltpu.SemaphoreType.DMA((4,))],
            ),
            out_shape=shape((half, inner), BF16),
            compiler_params=big,
            name="hidden",
        )(which[None], pieces, *up_sources)

    mine = (place // 2) % 2
    given = lax.ppermute(hidden_of(1 - mine), "seq", across)
    kept = hidden_of(mine)
    down_sources = (down_w, down_o, down_far, down_corner)
    partial = pl.pallas_call(
        down_kernel,
        grid=(1,),
        out_shape=shape((half, d_model), BF16),
        in_specs=[pl.BlockSpec((half, inner), lambda i: (0, 0))] * 2 + [hbm] * 4,
        out_specs=pl.BlockSpec((half, d_model), lambda i: (0, 0)),
        scratch_shapes=[pltpu.VMEM(w.shape, BF16) for w in down_sources] + [pltpu.SemaphoreType.DMA((4,))],
        compiler_params=big,
        name="down",
    )(kept, given, *down_sources)
    partial, share, residual, slots = fence(partial, share, residual, slots)
    partial = exchanged(partial, "seq", kinds).reshape(n_seq // 4, capacity, d_model)
    partial, share, residual, slots = fence(partial, share, residual, slots)
    weighted = pl.pallas_call(
        weigh_kernel,
        grid=(groups,),
        out_shape=shape((groups, capacity, width), BF16),
        in_specs=[
            pl.BlockSpec((n_seq // 4, capacity, width), lambda j: (0, 0, j)),
            pl.BlockSpec((capacity, 128), lambda j: (0, 0)),
        ],
        out_specs=pl.BlockSpec((1, capacity, width), lambda j: (j, 0, 0)),
        compiler_params=WIDE,
        name="weigh",
    )(partial, share)
    back = exchanged(weighted, "expert")
    total = call(combine_kernel, shape((rows, width)), [VM] * 3, name="combine")(residual, back, slots)
    out = exchanged(total, "expert").reshape(groups, own_rows, width)
    return out.transpose(1, 0, 2).reshape(own_rows // prompts, prompts, d_model)


def solution(mesh):
    return jax.shard_map(
        shards,
        mesh=mesh,
        in_specs=(
            P(("seq", "expert"), None, None),
            P("seq", None, "expert"),
            P("seq", None, "expert"),
            P(None, "expert"),
            P("expert"),
            P("expert", None),
            P(None, "expert"),
            P("expert"),
            P("expert", None),
            P("expert"),
            P(None, "expert", None),
            P(None, None, "expert"),
            P("expert", None),
            P(),
            P(),
            P(),
            P(),
            P("expert", None, "seq"),
            P("expert", None, "seq"),
            P("expert", "seq", None),
            P("seq", None, None),
        ),
        out_specs=P(("seq", "expert"), None, None),
        check_vma=False,
    )
```

```python
import functools

import jax
import jax.numpy as jnp
from jax import lax
from jax.experimental import pallas as pl
from jax.experimental.pallas import tpu as pltpu
from jax.sharding import PartitionSpec as P

EPS = 1e-06
LOG2E = 1.4426950408889634
F32 = jnp.float32
BF16 = jnp.bfloat16
WIDE = pltpu.CompilerParams(vmem_limit_bytes=40 * 1024 * 1024)


def silu(v):
    return v * jax.nn.sigmoid(v)


def dot(a, b):
    return jnp.dot(a, b, preferred_element_type=F32)


def fence(*values):
    return lax.optimization_barrier(values)


def exchanged(blocks, axis, groups=None):
    return lax.all_to_all(blocks, axis, 0, 0, tiled=True, axis_index_groups=groups)


def conv_kernel(lead_ref, x_ref, got_ref, carry_ref, w_ref, b_ref, xp_ref, act_ref, part_ref, pad_ref):
    rows = x_ref.shape[0]
    taps = w_ref.shape[0]
    halo = got_ref.shape[0]
    step = halo // (taps - 1)
    first = lead_ref[0] == 0
    pad_ref[:halo, :] = jnp.where(first, carry_ref[...].astype(F32), got_ref[...].astype(F32))
    pad_ref[halo : halo + rows, :] = x_ref[...].astype(F32)
    total = b_ref[...].astype(F32)
    w = w_ref[...].astype(F32)
    for k in range(taps):
        total = total + w[k : k + 1, :] * pad_ref[k * step : k * step + rows, :]
    act = silu(total)
    act_ref[...] = act
    part_ref[...] = lax.dot_general(act.astype(BF16), xp_ref[...], (((1,), (1,)), ((), ())), preferred_element_type=F32)


def advance(state, rate, step, drive, b):
    return jnp.exp2(step * rate) * state + drive * b


def local_kernel(prompts, proj_ref, dtp_ref, dtb_ref, act_ref, bc_ref, alog_ref, step_ref, out_ref):
    rows, channels = act_ref.shape
    states = alog_ref.shape[0]
    rank = dtp_ref.shape[0]
    low = proj_ref[:, :rank].astype(BF16)
    step_ref[...] = jax.nn.softplus(dot(low, dtp_ref[...]) + dtb_ref[...])
    rate = -jnp.exp(alog_ref[...]) * LOG2E

    def body(i, carried):
        carried = list(carried)
        at = pl.multiple_of(i * 8, 8)
        step = step_ref[pl.ds(at, 8), :]
        drive = step * act_ref[pl.ds(at, 8), :]
        for r in range(8):
            p = r % prompts
            b = jnp.tile(bc_ref[at + r, :states, :], (1, channels // 128))
            carried[p] = advance(carried[p], rate, step[r : r + 1, :], drive[r : r + 1, :], b)
        return tuple(carried)

    zero = jnp.zeros((states, channels), F32)
    ends = lax.fori_loop(0, rows // 8, body, (zero,) * prompts)
    for p in range(prompts):
        out_ref[p * states : (p + 1) * states, :] = ends[p].astype(BF16)
    step = step_ref[...].reshape(rows // 8, 8, channels).sum(axis=0)
    sums = [sum(step[r : r + 1, :] for r in range(p, 8, prompts)) for p in range(prompts)]
    high = [s.astype(BF16).astype(F32) for s in sums]
    low_part = [(s - h) for s, h in zip(sums, high)]
    rest = jnp.zeros((8 - 2 * prompts, channels), F32)
    out_ref[prompts * states :, :] = jnp.concatenate(high + low_part + [rest], axis=0).astype(BF16)


def scan_kernel(
    prompts, ids_ref, all_ref, carry_ref, step_ref, act_ref, bc_ref, alog_ref, skip_ref, gate_ref, own_ref,
    outp_ref, mixed_ref, y_ref, w_ref, sem,
):
    rows, channels = act_ref.shape
    states = alog_ref.shape[0]
    copy = pltpu.make_async_copy(outp_ref, w_ref, sem)
    copy.start()
    rate = -jnp.exp(alog_ref[...]) * LOG2E

    def earlier(j, carried):
        block = all_ref[j].astype(F32)
        at = prompts * states
        out = []
        for p in range(prompts):
            total = block[at + p : at + p + 1, :] + block[at + prompts + p : at + prompts + p + 1, :]
            out.append(jnp.exp2(total * rate) * carried[p] + block[p * states : (p + 1) * states, :])
        return tuple(out)

    entering = lax.fori_loop(0, ids_ref[0], earlier, tuple(carry_ref[p] for p in range(prompts)))

    def body(i, carried):
        carried = list(carried)
        at = pl.multiple_of(i * 8, 8)
        step = step_ref[pl.ds(at, 8), :]
        drive = step * act_ref[pl.ds(at, 8), :]
        outs = []
        for r in range(8):
            p = r % prompts
            bc = bc_ref[at + r]
            b = jnp.tile(bc[:states], (1, channels // 128))
            c = jnp.tile(bc[states:], (1, channels // 128))
            carried[p] = advance(carried[p], rate, step[r : r + 1, :], drive[r : r + 1, :], b)
            outs.append(jnp.sum(carried[p] * c, axis=0, keepdims=True))
        y_ref[pl.ds(at, 8), :] = jnp.concatenate(outs, axis=0)
        return tuple(carried)

    lax.fori_loop(0, rows // 8, body, entering)
    y = y_ref[...] + skip_ref[...] * act_ref[...]
    gated = (y * silu(gate_ref[...].astype(F32))).astype(BF16)
    copy.wait()
    blocks, _, width = mixed_ref.shape
    own_rows = own_ref.shape[0]
    row_group = lax.broadcasted_iota(jnp.int32, (rows, width), 0) // own_rows
    mine = row_group == ids_ref[1]
    for j in range(blocks):
        part = dot(gated, w_ref[:, j * width : (j + 1) * width])
        own = jnp.tile(own_ref[:, j * width : (j + 1) * width].astype(F32), (rows // own_rows, 1))
        mixed_ref[j] = (part + jnp.where(mine, own, 0.0)).astype(BF16)


def clean_kernel(steer_ref, refusal_ref, out_ref):
    vector = steer_ref[...].astype(F32)
    units = []
    for k in range(refusal_ref.shape[0]):
        r = refusal_ref[k].astype(F32)
        for q in units:
            r = r - jnp.sum(q * r) * q
        r = r * lax.rsqrt(jnp.sum(r * r) + EPS)
        units.append(r)
    for q in units:
        vector = vector - jnp.sum(q * vector) * q
    out_ref[...] = vector


def dispatch_kernel(mixed_ref, clean_ref, gain_ref, lanes_ref, res_ref, send_ref, slots_ref):
    experts, capacity, rows = slots_ref.shape
    width = res_ref.shape[1]
    residual = clean_ref[...]
    for j in range(mixed_ref.shape[0]):
        residual = residual + mixed_ref[j].astype(F32)
    res_ref[...] = residual
    scaled = (residual * gain_ref[...].astype(F32)).astype(BF16)
    square = jnp.sum(residual * residual, axis=1, keepdims=True)
    high = square.astype(BF16).astype(F32)
    middle = (square - high).astype(BF16).astype(F32)
    low = square - high - middle
    lane = lax.broadcasted_iota(jnp.int32, (rows, 128), 1)
    extra = jnp.where(lane == 0, high, jnp.where(lane == 1, middle, jnp.where(lane == 2, low, 0.0)))
    payload = jnp.concatenate([scaled, extra.astype(BF16)], axis=1)
    label = lax.broadcasted_iota(jnp.int32, (experts, rows), 0)
    member = (lanes_ref[0:1, :] == label) | (lanes_ref[1:2, :] == label)
    upper = lax.broadcasted_iota(jnp.int32, (rows, rows), 0) <= lax.broadcasted_iota(jnp.int32, (rows, rows), 1)
    order = dot(member.astype(F32).astype(BF16), upper.astype(F32).astype(BF16))
    place = jnp.where(member, order - 1.0, -1.0)
    slot = lax.broadcasted_iota(jnp.int32, (capacity, rows), 0).astype(F32)
    for e in range(experts):
        chosen = (place[e : e + 1, :] == slot).astype(F32).astype(BF16)
        slots_ref[e] = chosen
        send_ref[e] = dot(chosen, payload).astype(BF16)


def normed_kernel(features, got_ref, out_ref):
    width = out_ref.shape[1] // got_ref.shape[0]
    total = jnp.zeros((out_ref.shape[0], 128), F32)
    for j in range(got_ref.shape[0]):
        total = total + got_ref[j, :, width:].astype(F32)
    scale = lax.rsqrt(jnp.sum(total, axis=1, keepdims=True) / features + EPS)
    for j in range(got_ref.shape[0]):
        out_ref[:, j * width : (j + 1) * width] = (got_ref[j, :, :width].astype(F32) * scale).astype(BF16)


def share_kernel(owner_ref, x_ref, router_ref, slots_ref, rows_ref, out_ref):
    logits = lax.dot_general(x_ref[...], router_ref[...], (((1,), (1,)), ((), ())), preferred_element_type=F32)
    experts = router_ref.shape[0]
    rows = rows_ref.shape[0]
    label = lax.broadcasted_iota(jnp.int32, (rows, experts), 1)
    member = (rows_ref[:, 0:1] == label) | (rows_ref[:, 1:2] == label)
    both = dot(slots_ref[owner_ref[0]], member.astype(F32).astype(BF16))
    own = (lax.broadcasted_iota(jnp.int32, both.shape, 1) == owner_ref[0]).astype(F32) * both
    gap = jnp.sum(logits * (2.0 * own - both), axis=1, keepdims=True)
    out_ref[...] = jnp.broadcast_to(jax.nn.sigmoid(gap), out_ref.shape)


def fetched(sources, held, sem):
    copies = [pltpu.make_async_copy(a, b, sem.at[i]) for i, (a, b) in enumerate(zip(sources, held))]
    for copy in copies:
        copy.start()
    return copies


def expert_kernel(x_ref, g0_ref, u0_ref, g1_ref, u1_ref, d0_ref, d1_ref, out_ref, x_held, g0, u0, g1, u1, d0, d1, sem):
    tiles, tile, _ = x_held.shape
    sources = [x_ref.at[pl.ds(0, tile)], g0_ref, u0_ref, g1_ref, u1_ref, d0_ref, d1_ref]
    targets = [x_held.at[0], g0, u0, g1, u1, d0, d1]
    sources += [x_ref.at[pl.ds(i * tile, tile)] for i in range(1, tiles)]
    targets += [x_held.at[i] for i in range(1, tiles)]
    copies = fetched(sources, targets, sem)
    for i in range(tiles):
        copies[7 + i - 1 if i else 0].wait()
        x = x_held[i]
        hidden = []
        for k, (g, u) in enumerate(((g0, u0), (g1, u1))):
            if i == 0:
                copies[1 + 2 * k].wait()
            gate = dot(x, g[...])
            if i == 0:
                copies[2 + 2 * k].wait()
            hidden.append((silu(gate) * dot(x, u[...])).astype(BF16))
        if i == 0:
            copies[5].wait()
            copies[6].wait()
        for j in range(0, out_ref.shape[1], 512):
            total = dot(hidden[0], d0[:, j : j + 512]) + dot(hidden[1], d1[:, j : j + 512])
            out_ref[i * tile : (i + 1) * tile, j : j + 512] = total.astype(BF16)


def weigh_kernel(got_ref, share_ref, out_ref):
    total = got_ref[0].astype(F32)
    for i in range(1, got_ref.shape[0]):
        total = total + got_ref[i].astype(F32)
    out_ref[0] = (total * share_ref[:, :1]).astype(BF16)


def combine_kernel(got_ref, slots_ref, out_ref):
    total = jnp.zeros(out_ref.shape, F32)
    for e in range(got_ref.shape[0]):
        total = total + lax.dot_general(
            slots_ref[e], got_ref[e], (((0,), (0,)), ((), ())), preferred_element_type=F32
        )
    out_ref[...] = total.astype(BF16)


def shape(dims, dtype=F32):
    return jax.ShapeDtypeStruct(dims, dtype)


SCALAR = pl.BlockSpec(memory_space=pltpu.SMEM)
VM = pl.BlockSpec(memory_space=pltpu.VMEM)


def call(kernel, outs, specs, scratch=(), name=None):
    return pl.pallas_call(
        kernel, out_shape=outs, in_specs=specs, scratch_shapes=list(scratch), compiler_params=WIDE, name=name
    )


def shards(
    layer_input, x_branch, gate_branch, conv_weight, conv_bias, x_proj, dt_proj, dt_bias, a_log, d_skip, carry_state,
    carry_tail, out_proj, steering, refusal, norm_gain, router, specialist_switch_matrix, w_up, w_down, expert_ids,
):
    taps = conv_weight.shape[0]
    length, prompts, channels = x_branch.shape
    rows = length * prompts
    states = a_log.shape[1]
    rank = dt_proj.shape[0]
    d_model = out_proj.shape[1]
    experts = router.shape[1]
    top_count = expert_ids.shape[-1]
    capacity = rows * top_count * 5 // (4 * experts)
    n_seq = lax.axis_size("seq")
    groups = lax.axis_size("expert")
    width = d_model // groups
    own_rows = rows // groups
    place = lax.axis_index("seq").astype(jnp.int32)
    owner = lax.axis_index("expert").astype(jnp.int32)

    near = [(i, i ^ 1) for i in range(n_seq)]
    weights = (specialist_switch_matrix[0], w_up[0], w_down[0])
    others = tuple(lax.ppermute(w, "seq", near) for w in weights)

    halo = (taps - 1) * prompts
    x_rows = x_branch.reshape(rows, channels)
    received = lax.ppermute(x_rows[rows - halo :], "seq", [(i, i + 1) for i in range(n_seq - 1)])
    here = (
        a_log.T, carry_state.transpose(0, 2, 1), gate_branch.reshape(rows, channels),
        layer_input.reshape(own_rows, d_model), jnp.stack([place, owner]),
    )

    activated, part = call(
        conv_kernel,
        (shape((rows, channels)), shape((rows, x_proj.shape[1]))),
        [SCALAR] + [VM] * 6,
        [pltpu.VMEM((rows + 8, channels), F32)],
        name="conv",
    )(place[None], x_rows, received, carry_tail.reshape(halo, channels), conv_weight, conv_bias[None], x_proj.T)
    part, activated, *here = fence(part, activated, *here)
    summed = exchanged(part, "expert").reshape(groups, own_rows, part.shape[1]).sum(axis=0)
    summed, activated, *here = fence(summed, activated, *here)
    projected = exchanged(jnp.tile(summed, (groups, 1)), "expert")
    projected, activated, *rest = fence(projected, activated, *here, *others)
    (a_log_t, carry_t, gate_rows, own, spot), others = rest[:-3], rest[-3:]
    bc = jnp.broadcast_to(projected[:, rank:, None], (rows, 2 * states, 128))
    step, ends = call(
        functools.partial(local_kernel, prompts),
        (shape((rows, channels)), shape((prompts * states + 8, channels), BF16)),
        [VM] * 6,
        name="local",
    )(projected, dt_proj, dt_bias[None], activated, bc, a_log_t)
    ends, step, bc = fence(jnp.broadcast_to(ends[None], (n_seq,) + ends.shape), step, bc)
    every = exchanged(ends, "seq")
    every, step, bc, activated, a_log_t, carry_t, gate_rows, own = fence(
        every, step, bc, activated, a_log_t, carry_t, gate_rows, own
    )
    mixed = call(
        functools.partial(scan_kernel, prompts),
        shape((groups, rows, width), BF16),
        [SCALAR] + [VM] * 9 + [pl.BlockSpec(memory_space=pl.ANY)],
        [pltpu.VMEM((rows, channels), F32), pltpu.VMEM((channels, d_model), BF16), pltpu.SemaphoreType.DMA],
        name="scan",
    )(spot, every, carry_t, step, activated, bc, a_log_t, d_skip[None], gate_rows, own, out_proj)
    mixed, steering, refusal, norm_gain, expert_ids = fence(mixed, steering, refusal, norm_gain, expert_ids)
    mixed = exchanged(mixed, "expert")
    clean = call(clean_kernel, shape((d_model // 128, 128)), [VM] * 2, name="clean")(
        steering.reshape(-1, 128), refusal.reshape(refusal.shape[0], -1, 128)
    )
    start = owner * width
    clean = lax.dynamic_slice_in_dim(clean.reshape(1, d_model), start, width, 1)
    gain = lax.dynamic_slice_in_dim(norm_gain[None], start, width, 1)
    ids = expert_ids.reshape(rows, top_count)

    residual, send, slots = call(
        dispatch_kernel,
        (
            shape((rows, width)),
            shape((experts, capacity, width + 128), BF16),
            shape((experts, capacity, rows), BF16),
        ),
        [VM] * 4,
        name="dispatch",
    )(mixed, clean, gain, ids.T)
    got = exchanged(send, "expert")
    normed = call(
        functools.partial(normed_kernel, float(d_model)), shape((capacity, d_model), BF16), [VM], name="normed"
    )(got)

    same_core = [[i for i in range(n_seq) if i % 2 == c] for c in range(2)]
    pieces = lax.all_gather(normed, "seq", axis=0, tiled=True, axis_index_groups=same_core)
    share = call(share_kernel, shape((capacity, 128)), [SCALAR] + [VM] * 4, name="share")(
        owner[None], normed, router.T, slots, ids
    )
    residual, share = fence(residual, share)
    own_residual = exchanged(residual, "expert").reshape(groups, own_rows, width)
    hbm = pl.BlockSpec(memory_space=pltpu.HBM)
    pieces, own_residual, share = fence(pieces, own_residual, share)
    held = (weights[0], weights[1], others[0], others[1], weights[2], others[2])
    tiles = 2
    partial = pl.pallas_call(
        expert_kernel,
        out_shape=pltpu.VMEM(pieces.shape, BF16),
        in_specs=[hbm] * (1 + len(held)),
        out_specs=VM,
        scratch_shapes=[pltpu.VMEM((tiles, pieces.shape[0] // tiles, d_model), BF16)]
        + [pltpu.VMEM(w.shape, BF16) for w in held]
        + [pltpu.SemaphoreType.DMA((tiles + len(held),))],
        compiler_params=pltpu.CompilerParams(vmem_limit_bytes=54 * 1024 * 1024),
        name="expert",
    )(pieces, *held)
    partial, share, slots, own_residual = fence(partial, share, slots, own_residual)
    partial = exchanged(partial, "seq", same_core).reshape(n_seq // 2, capacity, d_model)
    partial, share, slots, own_residual = fence(partial, share, slots, own_residual)
    weighted = pl.pallas_call(
        weigh_kernel,
        grid=(groups,),
        out_shape=shape((groups, capacity, width), BF16),
        in_specs=[
            pl.BlockSpec((n_seq // 2, capacity, width), lambda j: (0, 0, j)),
            pl.BlockSpec((capacity, 128), lambda j: (0, 0)),
        ],
        out_specs=pl.BlockSpec((1, capacity, width), lambda j: (j, 0, 0)),
        compiler_params=WIDE,
        name="weigh",
    )(partial, share)
    back = exchanged(weighted, "expert")
    total = call(combine_kernel, shape((rows, width), BF16), [VM] * 2, name="combine")(back, slots)
    out = exchanged(total, "expert").reshape(groups, own_rows, width)
    out = own_residual + out.astype(F32)
    return out.transpose(1, 0, 2).reshape(own_rows // prompts, prompts, d_model)


def solution(mesh):
    return jax.shard_map(
        shards,
        mesh=mesh,
        in_specs=(
            P(("seq", "expert"), None, None),
            P("seq", None, "expert"),
            P("seq", None, "expert"),
            P(None, "expert"),
            P("expert"),
            P("expert", None),
            P(None, "expert"),
            P("expert"),
            P("expert", None),
            P("expert"),
            P(None, "expert", None),
            P(None, None, "expert"),
            P("expert", None),
            P(),
            P(),
            P(),
            P(),
            P("expert", None, "seq"),
            P("expert", None, "seq"),
            P("expert", "seq", None),
            P("seq", None, None),
        ),
        out_specs=P(("seq", "expert"), None, None),
        check_vma=False,
    )
```

```python
import functools

import jax
import jax.numpy as jnp
from jax import lax
from jax.experimental import pallas as pl
from jax.experimental.pallas import tpu as pltpu
from jax.sharding import PartitionSpec as P

EPS = 1e-06
LOG2E = 1.4426950408889634
F32 = jnp.float32
BF16 = jnp.bfloat16
WIDE = pltpu.CompilerParams(vmem_limit_bytes=40 * 1024 * 1024)


def silu(v):
    return v * jax.nn.sigmoid(v)


def dot(a, b):
    return jnp.dot(a, b, preferred_element_type=F32)


def fence(*values):
    return lax.optimization_barrier(values)


def exchanged(blocks, axis, groups=None):
    return lax.all_to_all(blocks, axis, 0, 0, tiled=True, axis_index_groups=groups)


def conv_kernel(lead_ref, x_ref, got_ref, carry_ref, w_ref, b_ref, xp_ref, act_ref, part_ref, pad_ref):
    rows = x_ref.shape[0]
    taps = w_ref.shape[0]
    halo = got_ref.shape[0]
    step = halo // (taps - 1)
    first = lead_ref[0] == 0
    pad_ref[:halo, :] = jnp.where(first, carry_ref[...].astype(F32), got_ref[...].astype(F32))
    pad_ref[halo : halo + rows, :] = x_ref[...].astype(F32)
    total = b_ref[...].astype(F32)
    w = w_ref[...].astype(F32)
    for k in range(taps):
        total = total + w[k : k + 1, :] * pad_ref[k * step : k * step + rows, :]
    act = silu(total)
    act_ref[...] = act
    part_ref[...] = lax.dot_general(act.astype(BF16), xp_ref[...], (((1,), (1,)), ((), ())), preferred_element_type=F32)


def advance(state, rate, step, drive, b):
    return jnp.exp2(step * rate) * state + drive * b


def local_kernel(prompts, proj_ref, dtp_ref, dtb_ref, act_ref, bc_ref, alog_ref, step_ref, out_ref):
    rows, channels = act_ref.shape
    states = alog_ref.shape[0]
    rank = dtp_ref.shape[0]
    low = proj_ref[:, :rank].astype(BF16)
    step_ref[...] = jax.nn.softplus(dot(low, dtp_ref[...]) + dtb_ref[...])
    rate = -jnp.exp(alog_ref[...]) * LOG2E

    def body(i, carried):
        carried = list(carried)
        at = pl.multiple_of(i * 8, 8)
        step = step_ref[pl.ds(at, 8), :]
        drive = step * act_ref[pl.ds(at, 8), :]
        for r in range(8):
            p = r % prompts
            b = jnp.tile(bc_ref[at + r, :states, :], (1, channels // 128))
            carried[p] = advance(carried[p], rate, step[r : r + 1, :], drive[r : r + 1, :], b)
        return tuple(carried)

    zero = jnp.zeros((states, channels), F32)
    ends = lax.fori_loop(0, rows // 8, body, (zero,) * prompts)
    for p in range(prompts):
        out_ref[p * states : (p + 1) * states, :] = ends[p].astype(BF16)
    step = step_ref[...].reshape(rows // 8, 8, channels).sum(axis=0)
    sums = [sum(step[r : r + 1, :] for r in range(p, 8, prompts)) for p in range(prompts)]
    high = [s.astype(BF16).astype(F32) for s in sums]
    low_part = [(s - h) for s, h in zip(sums, high)]
    rest = jnp.zeros((8 - 2 * prompts, channels), F32)
    out_ref[prompts * states :, :] = jnp.concatenate(high + low_part + [rest], axis=0).astype(BF16)


def scan_kernel(
    prompts, ids_ref, all_ref, carry_ref, step_ref, act_ref, bc_ref, alog_ref, skip_ref, gate_ref, own_ref,
    outp_ref, mixed_ref, y_ref, w_ref, sem,
):
    rows, channels = act_ref.shape
    states = alog_ref.shape[0]
    copy = pltpu.make_async_copy(outp_ref, w_ref, sem)
    copy.start()
    rate = -jnp.exp(alog_ref[...]) * LOG2E

    def earlier(j, carried):
        block = all_ref[j].astype(F32)
        at = prompts * states
        out = []
        for p in range(prompts):
            total = block[at + p : at + p + 1, :] + block[at + prompts + p : at + prompts + p + 1, :]
            out.append(jnp.exp2(total * rate) * carried[p] + block[p * states : (p + 1) * states, :])
        return tuple(out)

    entering = lax.fori_loop(0, ids_ref[0], earlier, tuple(carry_ref[p] for p in range(prompts)))

    def body(i, carried):
        carried = list(carried)
        at = pl.multiple_of(i * 8, 8)
        step = step_ref[pl.ds(at, 8), :]
        drive = step * act_ref[pl.ds(at, 8), :]
        outs = []
        for r in range(8):
            p = r % prompts
            bc = bc_ref[at + r]
            b = jnp.tile(bc[:states], (1, channels // 128))
            c = jnp.tile(bc[states:], (1, channels // 128))
            carried[p] = advance(carried[p], rate, step[r : r + 1, :], drive[r : r + 1, :], b)
            outs.append(jnp.sum(carried[p] * c, axis=0, keepdims=True))
        y_ref[pl.ds(at, 8), :] = jnp.concatenate(outs, axis=0)
        return tuple(carried)

    lax.fori_loop(0, rows // 8, body, entering)
    y = y_ref[...] + skip_ref[...] * act_ref[...]
    gated = (y * silu(gate_ref[...].astype(F32))).astype(BF16)
    copy.wait()
    blocks, _, width = mixed_ref.shape
    own_rows = own_ref.shape[0]
    row_group = lax.broadcasted_iota(jnp.int32, (rows, width), 0) // own_rows
    mine = row_group == ids_ref[1]
    for j in range(blocks):
        part = dot(gated, w_ref[:, j * width : (j + 1) * width])
        own = jnp.tile(own_ref[:, j * width : (j + 1) * width].astype(F32), (rows // own_rows, 1))
        mixed_ref[j] = (part + jnp.where(mine, own, 0.0)).astype(BF16)


def clean_kernel(steer_ref, refusal_ref, out_ref):
    vector = steer_ref[...].astype(F32)
    units = []
    for k in range(refusal_ref.shape[0]):
        r = refusal_ref[k].astype(F32)
        for q in units:
            r = r - jnp.sum(q * r) * q
        r = r * lax.rsqrt(jnp.sum(r * r) + EPS)
        units.append(r)
    for q in units:
        vector = vector - jnp.sum(q * vector) * q
    out_ref[...] = vector


def dispatch_kernel(mixed_ref, clean_ref, gain_ref, lanes_ref, res_ref, send_ref, slots_ref):
    experts, capacity, rows = slots_ref.shape
    width = res_ref.shape[1]
    residual = clean_ref[...]
    for j in range(mixed_ref.shape[0]):
        residual = residual + mixed_ref[j].astype(F32)
    res_ref[...] = residual
    scaled = (residual * gain_ref[...].astype(F32)).astype(BF16)
    square = jnp.sum(residual * residual, axis=1, keepdims=True)
    high = square.astype(BF16).astype(F32)
    middle = (square - high).astype(BF16).astype(F32)
    low = square - high - middle
    lane = lax.broadcasted_iota(jnp.int32, (rows, 128), 1)
    extra = jnp.where(lane == 0, high, jnp.where(lane == 1, middle, jnp.where(lane == 2, low, 0.0)))
    payload = jnp.concatenate([scaled, extra.astype(BF16)], axis=1)
    label = lax.broadcasted_iota(jnp.int32, (experts, rows), 0)
    member = (lanes_ref[0:1, :] == label) | (lanes_ref[1:2, :] == label)
    upper = lax.broadcasted_iota(jnp.int32, (rows, rows), 0) <= lax.broadcasted_iota(jnp.int32, (rows, rows), 1)
    order = dot(member.astype(F32).astype(BF16), upper.astype(F32).astype(BF16))
    place = jnp.where(member, order - 1.0, -1.0)
    slot = lax.broadcasted_iota(jnp.int32, (capacity, rows), 0).astype(F32)
    for e in range(experts):
        chosen = (place[e : e + 1, :] == slot).astype(F32).astype(BF16)
        slots_ref[e] = chosen
        send_ref[e] = dot(chosen, payload).astype(BF16)


def normed_kernel(features, got_ref, out_ref):
    width = out_ref.shape[1] // got_ref.shape[0]
    total = jnp.zeros((out_ref.shape[0], 128), F32)
    for j in range(got_ref.shape[0]):
        total = total + got_ref[j, :, width:].astype(F32)
    scale = lax.rsqrt(jnp.sum(total, axis=1, keepdims=True) / features + EPS)
    for j in range(got_ref.shape[0]):
        out_ref[:, j * width : (j + 1) * width] = (got_ref[j, :, :width].astype(F32) * scale).astype(BF16)


def share_kernel(owner_ref, x_ref, router_ref, slots_ref, rows_ref, out_ref):
    logits = lax.dot_general(x_ref[...], router_ref[...], (((1,), (1,)), ((), ())), preferred_element_type=F32)
    experts = router_ref.shape[0]
    rows = rows_ref.shape[0]
    label = lax.broadcasted_iota(jnp.int32, (rows, experts), 1)
    member = (rows_ref[:, 0:1] == label) | (rows_ref[:, 1:2] == label)
    both = dot(slots_ref[owner_ref[0]], member.astype(F32).astype(BF16))
    own = (lax.broadcasted_iota(jnp.int32, both.shape, 1) == owner_ref[0]).astype(F32) * both
    gap = jnp.sum(logits * (2.0 * own - both), axis=1, keepdims=True)
    out_ref[...] = jnp.broadcast_to(jax.nn.sigmoid(gap), out_ref.shape)


def fetched(sources, held, sem):
    copies = [pltpu.make_async_copy(a, b, sem.at[i]) for i, (a, b) in enumerate(zip(sources, held))]
    for copy in copies:
        copy.start()
    return copies


def gathered_half(x_ref, held_ref, sem, parity):
    pairs, _, capacity, _ = x_ref.shape
    copies = [pltpu.make_async_copy(x_ref.at[i, parity], held_ref.at[i], sem.at[i]) for i in range(pairs)]
    for copy in copies:
        copy.start()
    return copies


def first_kernel(parity_ref, x_ref, g0_ref, u0_ref, g1_ref, u1_ref, out_ref, own_ref, g0, u0, g1, u1, x_held, sems, sem):
    theirs = gathered_half(x_ref, x_held, sems.at[0], 1 - parity_ref[0])
    copies = fetched((g0_ref, u0_ref, g1_ref, u1_ref), (g0, u0, g1, u1), sem)
    ours = gathered_half(x_ref, own_ref, sems.at[1], parity_ref[0])
    for copy in theirs:
        copy.wait()
    x = x_held[...].reshape(out_ref.shape[0], -1)
    width = g0.shape[1]
    for k, (g, u) in enumerate(((g0, u0), (g1, u1))):
        copies[2 * k].wait()
        gate = dot(x, g[...])
        copies[2 * k + 1].wait()
        out_ref[:, k * width : (k + 1) * width] = (silu(gate) * dot(x, u[...])).astype(BF16)
    for copy in ours:
        copy.wait()


def second_kernel(x_ref, g0, u0, g1, u1, *refs):
    sources, out_ref, held, sem = refs[:6], refs[6], refs[7:11], refs[11]
    part = sources[2].shape[0]
    targets = held[:2] + tuple(d.at[pl.ds(k * part, part)] for d in held[2:] for k in range(2))
    copies = fetched(sources, targets, sem)
    x = x_ref[...].reshape(out_ref.shape[0], -1)
    width = g0.shape[1]
    for k, (g, u) in enumerate(((g0, u0), (g1, u1))):
        out_ref[:, k * width : (k + 1) * width] = (silu(dot(x, g[...])) * dot(x, u[...])).astype(BF16)
    for copy in copies:
        copy.wait()


def down_kernel(own_ref, far_ref, d0, d1, d2, d3, out_ref):
    width = d0.shape[0]
    hidden = [ref[:, k * width : (k + 1) * width] for ref in (own_ref, far_ref) for k in range(2)]
    for j in range(0, out_ref.shape[1], 512):
        total = dot(hidden[0], d0[:, j : j + 512])
        for h, d in zip(hidden[1:], (d1, d2, d3)):
            total = total + dot(h, d[:, j : j + 512])
        out_ref[:, j : j + 512] = total.astype(BF16)


def weigh_kernel(got_ref, share_ref, out_ref):
    total = got_ref[0].astype(F32)
    for i in range(1, got_ref.shape[0]):
        total = total + got_ref[i].astype(F32)
    out_ref[0] = (total * share_ref[:, :1]).astype(BF16)


def combine_kernel(got_ref, slots_ref, out_ref):
    total = jnp.zeros(out_ref.shape, F32)
    for e in range(got_ref.shape[0]):
        total = total + lax.dot_general(
            slots_ref[e], got_ref[e], (((0,), (0,)), ((), ())), preferred_element_type=F32
        )
    out_ref[...] = total.astype(BF16)


def shape(dims, dtype=F32):
    return jax.ShapeDtypeStruct(dims, dtype)


SCALAR = pl.BlockSpec(memory_space=pltpu.SMEM)
VM = pl.BlockSpec(memory_space=pltpu.VMEM)


def call(kernel, outs, specs, scratch=(), name=None):
    return pl.pallas_call(
        kernel, out_shape=outs, in_specs=specs, scratch_shapes=list(scratch), compiler_params=WIDE, name=name
    )


def shards(
    layer_input, x_branch, gate_branch, conv_weight, conv_bias, x_proj, dt_proj, dt_bias, a_log, d_skip, carry_state,
    carry_tail, out_proj, steering, refusal, norm_gain, router, specialist_switch_matrix, w_up, w_down, expert_ids,
):
    taps = conv_weight.shape[0]
    length, prompts, channels = x_branch.shape
    rows = length * prompts
    states = a_log.shape[1]
    rank = dt_proj.shape[0]
    d_model = out_proj.shape[1]
    experts = router.shape[1]
    top_count = expert_ids.shape[-1]
    capacity = rows * top_count * 5 // (4 * experts)
    n_seq = lax.axis_size("seq")
    groups = lax.axis_size("expert")
    width = d_model // groups
    own_rows = rows // groups
    place = lax.axis_index("seq").astype(jnp.int32)
    owner = lax.axis_index("expert").astype(jnp.int32)

    near, across = ([(i, i ^ d) for i in range(n_seq)] for d in (1, 2))
    weights = (specialist_switch_matrix[0], w_up[0], w_down[0])
    others = tuple(lax.ppermute(w, "seq", near) for w in weights)

    halo = (taps - 1) * prompts
    x_rows = x_branch.reshape(rows, channels)
    received = lax.ppermute(x_rows[rows - halo :], "seq", [(i, i + 1) for i in range(n_seq - 1)])
    here = (
        a_log.T, carry_state.transpose(0, 2, 1), gate_branch.reshape(rows, channels),
        layer_input.reshape(own_rows, d_model), jnp.stack([place, owner]),
    )

    activated, part = call(
        conv_kernel,
        (shape((rows, channels)), shape((rows, x_proj.shape[1]))),
        [SCALAR] + [VM] * 6,
        [pltpu.VMEM((rows + 8, channels), F32)],
        name="conv",
    )(place[None], x_rows, received, carry_tail.reshape(halo, channels), conv_weight, conv_bias[None], x_proj.T)
    part, activated, *here = fence(part, activated, *here)
    summed = exchanged(part, "expert").reshape(groups, own_rows, part.shape[1]).sum(axis=0)
    summed, activated, *here = fence(summed, activated, *here)
    projected = exchanged(jnp.tile(summed, (groups, 1)), "expert")
    projected, activated, *rest = fence(projected, activated, *here, *others)
    (a_log_t, carry_t, gate_rows, own, spot), others = rest[:-3], rest[-3:]
    bc = jnp.broadcast_to(projected[:, rank:, None], (rows, 2 * states, 128))
    step, ends = call(
        functools.partial(local_kernel, prompts),
        (shape((rows, channels)), shape((prompts * states + 8, channels), BF16)),
        [VM] * 6,
        name="local",
    )(projected, dt_proj, dt_bias[None], activated, bc, a_log_t)
    ends, step, bc = fence(jnp.broadcast_to(ends[None], (n_seq,) + ends.shape), step, bc)
    every = exchanged(ends, "seq")
    every, step, bc, activated, a_log_t, carry_t, gate_rows, own, down_w = fence(
        every, step, bc, activated, a_log_t, carry_t, gate_rows, own, weights[2]
    )
    part = down_w.shape[0] // 2
    far_a, far_b = (lax.ppermute(down_w[k * part : (k + 1) * part], "seq", across) for k in range(2))
    mixed = call(
        functools.partial(scan_kernel, prompts),
        shape((groups, rows, width), BF16),
        [SCALAR] + [VM] * 9 + [pl.BlockSpec(memory_space=pl.ANY)],
        [pltpu.VMEM((rows, channels), F32), pltpu.VMEM((channels, d_model), BF16), pltpu.SemaphoreType.DMA],
        name="scan",
    )(spot, every, carry_t, step, activated, bc, a_log_t, d_skip[None], gate_rows, own, out_proj)
    mixed, steering, refusal, norm_gain, expert_ids = fence(mixed, steering, refusal, norm_gain, expert_ids)
    mixed = exchanged(mixed, "expert")
    clean = call(clean_kernel, shape((d_model // 128, 128)), [VM] * 2, name="clean")(
        steering.reshape(-1, 128), refusal.reshape(refusal.shape[0], -1, 128)
    )
    start = owner * width
    clean = lax.dynamic_slice_in_dim(clean.reshape(1, d_model), start, width, 1)
    gain = lax.dynamic_slice_in_dim(norm_gain[None], start, width, 1)
    ids = expert_ids.reshape(rows, top_count)

    residual, send, slots = call(
        dispatch_kernel,
        (
            shape((rows, width)),
            shape((experts, capacity, width + 128), BF16),
            shape((experts, capacity, rows), BF16),
        ),
        [VM] * 4,
        name="dispatch",
    )(mixed, clean, gain, ids.T)
    got = exchanged(send, "expert")
    normed = call(
        functools.partial(normed_kernel, float(d_model)), shape((capacity, d_model), BF16), [VM], name="normed"
    )(got)

    same_core = [[i for i in range(n_seq) if i % 2 == c] for c in range(2)]
    normed, far_a = fence(normed, far_a)
    corner_a = lax.ppermute(far_a, "seq", near)
    pieces = lax.all_gather(normed, "seq", axis=0, tiled=True, axis_index_groups=same_core)
    share = call(share_kernel, shape((capacity, 128)), [SCALAR] + [VM] * 4, name="share")(
        owner[None], normed, router.T, slots, ids
    )
    residual, share = fence(residual, share)
    own_residual = exchanged(residual, "expert").reshape(groups, own_rows, width)
    own_residual, share, far_b = fence(own_residual, share, far_b)
    corner_b = lax.ppermute(far_b, "seq", near)
    hbm = pl.BlockSpec(memory_space=pltpu.HBM)
    pieces, own_residual, share, corner_a, corner_b = fence(pieces, own_residual, share, corner_a, corner_b)
    pairs = n_seq // 4
    pieces = pieces.reshape(pairs, 2, capacity, d_model)
    ups = (weights[0], weights[1], others[0], others[1])
    downs = (down_w, others[2], far_a, far_b, corner_a, corner_b)
    half = pairs * capacity
    inner = 2 * ups[0].shape[1]
    dma = pltpu.SemaphoreType.DMA
    theirs, x_own, *ups = pl.pallas_call(
        first_kernel,
        out_shape=(shape((half, inner), BF16), pltpu.VMEM((pairs, capacity, d_model), BF16))
        + tuple(pltpu.VMEM(w.shape, BF16) for w in ups),
        in_specs=[SCALAR] + [hbm] * 5,
        out_specs=(VM,) * 6,
        scratch_shapes=[pltpu.VMEM((pairs, capacity, d_model), BF16), dma((2, pairs)), dma((4,))],
        compiler_params=pltpu.CompilerParams(vmem_limit_bytes=16 * 1024 * 1024),
        name="first",
    )(((place // 2) % 2)[None], *(pltpu.with_memory_space_constraint(v, pltpu.HBM) for v in (pieces, *ups)))
    given = lax.ppermute(theirs, "seq", across)
    kept, *downs = pl.pallas_call(
        second_kernel,
        out_shape=(shape((half, inner), BF16),) + (pltpu.VMEM(down_w.shape, BF16),) * 4,
        in_specs=[VM] * 5 + [hbm] * 6,
        out_specs=(VM,) * 5,
        scratch_shapes=[dma((6,))],
        compiler_params=pltpu.CompilerParams(vmem_limit_bytes=16 * 1024 * 1024),
        cost_estimate=pl.CostEstimate(flops=4 * half * inner * d_model, bytes_accessed=1 << 24, transcendentals=0),
        name="second",
    )(x_own, *ups, *(pltpu.with_memory_space_constraint(v, pltpu.HBM) for v in downs))
    partial = pl.pallas_call(
        down_kernel,
        out_shape=pltpu.VMEM((half, d_model), BF16),
        in_specs=[VM] * 6,
        out_specs=VM,
        compiler_params=pltpu.CompilerParams(vmem_limit_bytes=16 * 1024 * 1024),
        name="down",
    )(kept, given, *downs)
    kinds = [[i for i in range(n_seq) if i % 4 == k] for k in range(4)]
    partial, share, slots, own_residual = fence(partial, share, slots, own_residual)
    partial = exchanged(partial, "seq", kinds).reshape(pairs, capacity, d_model)
    partial, share, slots, own_residual = fence(partial, share, slots, own_residual)
    weighted = pl.pallas_call(
        weigh_kernel,
        grid=(groups,),
        out_shape=shape((groups, capacity, width), BF16),
        in_specs=[
            pl.BlockSpec((pairs, capacity, width), lambda j: (0, 0, j)),
            pl.BlockSpec((capacity, 128), lambda j: (0, 0)),
        ],
        out_specs=pl.BlockSpec((1, capacity, width), lambda j: (j, 0, 0)),
        compiler_params=WIDE,
        name="weigh",
    )(partial, share)
    back = exchanged(weighted, "expert")
    total = call(combine_kernel, shape((rows, width), BF16), [VM] * 2, name="combine")(back, slots)
    out = exchanged(total, "expert").reshape(groups, own_rows, width)
    out = own_residual + out.astype(F32)
    return out.transpose(1, 0, 2).reshape(own_rows // prompts, prompts, d_model)


def solution(mesh):
    return jax.shard_map(
        shards,
        mesh=mesh,
        in_specs=(
            P(("seq", "expert"), None, None),
            P("seq", None, "expert"),
            P("seq", None, "expert"),
            P(None, "expert"),
            P("expert"),
            P("expert", None),
            P(None, "expert"),
            P("expert"),
            P("expert", None),
            P("expert"),
            P(None, "expert", None),
            P(None, None, "expert"),
            P("expert", None),
            P(),
            P(),
            P(),
            P(),
            P("expert", None, "seq"),
            P("expert", None, "seq"),
            P("expert", "seq", None),
            P("seq", None, None),
        ),
        out_specs=P(("seq", "expert"), None, None),
        check_vma=False,
    )
```

```python
import functools

import jax
import jax.numpy as jnp
from jax import lax
from jax.experimental import pallas as pl
from jax.experimental.pallas import tpu as pltpu
from jax.sharding import PartitionSpec as P

EPS = 1e-06
LOG2E = 1.4426950408889634
F32 = jnp.float32
BF16 = jnp.bfloat16
WIDE = pltpu.CompilerParams(vmem_limit_bytes=40 * 1024 * 1024)


def silu(v):
    return v * jax.nn.sigmoid(v)


def dot(a, b):
    return jnp.dot(a, b, preferred_element_type=F32)


def fence(*values):
    return lax.optimization_barrier(values)


def exchanged(blocks, axis, groups=None):
    return lax.all_to_all(blocks, axis, 0, 0, tiled=True, axis_index_groups=groups)


def conv_kernel(
    lead_ref, x_ref, got_ref, carry_ref, taps_ref, b_ref, proj_ref, act_ref, part_ref, pad_ref, w_ref, xp_ref, sem
):
    copies = [pltpu.make_async_copy(a, b, sem.at[i]) for i, (a, b) in enumerate(((taps_ref, w_ref), (proj_ref, xp_ref)))]
    for copy in copies:
        copy.start()
    rows = x_ref.shape[0]
    taps = w_ref.shape[0]
    halo = got_ref.shape[0]
    step = halo // (taps - 1)
    first = lead_ref[0] == 0
    pad_ref[:halo, :] = jnp.where(first, carry_ref[...].astype(F32), got_ref[...].astype(F32))
    pad_ref[halo : halo + rows, :] = x_ref[...].astype(F32)
    total = b_ref[...].astype(F32)
    copies[0].wait()
    w = w_ref[...].astype(F32)
    for k in range(taps):
        total = total + w[k : k + 1, :] * pad_ref[k * step : k * step + rows, :]
    act = silu(total)
    act_ref[...] = act
    copies[1].wait()
    part_ref[...] = lax.dot_general(act.astype(BF16), xp_ref[...], (((1,), (1,)), ((), ())), preferred_element_type=F32)


def sum_kernel(rank, got_ref, out_ref):
    total = got_ref[0]
    for j in range(1, got_ref.shape[0]):
        total = total + got_ref[j]
    rest = total[:, rank:]
    high = rest.astype(BF16).astype(F32)
    middle = (rest - high).astype(BF16).astype(F32)
    out = [total[:, :rank], high, middle, rest - high - middle]
    pad = out_ref.shape[2] - rank - 3 * rest.shape[1]
    out = jnp.concatenate(out + [jnp.zeros((rest.shape[0], pad), F32)], axis=1).astype(BF16)
    for j in range(out_ref.shape[0]):
        out_ref[j] = out


def advance(state, rate, step, drive, b):
    return jnp.exp2(step * rate) * state + drive * b


def local_kernel(prompts, proj_ref, dtp_ref, dtb_ref, act_ref, bc_ref, alog_ref, step_ref, out_ref):
    rows, channels = act_ref.shape
    states = alog_ref.shape[0]
    rank = dtp_ref.shape[0]
    low = proj_ref[:, :rank]
    step_ref[...] = jax.nn.softplus(dot(low, dtp_ref[...]) + dtb_ref[...])
    rate = -jnp.exp(alog_ref[...]) * LOG2E

    def body(i, carried):
        carried = list(carried)
        at = pl.multiple_of(i * 8, 8)
        step = step_ref[pl.ds(at, 8), :]
        drive = step * act_ref[pl.ds(at, 8), :]
        for r in range(8):
            p = r % prompts
            b = jnp.tile(bc_ref[at + r, :states, :], (1, channels // 128))
            carried[p] = advance(carried[p], rate, step[r : r + 1, :], drive[r : r + 1, :], b)
        return tuple(carried)

    zero = jnp.zeros((states, channels), F32)
    ends = lax.fori_loop(0, rows // 8, body, (zero,) * prompts)
    for p in range(prompts):
        out_ref[p * states : (p + 1) * states, :] = ends[p].astype(BF16)
    step = step_ref[...].reshape(rows // 8, 8, channels).sum(axis=0)
    sums = [sum(step[r : r + 1, :] for r in range(p, 8, prompts)) for p in range(prompts)]
    high = [s.astype(BF16).astype(F32) for s in sums]
    low_part = [(s - h) for s, h in zip(sums, high)]
    rest = jnp.zeros((8 - 2 * prompts, channels), F32)
    out_ref[prompts * states :, :] = jnp.concatenate(high + low_part + [rest], axis=0).astype(BF16)


def scan_kernel(
    prompts, ids_ref, all_ref, carry_ref, step_ref, act_ref, bc_ref, alog_ref, skip_ref, gate_ref, own_ref,
    outp_ref, mixed_ref, y_ref, w_ref, sem,
):
    rows, channels = act_ref.shape
    states = alog_ref.shape[0]
    copy = pltpu.make_async_copy(outp_ref, w_ref, sem)
    copy.start()
    rate = -jnp.exp(alog_ref[...]) * LOG2E

    def earlier(j, carried):
        block = all_ref[j].astype(F32)
        at = prompts * states
        out = []
        for p in range(prompts):
            total = block[at + p : at + p + 1, :] + block[at + prompts + p : at + prompts + p + 1, :]
            out.append(jnp.exp2(total * rate) * carried[p] + block[p * states : (p + 1) * states, :])
        return tuple(out)

    entering = lax.fori_loop(0, ids_ref[0], earlier, tuple(carry_ref[p] for p in range(prompts)))

    def body(i, carried):
        carried = list(carried)
        at = pl.multiple_of(i * 8, 8)
        step = step_ref[pl.ds(at, 8), :]
        drive = step * act_ref[pl.ds(at, 8), :]
        outs = []
        for r in range(8):
            p = r % prompts
            bc = bc_ref[at + r]
            b = jnp.tile(bc[:states], (1, channels // 128))
            c = jnp.tile(bc[states:], (1, channels // 128))
            carried[p] = advance(carried[p], rate, step[r : r + 1, :], drive[r : r + 1, :], b)
            outs.append(jnp.sum(carried[p] * c, axis=0, keepdims=True))
        y_ref[pl.ds(at, 8), :] = jnp.concatenate(outs, axis=0)
        return tuple(carried)

    lax.fori_loop(0, rows // 8, body, entering)
    y = y_ref[...] + skip_ref[...] * act_ref[...]
    gated = (y * silu(gate_ref[...].astype(F32))).astype(BF16)
    copy.wait()
    blocks, _, width = mixed_ref.shape
    own_rows = own_ref.shape[0]
    row_group = lax.broadcasted_iota(jnp.int32, (rows, width), 0) // own_rows
    mine = row_group == ids_ref[1]
    for j in range(blocks):
        part = dot(gated, w_ref[:, j * width : (j + 1) * width])
        own = jnp.tile(own_ref[:, j * width : (j + 1) * width].astype(F32), (rows // own_rows, 1))
        mixed_ref[j] = (part + jnp.where(mine, own, 0.0)).astype(BF16)


def clean_kernel(steer_ref, refusal_ref, out_ref):
    vector = steer_ref[...].astype(F32)
    units = []
    for k in range(refusal_ref.shape[0]):
        r = refusal_ref[k].astype(F32)
        for q in units:
            r = r - jnp.sum(q * r) * q
        r = r * lax.rsqrt(jnp.sum(r * r) + EPS)
        units.append(r)
    for q in units:
        vector = vector - jnp.sum(q * vector) * q
    out_ref[...] = vector


def dispatch_kernel(mixed_ref, clean_ref, gain_ref, lanes_ref, res_ref, send_ref, slots_ref):
    experts, capacity, rows = slots_ref.shape
    width = res_ref.shape[1]
    residual = clean_ref[...]
    for j in range(mixed_ref.shape[0]):
        residual = residual + mixed_ref[j].astype(F32)
    res_ref[...] = residual
    scaled = (residual * gain_ref[...].astype(F32)).astype(BF16)
    square = jnp.sum(residual * residual, axis=1, keepdims=True)
    high = square.astype(BF16).astype(F32)
    middle = (square - high).astype(BF16).astype(F32)
    low = square - high - middle
    lane = lax.broadcasted_iota(jnp.int32, (rows, 128), 1)
    extra = jnp.where(lane == 0, high, jnp.where(lane == 1, middle, jnp.where(lane == 2, low, 0.0)))
    payload = jnp.concatenate([scaled, extra.astype(BF16)], axis=1)
    label = lax.broadcasted_iota(jnp.int32, (experts, rows), 0)
    member = (lanes_ref[0:1, :] == label) | (lanes_ref[1:2, :] == label)
    upper = lax.broadcasted_iota(jnp.int32, (rows, rows), 0) <= lax.broadcasted_iota(jnp.int32, (rows, rows), 1)
    order = dot(member.astype(F32).astype(BF16), upper.astype(F32).astype(BF16))
    place = jnp.where(member, order - 1.0, -1.0)
    slot = lax.broadcasted_iota(jnp.int32, (capacity, rows), 0).astype(F32)
    for e in range(experts):
        chosen = (place[e : e + 1, :] == slot).astype(F32).astype(BF16)
        slots_ref[e] = chosen
        send_ref[e] = dot(chosen, payload).astype(BF16)


def normed_kernel(features, got_ref, out_ref):
    width = out_ref.shape[1] // got_ref.shape[0]
    total = jnp.zeros((out_ref.shape[0], 128), F32)
    for j in range(got_ref.shape[0]):
        total = total + got_ref[j, :, width:].astype(F32)
    scale = lax.rsqrt(jnp.sum(total, axis=1, keepdims=True) / features + EPS)
    for j in range(got_ref.shape[0]):
        out_ref[:, j * width : (j + 1) * width] = (got_ref[j, :, :width].astype(F32) * scale).astype(BF16)


def share_kernel(owner_ref, x_ref, router_ref, slots_ref, rows_ref, out_ref):
    logits = lax.dot_general(x_ref[...], router_ref[...], (((1,), (1,)), ((), ())), preferred_element_type=F32)
    experts = router_ref.shape[0]
    rows = rows_ref.shape[0]
    label = lax.broadcasted_iota(jnp.int32, (rows, experts), 1)
    member = (rows_ref[:, 0:1] == label) | (rows_ref[:, 1:2] == label)
    both = dot(slots_ref[owner_ref[0]], member.astype(F32).astype(BF16))
    own = (lax.broadcasted_iota(jnp.int32, both.shape, 1) == owner_ref[0]).astype(F32) * both
    gap = jnp.sum(logits * (2.0 * own - both), axis=1, keepdims=True)
    out_ref[...] = jnp.broadcast_to(jax.nn.sigmoid(gap), out_ref.shape)


def fetched(sources, held, sem):
    copies = [pltpu.make_async_copy(a, b, sem.at[i]) for i, (a, b) in enumerate(zip(sources, held))]
    for copy in copies:
        copy.start()
    return copies


def gathered_half(x_ref, held_ref, sem, parity):
    pairs, _, capacity, _ = x_ref.shape
    copies = [pltpu.make_async_copy(x_ref.at[i, parity], held_ref.at[i], sem.at[i]) for i in range(pairs)]
    for copy in copies:
        copy.start()
    return copies


def first_kernel(parity_ref, x_ref, g0_ref, u0_ref, g1_ref, u1_ref, out_ref, g0, u0, g1, u1, x_held, sems, sem):
    theirs = gathered_half(x_ref, x_held, sems, 1 - parity_ref[0])
    copies = fetched((g0_ref, u0_ref, g1_ref, u1_ref), (g0, u0, g1, u1), sem)
    for copy in theirs:
        copy.wait()
    x = x_held[...].reshape(out_ref.shape[0], -1)
    width = g0.shape[1]
    for k, (g, u) in enumerate(((g0, u0), (g1, u1))):
        copies[2 * k].wait()
        gate = dot(x, g[...])
        copies[2 * k + 1].wait()
        out_ref[:, k * width : (k + 1) * width] = (silu(gate) * dot(x, u[...])).astype(BF16)


def second_kernel(parity_ref, x_ref, g0, u0, g1, u1, *refs):
    sources, out_ref, held, x_held, sems, sem = refs[:6], refs[6], refs[7:11], refs[11], refs[12], refs[13]
    ours = gathered_half(x_ref, x_held, sems, parity_ref[0])
    part = sources[2].shape[0]
    targets = held[:2] + tuple(d.at[pl.ds(k * part, part)] for d in held[2:] for k in range(2))
    copies = fetched(sources, targets, sem)
    for copy in ours:
        copy.wait()
    x = x_held[...].reshape(out_ref.shape[0], -1)
    width = g0.shape[1]
    for k, (g, u) in enumerate(((g0, u0), (g1, u1))):
        out_ref[:, k * width : (k + 1) * width] = (silu(dot(x, g[...])) * dot(x, u[...])).astype(BF16)
    for copy in copies:
        copy.wait()


def down_kernel(own_ref, far_ref, d0, d1, d2, d3, out_ref):
    width = d0.shape[0]
    hidden = [ref[:, k * width : (k + 1) * width] for ref in (own_ref, far_ref) for k in range(2)]
    for j in range(0, out_ref.shape[1], 512):
        total = dot(hidden[0], d0[:, j : j + 512])
        for h, d in zip(hidden[1:], (d1, d2, d3)):
            total = total + dot(h, d[:, j : j + 512])
        out_ref[:, j : j + 512] = total.astype(BF16)


def weigh_kernel(got_ref, share_ref, out_ref):
    total = got_ref[0].astype(F32)
    for i in range(1, got_ref.shape[0]):
        total = total + got_ref[i].astype(F32)
    out_ref[0] = (total * share_ref[:, :1]).astype(BF16)


def combine_kernel(got_ref, slots_ref, out_ref):
    total = jnp.zeros(out_ref.shape, F32)
    for e in range(got_ref.shape[0]):
        total = total + lax.dot_general(
            slots_ref[e], got_ref[e], (((0,), (0,)), ((), ())), preferred_element_type=F32
        )
    out_ref[...] = total.astype(BF16)


def final_kernel(own_ref, got_ref, out_ref):
    width = got_ref.shape[2]
    for j in range(got_ref.shape[0]):
        out_ref[:, j * width : (j + 1) * width] = own_ref[j] + got_ref[j].astype(F32)


def shape(dims, dtype=F32):
    return jax.ShapeDtypeStruct(dims, dtype)


SCALAR = pl.BlockSpec(memory_space=pltpu.SMEM)
VM = pl.BlockSpec(memory_space=pltpu.VMEM)


def call(kernel, outs, specs, scratch=(), name=None):
    return pl.pallas_call(
        kernel, out_shape=outs, in_specs=specs, scratch_shapes=list(scratch), compiler_params=WIDE, name=name
    )


def shards(
    layer_input, x_branch, gate_branch, conv_weight, conv_bias, x_proj, dt_proj, dt_bias, a_log, d_skip, carry_state,
    carry_tail, out_proj, steering, refusal, norm_gain, router, specialist_switch_matrix, w_up, w_down, expert_ids,
):
    taps = conv_weight.shape[0]
    length, prompts, channels = x_branch.shape
    rows = length * prompts
    states = a_log.shape[1]
    rank = dt_proj.shape[0]
    d_model = out_proj.shape[1]
    experts = router.shape[1]
    top_count = expert_ids.shape[-1]
    capacity = rows * top_count * 5 // (4 * experts)
    n_seq = lax.axis_size("seq")
    groups = lax.axis_size("expert")
    width = d_model // groups
    own_rows = rows // groups
    place = lax.axis_index("seq").astype(jnp.int32)
    owner = lax.axis_index("expert").astype(jnp.int32)

    near, across = ([(i, i ^ d) for i in range(n_seq)] for d in (1, 2))
    weights = (specialist_switch_matrix[0], w_up[0], w_down[0])
    others = tuple(lax.ppermute(w, "seq", near) for w in weights)

    halo = (taps - 1) * prompts
    x_rows = x_branch.reshape(rows, channels)
    received = lax.ppermute(x_rows[rows - halo :], "seq", [(i, i + 1) for i in range(n_seq - 1)])
    here = (
        a_log.T, carry_state.transpose(0, 2, 1), gate_branch.reshape(rows, channels),
        layer_input.reshape(own_rows, d_model), jnp.stack([place, owner]),
    )

    activated, part = call(
        conv_kernel,
        (shape((rows, channels)), shape((rows, x_proj.shape[1]))),
        [SCALAR] + [VM] * 3 + [pl.BlockSpec(memory_space=pltpu.HBM), VM, pl.BlockSpec(memory_space=pltpu.HBM)],
        [
            pltpu.VMEM((rows + 8, channels), F32),
            pltpu.VMEM(conv_weight.shape, BF16),
            pltpu.VMEM(x_proj.shape[::-1], BF16),
            pltpu.SemaphoreType.DMA((2,)),
        ],
        name="conv",
    )(
        place[None], x_rows, received, carry_tail.reshape(halo, channels),
        pltpu.with_memory_space_constraint(conv_weight, pltpu.HBM), conv_bias[None],
        pltpu.with_memory_space_constraint(x_proj.T, pltpu.HBM),
    )
    part, activated, *here = fence(part, activated, *here)
    summed = exchanged(part, "expert").reshape(groups, own_rows, part.shape[1])
    summed = call(
        functools.partial(sum_kernel, rank),
        shape((groups, own_rows, -(-(rank + 6 * states) // 128) * 128), BF16),
        [VM],
        name="sum",
    )(summed)
    summed, activated, *here = fence(summed, activated, *here)
    projected = exchanged(summed, "expert").reshape(rows, -1)
    projected, activated, *rest = fence(projected, activated, *here, *others)
    (a_log_t, carry_t, gate_rows, own, spot), others = rest[:-3], rest[-3:]
    terms = [projected[:, rank + 2 * states * k : rank + 2 * states * (k + 1)].astype(F32) for k in range(3)]
    bc = (terms[0] + terms[1]) + terms[2]
    bc = jnp.broadcast_to(bc[:, :, None], (rows, 2 * states, 128))
    step, ends = call(
        functools.partial(local_kernel, prompts),
        (shape((rows, channels)), shape((prompts * states + 8, channels), BF16)),
        [VM] * 6,
        name="local",
    )(projected, dt_proj, dt_bias[None], activated, bc, a_log_t)
    ends, step, bc = fence(jnp.broadcast_to(ends[None], (n_seq,) + ends.shape), step, bc)
    every = exchanged(ends, "seq")
    every, step, bc, activated, a_log_t, carry_t, gate_rows, own, down_w = fence(
        every, step, bc, activated, a_log_t, carry_t, gate_rows, own, weights[2]
    )
    part = down_w.shape[0] // 2
    far_a, far_b = (lax.ppermute(down_w[k * part : (k + 1) * part], "seq", across) for k in range(2))
    mixed = call(
        functools.partial(scan_kernel, prompts),
        shape((groups, rows, width), BF16),
        [SCALAR] + [VM] * 9 + [pl.BlockSpec(memory_space=pl.ANY)],
        [pltpu.VMEM((rows, channels), F32), pltpu.VMEM((channels, d_model), BF16), pltpu.SemaphoreType.DMA],
        name="scan",
    )(spot, every, carry_t, step, activated, bc, a_log_t, d_skip[None], gate_rows, own, out_proj)
    mixed, steering, refusal, norm_gain, expert_ids = fence(mixed, steering, refusal, norm_gain, expert_ids)
    mixed = exchanged(mixed, "expert")
    clean = call(clean_kernel, shape((d_model // 128, 128)), [VM] * 2, name="clean")(
        steering.reshape(-1, 128), refusal.reshape(refusal.shape[0], -1, 128)
    )
    start = owner * width
    clean = lax.dynamic_slice_in_dim(clean.reshape(1, d_model), start, width, 1)
    gain = lax.dynamic_slice_in_dim(norm_gain[None], start, width, 1)
    ids = expert_ids.reshape(rows, top_count)

    residual, send, slots = call(
        dispatch_kernel,
        (
            shape((rows, width)),
            shape((experts, capacity, width + 128), BF16),
            shape((experts, capacity, rows), BF16),
        ),
        [VM] * 4,
        name="dispatch",
    )(mixed, clean, gain, ids.T)
    got = exchanged(send, "expert")
    normed = call(
        functools.partial(normed_kernel, float(d_model)), shape((capacity, d_model), BF16), [VM], name="normed"
    )(got)

    same_core = [[i for i in range(n_seq) if i % 2 == c] for c in range(2)]
    normed, far_a = fence(normed, far_a)
    corner_a = lax.ppermute(far_a, "seq", near)
    pieces = lax.all_gather(normed, "seq", axis=0, tiled=True, axis_index_groups=same_core)
    share = call(share_kernel, shape((capacity, 128)), [SCALAR] + [VM] * 4, name="share")(
        owner[None], normed, router.T, slots, ids
    )
    residual, share = fence(residual, share)
    own_residual = exchanged(residual, "expert").reshape(groups, own_rows, width)
    own_residual, share, far_b = fence(own_residual, share, far_b)
    corner_b = lax.ppermute(far_b, "seq", near)
    hbm = pl.BlockSpec(memory_space=pltpu.HBM)
    pieces, own_residual, share, corner_a, corner_b = fence(pieces, own_residual, share, corner_a, corner_b)
    pairs = n_seq // 4
    pieces = pieces.reshape(pairs, 2, capacity, d_model)
    ups = (weights[0], weights[1], others[0], others[1])
    downs = (down_w, others[2], far_a, far_b, corner_a, corner_b)
    half = pairs * capacity
    inner = 2 * ups[0].shape[1]
    dma = pltpu.SemaphoreType.DMA
    parity = ((place // 2) % 2)[None]
    pieces = pltpu.with_memory_space_constraint(pieces, pltpu.HBM)
    held_rows = [pltpu.VMEM((pairs, capacity, d_model), BF16), dma((pairs,))]
    theirs, *ups = pl.pallas_call(
        first_kernel,
        out_shape=(shape((half, inner), BF16),) + tuple(pltpu.VMEM(w.shape, BF16) for w in ups),
        in_specs=[SCALAR] + [hbm] * 5,
        out_specs=(VM,) * 5,
        scratch_shapes=held_rows + [dma((4,))],
        compiler_params=pltpu.CompilerParams(vmem_limit_bytes=16 * 1024 * 1024),
        name="first",
    )(parity, pieces, *(pltpu.with_memory_space_constraint(v, pltpu.HBM) for v in ups))
    given = lax.ppermute(theirs, "seq", across)
    kept, *downs = pl.pallas_call(
        second_kernel,
        out_shape=(shape((half, inner), BF16),) + (pltpu.VMEM(down_w.shape, BF16),) * 4,
        in_specs=[SCALAR, hbm] + [VM] * 4 + [hbm] * 6,
        out_specs=(VM,) * 5,
        scratch_shapes=held_rows + [dma((6,))],
        compiler_params=pltpu.CompilerParams(vmem_limit_bytes=16 * 1024 * 1024),
        cost_estimate=pl.CostEstimate(flops=4 * half * inner * d_model, bytes_accessed=1 << 24, transcendentals=0),
        name="second",
    )(parity, pieces, *ups, *(pltpu.with_memory_space_constraint(v, pltpu.HBM) for v in downs))
    partial = pl.pallas_call(
        down_kernel,
        out_shape=pltpu.VMEM((half, d_model), BF16),
        in_specs=[VM] * 6,
        out_specs=VM,
        compiler_params=pltpu.CompilerParams(vmem_limit_bytes=16 * 1024 * 1024),
        name="down",
    )(kept, given, *downs)
    kinds = [[i for i in range(n_seq) if i % 4 == k] for k in range(4)]
    partial, share, slots, own_residual = fence(partial, share, slots, own_residual)
    partial = exchanged(partial, "seq", kinds).reshape(pairs, capacity, d_model)
    partial, share, slots, own_residual = fence(partial, share, slots, own_residual)
    weighted = pl.pallas_call(
        weigh_kernel,
        grid=(groups,),
        out_shape=shape((groups, capacity, width), BF16),
        in_specs=[
            pl.BlockSpec((pairs, capacity, width), lambda j: (0, 0, j)),
            pl.BlockSpec((capacity, 128), lambda j: (0, 0)),
        ],
        out_specs=pl.BlockSpec((1, capacity, width), lambda j: (j, 0, 0)),
        compiler_params=WIDE,
        name="weigh",
    )(partial, share)
    back = exchanged(weighted, "expert")
    total = call(combine_kernel, shape((rows, width), BF16), [VM] * 2, name="combine")(back, slots)
    out = exchanged(total, "expert").reshape(groups, own_rows, width)
    out = call(final_kernel, shape((own_rows, d_model)), [VM] * 2, name="final")(own_residual, out)
    return out.reshape(own_rows // prompts, prompts, d_model)


def solution(mesh):
    return jax.shard_map(
        shards,
        mesh=mesh,
        in_specs=(
            P(("seq", "expert"), None, None),
            P("seq", None, "expert"),
            P("seq", None, "expert"),
            P(None, "expert"),
            P("expert"),
            P("expert", None),
            P(None, "expert"),
            P("expert"),
            P("expert", None),
            P("expert"),
            P(None, "expert", None),
            P(None, None, "expert"),
            P("expert", None),
            P(),
            P(),
            P(),
            P(),
            P("expert", None, "seq"),
            P("expert", None, "seq"),
            P("expert", "seq", None),
            P("seq", None, None),
        ),
        out_specs=P(("seq", "expert"), None, None),
        check_vma=False,
    )
```

```python
import functools

import jax
import jax.numpy as jnp
from jax import lax
from jax.experimental import pallas as pl
from jax.experimental.pallas import tpu as pltpu
from jax.sharding import PartitionSpec as P

EPS = 1e-06
LOG2E = 1.4426950408889634
F32 = jnp.float32
BF16 = jnp.bfloat16
WIDE = pltpu.CompilerParams(vmem_limit_bytes=40 * 1024 * 1024)


def silu(v):
    return v * jax.nn.sigmoid(v)


def dot(a, b):
    return jnp.dot(a, b, preferred_element_type=F32)


def fence(*values):
    return lax.optimization_barrier(values)


def exchanged(blocks, axis, groups=None):
    return lax.all_to_all(blocks, axis, 0, 0, tiled=True, axis_index_groups=groups)


def conv_kernel(
    lead_ref, x_ref, got_ref, carry_ref, taps_ref, b_ref, proj_ref, act_ref, part_ref, pad_ref, w_ref, xp_ref, sem
):
    copies = [pltpu.make_async_copy(a, b, sem.at[i]) for i, (a, b) in enumerate(((taps_ref, w_ref), (proj_ref, xp_ref)))]
    for copy in copies:
        copy.start()
    rows = x_ref.shape[0]
    taps = w_ref.shape[0]
    halo = got_ref.shape[0]
    step = halo // (taps - 1)
    first = lead_ref[0] == 0
    pad_ref[:halo, :] = jnp.where(first, carry_ref[...].astype(F32), got_ref[...].astype(F32))
    pad_ref[halo : halo + rows, :] = x_ref[...].astype(F32)
    total = b_ref[...].astype(F32)
    copies[0].wait()
    w = w_ref[...].astype(F32)
    for k in range(taps):
        total = total + w[k : k + 1, :] * pad_ref[k * step : k * step + rows, :]
    act = silu(total)
    act_ref[...] = act
    copies[1].wait()
    part_ref[...] = lax.dot_general(act.astype(BF16), xp_ref[...], (((1,), (1,)), ((), ())), preferred_element_type=F32)


def sum_kernel(rank, got_ref, out_ref):
    total = got_ref[0]
    for j in range(1, got_ref.shape[0]):
        total = total + got_ref[j]
    rest = total[:, rank:]
    high = rest.astype(BF16).astype(F32)
    middle = (rest - high).astype(BF16).astype(F32)
    out = [total[:, :rank], high, middle, rest - high - middle]
    pad = out_ref.shape[2] - rank - 3 * rest.shape[1]
    out = jnp.concatenate(out + [jnp.zeros((rest.shape[0], pad), F32)], axis=1).astype(BF16)
    for j in range(out_ref.shape[0]):
        out_ref[j] = out


def advance(state, rate, step, drive, b):
    return jnp.exp2(step * rate) * state + drive * b


def local_kernel(prompts, proj_ref, dtp_ref, dtb_ref, act_ref, bc_ref, alog_ref, step_ref, out_ref):
    rows, channels = act_ref.shape
    states = alog_ref.shape[0]
    rank = dtp_ref.shape[0]
    low = proj_ref[:, :rank]
    step_ref[...] = jax.nn.softplus(dot(low, dtp_ref[...]) + dtb_ref[...])
    rate = -jnp.exp(alog_ref[...]) * LOG2E

    def body(i, carried):
        carried = list(carried)
        at = pl.multiple_of(i * 8, 8)
        step = step_ref[pl.ds(at, 8), :]
        drive = step * act_ref[pl.ds(at, 8), :]
        for r in range(8):
            p = r % prompts
            b = jnp.tile(bc_ref[at + r, :states, :], (1, channels // 128))
            carried[p] = advance(carried[p], rate, step[r : r + 1, :], drive[r : r + 1, :], b)
        return tuple(carried)

    zero = jnp.zeros((states, channels), F32)
    ends = lax.fori_loop(0, rows // 8, body, (zero,) * prompts)
    for p in range(prompts):
        out_ref[p * states : (p + 1) * states, :] = ends[p].astype(BF16)
    step = step_ref[...].reshape(rows // 8, 8, channels).sum(axis=0)
    sums = [sum(step[r : r + 1, :] for r in range(p, 8, prompts)) for p in range(prompts)]
    high = [s.astype(BF16).astype(F32) for s in sums]
    low_part = [(s - h) for s, h in zip(sums, high)]
    rest = jnp.zeros((8 - 2 * prompts, channels), F32)
    out_ref[prompts * states :, :] = jnp.concatenate(high + low_part + [rest], axis=0).astype(BF16)


def scan_kernel(
    prompts, ids_ref, all_ref, carry_ref, step_ref, act_ref, bc_ref, alog_ref, skip_ref, gate_ref, own_ref,
    outp_ref, mixed_ref, y_ref, w_ref, sem,
):
    rows, channels = act_ref.shape
    states = alog_ref.shape[0]
    copy = pltpu.make_async_copy(outp_ref, w_ref, sem)
    copy.start()
    rate = -jnp.exp(alog_ref[...]) * LOG2E

    def earlier(j, carried):
        block = all_ref[j].astype(F32)
        at = prompts * states
        out = []
        for p in range(prompts):
            total = block[at + p : at + p + 1, :] + block[at + prompts + p : at + prompts + p + 1, :]
            out.append(jnp.exp2(total * rate) * carried[p] + block[p * states : (p + 1) * states, :])
        return tuple(out)

    entering = lax.fori_loop(0, ids_ref[0], earlier, tuple(carry_ref[p] for p in range(prompts)))

    def body(i, carried):
        carried = list(carried)
        at = pl.multiple_of(i * 8, 8)
        step = step_ref[pl.ds(at, 8), :]
        drive = step * act_ref[pl.ds(at, 8), :]
        outs = []
        for r in range(8):
            p = r % prompts
            bc = bc_ref[at + r]
            b = jnp.tile(bc[:states], (1, channels // 128))
            c = jnp.tile(bc[states:], (1, channels // 128))
            carried[p] = advance(carried[p], rate, step[r : r + 1, :], drive[r : r + 1, :], b)
            outs.append(jnp.sum(carried[p] * c, axis=0, keepdims=True))
        y_ref[pl.ds(at, 8), :] = jnp.concatenate(outs, axis=0)
        return tuple(carried)

    lax.fori_loop(0, rows // 8, body, entering)
    y = y_ref[...] + skip_ref[...] * act_ref[...]
    gated = (y * silu(gate_ref[...].astype(F32))).astype(BF16)
    copy.wait()
    blocks, _, width = mixed_ref.shape
    own_rows = own_ref.shape[0]
    row_group = lax.broadcasted_iota(jnp.int32, (rows, width), 0) // own_rows
    mine = row_group == ids_ref[1]
    for j in range(blocks):
        part = dot(gated, w_ref[:, j * width : (j + 1) * width])
        own = jnp.tile(own_ref[:, j * width : (j + 1) * width].astype(F32), (rows // own_rows, 1))
        mixed_ref[j] = (part + jnp.where(mine, own, 0.0)).astype(BF16)


def clean_kernel(steer_ref, refusal_ref, out_ref):
    vector = steer_ref[...].astype(F32)
    units = []
    for k in range(refusal_ref.shape[0]):
        r = refusal_ref[k].astype(F32)
        for q in units:
            r = r - jnp.sum(q * r) * q
        r = r * lax.rsqrt(jnp.sum(r * r) + EPS)
        units.append(r)
    for q in units:
        vector = vector - jnp.sum(q * vector) * q
    out_ref[...] = vector


def dispatch_kernel(mixed_ref, clean_ref, gain_ref, lanes_ref, res_ref, send_ref, slots_ref):
    experts, capacity, rows = slots_ref.shape
    width = res_ref.shape[1]
    residual = clean_ref[...]
    for j in range(mixed_ref.shape[0]):
        residual = residual + mixed_ref[j].astype(F32)
    res_ref[...] = residual
    scaled = (residual * gain_ref[...].astype(F32)).astype(BF16)
    square = jnp.sum(residual * residual, axis=1, keepdims=True)
    high = square.astype(BF16).astype(F32)
    middle = (square - high).astype(BF16).astype(F32)
    low = square - high - middle
    lane = lax.broadcasted_iota(jnp.int32, (rows, 128), 1)
    extra = jnp.where(lane == 0, high, jnp.where(lane == 1, middle, jnp.where(lane == 2, low, 0.0)))
    payload = jnp.concatenate([scaled, extra.astype(BF16)], axis=1)
    label = lax.broadcasted_iota(jnp.int32, (experts, rows), 0)
    member = (lanes_ref[0:1, :] == label) | (lanes_ref[1:2, :] == label)
    upper = lax.broadcasted_iota(jnp.int32, (rows, rows), 0) <= lax.broadcasted_iota(jnp.int32, (rows, rows), 1)
    order = dot(member.astype(F32).astype(BF16), upper.astype(F32).astype(BF16))
    place = jnp.where(member, order - 1.0, -1.0)
    slot = lax.broadcasted_iota(jnp.int32, (capacity, rows), 0).astype(F32)
    for e in range(experts):
        chosen = (place[e : e + 1, :] == slot).astype(F32).astype(BF16)
        slots_ref[e] = chosen
        send_ref[e] = dot(chosen, payload).astype(BF16)


def normed_kernel(features, got_ref, out_ref):
    width = out_ref.shape[1] // got_ref.shape[0]
    total = jnp.zeros((out_ref.shape[0], 128), F32)
    for j in range(got_ref.shape[0]):
        total = total + got_ref[j, :, width:].astype(F32)
    scale = lax.rsqrt(jnp.sum(total, axis=1, keepdims=True) / features + EPS)
    for j in range(got_ref.shape[0]):
        out_ref[:, j * width : (j + 1) * width] = (got_ref[j, :, :width].astype(F32) * scale).astype(BF16)


def share_kernel(owner_ref, x_ref, router_ref, slots_ref, rows_ref, out_ref):
    logits = lax.dot_general(x_ref[...], router_ref[...], (((1,), (1,)), ((), ())), preferred_element_type=F32)
    experts = router_ref.shape[0]
    rows = rows_ref.shape[0]
    label = lax.broadcasted_iota(jnp.int32, (rows, experts), 1)
    member = (rows_ref[:, 0:1] == label) | (rows_ref[:, 1:2] == label)
    both = dot(slots_ref[owner_ref[0]], member.astype(F32).astype(BF16))
    own = (lax.broadcasted_iota(jnp.int32, both.shape, 1) == owner_ref[0]).astype(F32) * both
    gap = jnp.sum(logits * (2.0 * own - both), axis=1, keepdims=True)
    out_ref[...] = jnp.broadcast_to(jax.nn.sigmoid(gap), out_ref.shape)


def fetched(sources, held, sem):
    copies = [pltpu.make_async_copy(a, b, sem.at[i]) for i, (a, b) in enumerate(zip(sources, held))]
    for copy in copies:
        copy.start()
    return copies


def sliced(source, target, sem, parts, axis):
    size = target.shape[axis] // parts
    at = lambda k: (slice(None),) * axis + (pl.ds(k * size, size),)
    return [pltpu.make_async_copy(source.at[at(k)], target.at[at(k)], sem.at[k]) for k in range(parts)]


def hidden_of(x_held, x_copies, weights, weight_copies, out_ref):
    parts = len(x_copies)
    size = x_held.shape[2] // parts
    totals = None
    for k in range(parts):
        x_copies[k].wait()
        for copies in weight_copies:
            copies[k].wait()
        x = x_held[:, :, k * size : (k + 1) * size].reshape(out_ref.shape[0], size)
        terms = [dot(x, w[k * size : (k + 1) * size, :]) for w in weights]
        totals = terms if totals is None else [a + b for a, b in zip(totals, terms)]
    width = weights[0].shape[1]
    for k in range(2):
        out_ref[:, k * width : (k + 1) * width] = (silu(totals[2 * k]) * totals[2 * k + 1]).astype(BF16)


def first_kernel(parity_ref, x_ref, g0_ref, u0_ref, g1_ref, u1_ref, out_ref, g0, u0, g1, u1, x_held, x_sem, sems):
    parts = x_sem.shape[0]
    x_copies = sliced(x_ref.at[:, 1 - parity_ref[0]], x_held, x_sem, parts, 2)
    held = (g0, u0, g1, u1)
    sources = (g0_ref, u0_ref, g1_ref, u1_ref)
    weight_copies = [sliced(a, b, sems.at[i], parts, 0) for i, (a, b) in enumerate(zip(sources, held))]
    for k in range(parts):
        x_copies[k].start()
        for copies in weight_copies:
            copies[k].start()
    hidden_of(x_held, x_copies, held, weight_copies, out_ref)


def second_kernel(parity_ref, x_ref, g0, u0, g1, u1, *refs):
    sources, out_ref, held, x_held, x_sem, sem = refs[:6], refs[6], refs[7:11], refs[11], refs[12], refs[13]
    x_copies = sliced(x_ref.at[:, parity_ref[0]], x_held, x_sem, x_sem.shape[0], 2)
    for copy in x_copies:
        copy.start()
    part = sources[2].shape[0]
    targets = held[:2] + tuple(d.at[pl.ds(k * part, part)] for d in held[2:] for k in range(2))
    copies = fetched(sources, targets, sem)
    hidden_of(x_held, x_copies, (g0, u0, g1, u1), (), out_ref)
    for copy in copies:
        copy.wait()


def down_kernel(own_ref, far_ref, d0, d1, d2, d3, out_ref):
    width = d0.shape[0]
    hidden = [ref[:, k * width : (k + 1) * width] for ref in (own_ref, far_ref) for k in range(2)]
    for j in range(0, out_ref.shape[1], 512):
        total = dot(hidden[0], d0[:, j : j + 512])
        for h, d in zip(hidden[1:], (d1, d2, d3)):
            total = total + dot(h, d[:, j : j + 512])
        out_ref[:, j : j + 512] = total.astype(BF16)


def weigh_kernel(got_ref, share_ref, out_ref):
    total = got_ref[0].astype(F32)
    for i in range(1, got_ref.shape[0]):
        total = total + got_ref[i].astype(F32)
    out_ref[0] = (total * share_ref[:, :1]).astype(BF16)


def combine_kernel(got_ref, slots_ref, out_ref):
    total = jnp.zeros(out_ref.shape, F32)
    for e in range(got_ref.shape[0]):
        total = total + lax.dot_general(
            slots_ref[e], got_ref[e], (((0,), (0,)), ((), ())), preferred_element_type=F32
        )
    out_ref[...] = total.astype(BF16)


def final_kernel(own_ref, got_ref, out_ref):
    width = got_ref.shape[2]
    for j in range(got_ref.shape[0]):
        total = own_ref[j] + got_ref[j].astype(F32)
        out_ref[:, :, j * width : (j + 1) * width] = total.reshape(out_ref.shape[0], out_ref.shape[1], width)


def shape(dims, dtype=F32):
    return jax.ShapeDtypeStruct(dims, dtype)


SCALAR = pl.BlockSpec(memory_space=pltpu.SMEM)
VM = pl.BlockSpec(memory_space=pltpu.VMEM)


def call(kernel, outs, specs, scratch=(), name=None):
    return pl.pallas_call(
        kernel, out_shape=outs, in_specs=specs, scratch_shapes=list(scratch), compiler_params=WIDE, name=name
    )


def shards(
    layer_input, x_branch, gate_branch, conv_weight, conv_bias, x_proj, dt_proj, dt_bias, a_log, d_skip, carry_state,
    carry_tail, out_proj, steering, refusal, norm_gain, router, specialist_switch_matrix, w_up, w_down, expert_ids,
):
    taps = conv_weight.shape[0]
    length, prompts, channels = x_branch.shape
    rows = length * prompts
    states = a_log.shape[1]
    rank = dt_proj.shape[0]
    d_model = out_proj.shape[1]
    experts = router.shape[1]
    top_count = expert_ids.shape[-1]
    capacity = rows * top_count * 5 // (4 * experts)
    n_seq = lax.axis_size("seq")
    groups = lax.axis_size("expert")
    width = d_model // groups
    own_rows = rows // groups
    place = lax.axis_index("seq").astype(jnp.int32)
    owner = lax.axis_index("expert").astype(jnp.int32)

    near, across = ([(i, i ^ d) for i in range(n_seq)] for d in (1, 2))
    weights = (specialist_switch_matrix[0], w_up[0], w_down[0])
    others = tuple(lax.ppermute(w, "seq", near) for w in weights)

    halo = (taps - 1) * prompts
    x_rows = x_branch.reshape(rows, channels)
    received = lax.ppermute(x_rows[rows - halo :], "seq", [(i, i + 1) for i in range(n_seq - 1)])
    here = (
        a_log.T, carry_state.transpose(0, 2, 1), gate_branch.reshape(rows, channels),
        layer_input.reshape(own_rows, d_model), jnp.stack([place, owner]),
    )

    activated, part = call(
        conv_kernel,
        (shape((rows, channels)), shape((rows, x_proj.shape[1]))),
        [SCALAR] + [VM] * 3 + [pl.BlockSpec(memory_space=pltpu.HBM), VM, pl.BlockSpec(memory_space=pltpu.HBM)],
        [
            pltpu.VMEM((rows + 8, channels), F32),
            pltpu.VMEM(conv_weight.shape, BF16),
            pltpu.VMEM(x_proj.shape[::-1], BF16),
            pltpu.SemaphoreType.DMA((2,)),
        ],
        name="conv",
    )(
        place[None], x_rows, received, carry_tail.reshape(halo, channels),
        pltpu.with_memory_space_constraint(conv_weight, pltpu.HBM), conv_bias[None],
        pltpu.with_memory_space_constraint(x_proj.T, pltpu.HBM),
    )
    part, activated, *here = fence(part, activated, *here)
    summed = exchanged(part, "expert").reshape(groups, own_rows, part.shape[1])
    summed = call(
        functools.partial(sum_kernel, rank),
        shape((groups, own_rows, -(-(rank + 6 * states) // 128) * 128), BF16),
        [VM],
        name="sum",
    )(summed)
    summed, activated, *here = fence(summed, activated, *here)
    projected = exchanged(summed, "expert").reshape(rows, -1)
    projected, activated, *rest = fence(projected, activated, *here, *others)
    (a_log_t, carry_t, gate_rows, own, spot), others = rest[:-3], rest[-3:]
    terms = [projected[:, rank + 2 * states * k : rank + 2 * states * (k + 1)].astype(F32) for k in range(3)]
    bc = (terms[0] + terms[1]) + terms[2]
    bc = jnp.broadcast_to(bc[:, :, None], (rows, 2 * states, 128))
    step, ends = call(
        functools.partial(local_kernel, prompts),
        (shape((rows, channels)), shape((prompts * states + 8, channels), BF16)),
        [VM] * 6,
        name="local",
    )(projected, dt_proj, dt_bias[None], activated, bc, a_log_t)
    ends, step, bc = fence(jnp.broadcast_to(ends[None], (n_seq,) + ends.shape), step, bc)
    every = exchanged(ends, "seq")
    every, step, bc, activated, a_log_t, carry_t, gate_rows, own, down_w = fence(
        every, step, bc, activated, a_log_t, carry_t, gate_rows, own, weights[2]
    )
    part = down_w.shape[0] // 2
    far_a, far_b = (lax.ppermute(down_w[k * part : (k + 1) * part], "seq", across) for k in range(2))
    mixed = call(
        functools.partial(scan_kernel, prompts),
        shape((groups, rows, width), BF16),
        [SCALAR] + [VM] * 9 + [pl.BlockSpec(memory_space=pl.ANY)],
        [pltpu.VMEM((rows, channels), F32), pltpu.VMEM((channels, d_model), BF16), pltpu.SemaphoreType.DMA],
        name="scan",
    )(spot, every, carry_t, step, activated, bc, a_log_t, d_skip[None], gate_rows, own, out_proj)
    mixed, steering, refusal, norm_gain, expert_ids = fence(mixed, steering, refusal, norm_gain, expert_ids)
    mixed = exchanged(mixed, "expert")
    clean = call(clean_kernel, shape((d_model // 128, 128)), [VM] * 2, name="clean")(
        steering.reshape(-1, 128), refusal.reshape(refusal.shape[0], -1, 128)
    )
    start = owner * width
    clean = lax.dynamic_slice_in_dim(clean.reshape(1, d_model), start, width, 1)
    gain = lax.dynamic_slice_in_dim(norm_gain[None], start, width, 1)
    ids = expert_ids.reshape(rows, top_count)

    residual, send, slots = call(
        dispatch_kernel,
        (
            shape((rows, width)),
            shape((experts, capacity, width + 128), BF16),
            shape((experts, capacity, rows), BF16),
        ),
        [VM] * 4,
        name="dispatch",
    )(mixed, clean, gain, ids.T)
    got = exchanged(send, "expert")
    normed = call(
        functools.partial(normed_kernel, float(d_model)), shape((capacity, d_model), BF16), [VM], name="normed"
    )(got)

    same_core = [[i for i in range(n_seq) if i % 2 == c] for c in range(2)]
    normed, far_a = fence(normed, far_a)
    corner_a = lax.ppermute(far_a, "seq", near)
    pieces = lax.all_gather(normed, "seq", axis=0, tiled=True, axis_index_groups=same_core)
    share = call(share_kernel, shape((capacity, 128)), [SCALAR] + [VM] * 4, name="share")(
        owner[None], normed, router.T, slots, ids
    )
    residual, share = fence(residual, share)
    own_residual = exchanged(residual, "expert").reshape(groups, own_rows, width)
    own_residual, share, far_b = fence(own_residual, share, far_b)
    corner_b = lax.ppermute(far_b, "seq", near)
    hbm = pl.BlockSpec(memory_space=pltpu.HBM)
    pieces, own_residual, share, corner_a, corner_b = fence(pieces, own_residual, share, corner_a, corner_b)
    pairs = n_seq // 4
    pieces = pieces.reshape(pairs, 2, capacity, d_model)
    ups = (weights[0], weights[1], others[0], others[1])
    downs = (down_w, others[2], far_a, far_b, corner_a, corner_b)
    half = pairs * capacity
    inner = 2 * ups[0].shape[1]
    dma = pltpu.SemaphoreType.DMA
    parity = ((place // 2) % 2)[None]
    pieces = pltpu.with_memory_space_constraint(pieces, pltpu.HBM)
    parts = 4
    held_rows = [pltpu.VMEM((pairs, capacity, d_model), BF16), dma((parts,))]
    theirs, *ups = pl.pallas_call(
        first_kernel,
        out_shape=(shape((half, inner), BF16),) + tuple(pltpu.VMEM(w.shape, BF16) for w in ups),
        in_specs=[SCALAR] + [hbm] * 5,
        out_specs=(VM,) * 5,
        scratch_shapes=held_rows + [dma((4, parts))],
        compiler_params=pltpu.CompilerParams(vmem_limit_bytes=16 * 1024 * 1024),
        name="first",
    )(parity, pieces, *(pltpu.with_memory_space_constraint(v, pltpu.HBM) for v in ups))
    given = lax.ppermute(theirs, "seq", across)
    kept, *downs = pl.pallas_call(
        second_kernel,
        out_shape=(shape((half, inner), BF16),) + (pltpu.VMEM(down_w.shape, BF16),) * 4,
        in_specs=[SCALAR, hbm] + [VM] * 4 + [hbm] * 6,
        out_specs=(VM,) * 5,
        scratch_shapes=held_rows + [dma((6,))],
        compiler_params=pltpu.CompilerParams(vmem_limit_bytes=16 * 1024 * 1024),
        cost_estimate=pl.CostEstimate(flops=4 * half * inner * d_model, bytes_accessed=1 << 24, transcendentals=0),
        name="second",
    )(parity, pieces, *ups, *(pltpu.with_memory_space_constraint(v, pltpu.HBM) for v in downs))
    partial = pl.pallas_call(
        down_kernel,
        out_shape=pltpu.VMEM((half, d_model), BF16),
        in_specs=[VM] * 6,
        out_specs=VM,
        compiler_params=pltpu.CompilerParams(vmem_limit_bytes=16 * 1024 * 1024),
        name="down",
    )(kept, given, *downs)
    kinds = [[i for i in range(n_seq) if i % 4 == k] for k in range(4)]
    partial, share, slots, own_residual = fence(partial, share, slots, own_residual)
    partial = exchanged(partial, "seq", kinds).reshape(pairs, capacity, d_model)
    partial, share, slots, own_residual = fence(partial, share, slots, own_residual)
    weighted = pl.pallas_call(
        weigh_kernel,
        grid=(groups,),
        out_shape=shape((groups, capacity, width), BF16),
        in_specs=[
            pl.BlockSpec((pairs, capacity, width), lambda j: (0, 0, j)),
            pl.BlockSpec((capacity, 128), lambda j: (0, 0)),
        ],
        out_specs=pl.BlockSpec((1, capacity, width), lambda j: (j, 0, 0)),
        compiler_params=WIDE,
        name="weigh",
    )(partial, share)
    back = exchanged(weighted, "expert")
    total = call(combine_kernel, shape((rows, width), BF16), [VM] * 2, name="combine")(back, slots)
    out = exchanged(total, "expert").reshape(groups, own_rows, width)
    return call(final_kernel, shape((own_rows // prompts, prompts, d_model)), [VM] * 2, name="final")(own_residual, out)


def solution(mesh):
    return jax.shard_map(
        shards,
        mesh=mesh,
        in_specs=(
            P(("seq", "expert"), None, None),
            P("seq", None, "expert"),
            P("seq", None, "expert"),
            P(None, "expert"),
            P("expert"),
            P("expert", None),
            P(None, "expert"),
            P("expert"),
            P("expert", None),
            P("expert"),
            P(None, "expert", None),
            P(None, None, "expert"),
            P("expert", None),
            P(),
            P(),
            P(),
            P(),
            P("expert", None, "seq"),
            P("expert", None, "seq"),
            P("expert", "seq", None),
            P("seq", None, None),
        ),
        out_specs=P(("seq", "expert"), None, None),
        check_vma=False,
    )
```

```python
import functools

import jax
import jax.numpy as jnp
from jax import lax
from jax.experimental import pallas as pl
from jax.experimental.pallas import tpu as pltpu
from jax.sharding import PartitionSpec as P

EPS = 1e-06
LOG2E = 1.4426950408889634
F32 = jnp.float32
BF16 = jnp.bfloat16
WIDE = pltpu.CompilerParams(vmem_limit_bytes=40 * 1024 * 1024)


def silu(v):
    return v * jax.nn.sigmoid(v)


def dot(a, b):
    return jnp.dot(a, b, preferred_element_type=F32)


def fence(*values):
    return lax.optimization_barrier(values)


def exchanged(blocks, axis, groups=None):
    return lax.all_to_all(blocks, axis, 0, 0, tiled=True, axis_index_groups=groups)


def conv_kernel(
    lead_ref, x_ref, got_ref, carry_ref, taps_ref, b_ref, proj_ref, act_ref, part_ref, pad_ref, w_ref, xp_ref, sem
):
    copies = [pltpu.make_async_copy(a, b, sem.at[i]) for i, (a, b) in enumerate(((taps_ref, w_ref), (proj_ref, xp_ref)))]
    for copy in copies:
        copy.start()
    rows = x_ref.shape[0]
    taps = w_ref.shape[0]
    halo = got_ref.shape[0]
    step = halo // (taps - 1)
    first = lead_ref[0] == 0
    pad_ref[:halo, :] = jnp.where(first, carry_ref[...].astype(F32), got_ref[...].astype(F32))
    pad_ref[halo : halo + rows, :] = x_ref[...].astype(F32)
    total = b_ref[...].astype(F32)
    copies[0].wait()
    w = w_ref[...].astype(F32)
    for k in range(taps):
        total = total + w[k : k + 1, :] * pad_ref[k * step : k * step + rows, :]
    act = silu(total)
    act_ref[...] = act
    copies[1].wait()
    part_ref[...] = lax.dot_general(act.astype(BF16), xp_ref[...], (((1,), (1,)), ((), ())), preferred_element_type=F32)


def sum_kernel(rank, got_ref, out_ref):
    total = got_ref[0]
    for j in range(1, got_ref.shape[0]):
        total = total + got_ref[j]
    rest = total[:, rank:]
    high = rest.astype(BF16).astype(F32)
    middle = (rest - high).astype(BF16).astype(F32)
    out = [total[:, :rank], high, middle, rest - high - middle]
    pad = out_ref.shape[2] - rank - 3 * rest.shape[1]
    out = jnp.concatenate(out + [jnp.zeros((rest.shape[0], pad), F32)], axis=1).astype(BF16)
    for j in range(out_ref.shape[0]):
        out_ref[j] = out


def advance(state, rate, step, drive, b):
    return jnp.exp2(step * rate) * state + drive * b


def local_kernel(prompts, proj_ref, dtp_ref, dtb_ref, act_ref, bc_ref, alog_ref, step_ref, out_ref):
    rows, channels = act_ref.shape
    states = alog_ref.shape[0]
    rank = dtp_ref.shape[0]
    low = proj_ref[:, :rank]
    step_ref[...] = jax.nn.softplus(dot(low, dtp_ref[...]) + dtb_ref[...])
    rate = -jnp.exp(alog_ref[...]) * LOG2E

    def body(i, carried):
        carried = list(carried)
        at = pl.multiple_of(i * 8, 8)
        step = step_ref[pl.ds(at, 8), :]
        drive = step * act_ref[pl.ds(at, 8), :]
        for r in range(8):
            p = r % prompts
            b = jnp.tile(bc_ref[at + r, :states, :], (1, channels // 128))
            carried[p] = advance(carried[p], rate, step[r : r + 1, :], drive[r : r + 1, :], b)
        return tuple(carried)

    zero = jnp.zeros((states, channels), F32)
    ends = lax.fori_loop(0, rows // 8, body, (zero,) * prompts)
    for p in range(prompts):
        out_ref[p * states : (p + 1) * states, :] = ends[p].astype(BF16)
    step = step_ref[...].reshape(rows // 8, 8, channels).sum(axis=0)
    sums = [sum(step[r : r + 1, :] for r in range(p, 8, prompts)) for p in range(prompts)]
    high = [s.astype(BF16).astype(F32) for s in sums]
    low_part = [(s - h) for s, h in zip(sums, high)]
    rest = jnp.zeros((8 - 2 * prompts, channels), F32)
    out_ref[prompts * states :, :] = jnp.concatenate(high + low_part + [rest], axis=0).astype(BF16)


def scan_kernel(
    prompts, ids_ref, all_ref, carry_ref, step_ref, act_ref, bc_ref, alog_ref, skip_ref, gate_ref, own_ref,
    outp_ref, mixed_ref, y_ref, w_ref, sem,
):
    rows, channels = act_ref.shape
    states = alog_ref.shape[0]
    copy = pltpu.make_async_copy(outp_ref, w_ref, sem)
    copy.start()
    rate = -jnp.exp(alog_ref[...]) * LOG2E

    def earlier(j, carried):
        block = all_ref[j].astype(F32)
        at = prompts * states
        out = []
        for p in range(prompts):
            total = block[at + p : at + p + 1, :] + block[at + prompts + p : at + prompts + p + 1, :]
            out.append(jnp.exp2(total * rate) * carried[p] + block[p * states : (p + 1) * states, :])
        return tuple(out)

    entering = lax.fori_loop(0, ids_ref[0], earlier, tuple(carry_ref[p] for p in range(prompts)))

    def body(i, carried):
        carried = list(carried)
        at = pl.multiple_of(i * 8, 8)
        step = step_ref[pl.ds(at, 8), :]
        drive = step * act_ref[pl.ds(at, 8), :]
        outs = []
        for r in range(8):
            p = r % prompts
            bc = bc_ref[at + r]
            b = jnp.tile(bc[:states], (1, channels // 128))
            c = jnp.tile(bc[states:], (1, channels // 128))
            carried[p] = advance(carried[p], rate, step[r : r + 1, :], drive[r : r + 1, :], b)
            outs.append(jnp.sum(carried[p] * c, axis=0, keepdims=True))
        y_ref[pl.ds(at, 8), :] = jnp.concatenate(outs, axis=0)
        return tuple(carried)

    lax.fori_loop(0, rows // 8, body, entering)
    y = y_ref[...] + skip_ref[...] * act_ref[...]
    gated = (y * silu(gate_ref[...].astype(F32))).astype(BF16)
    copy.wait()
    blocks, _, width = mixed_ref.shape
    own_rows = own_ref.shape[0]
    row_group = lax.broadcasted_iota(jnp.int32, (rows, width), 0) // own_rows
    mine = row_group == ids_ref[1]
    for j in range(blocks):
        part = dot(gated, w_ref[:, j * width : (j + 1) * width])
        own = jnp.tile(own_ref[:, j * width : (j + 1) * width].astype(F32), (rows // own_rows, 1))
        mixed_ref[j] = (part + jnp.where(mine, own, 0.0)).astype(BF16)


def clean_kernel(steer_ref, refusal_ref, out_ref):
    vector = steer_ref[...].astype(F32)
    units = []
    for k in range(refusal_ref.shape[0]):
        r = refusal_ref[k].astype(F32)
        for q in units:
            r = r - jnp.sum(q * r) * q
        r = r * lax.rsqrt(jnp.sum(r * r) + EPS)
        units.append(r)
    for q in units:
        vector = vector - jnp.sum(q * vector) * q
    out_ref[...] = vector


def dispatch_kernel(mixed_ref, clean_ref, lanes_ref, res_ref, send_ref, slots_ref):
    experts, capacity, rows = slots_ref.shape
    width = res_ref.shape[1]
    residual = clean_ref[...]
    for j in range(mixed_ref.shape[0]):
        residual = residual + mixed_ref[j].astype(F32)
    res_ref[...] = residual
    payload = residual.astype(BF16)
    label = lax.broadcasted_iota(jnp.int32, (experts, rows), 0)
    member = (lanes_ref[0:1, :] == label) | (lanes_ref[1:2, :] == label)
    upper = lax.broadcasted_iota(jnp.int32, (rows, rows), 0) <= lax.broadcasted_iota(jnp.int32, (rows, rows), 1)
    order = dot(member.astype(F32).astype(BF16), upper.astype(F32).astype(BF16))
    place = jnp.where(member, order - 1.0, -1.0)
    slot = lax.broadcasted_iota(jnp.int32, (capacity, rows), 0).astype(F32)
    for e in range(experts):
        chosen = (place[e : e + 1, :] == slot).astype(F32).astype(BF16)
        slots_ref[e] = chosen
        send_ref[e] = dot(chosen, payload).astype(BF16)


def normed_kernel(got_ref, gain_ref, out_ref):
    blocks, rows, width = got_ref.shape
    total = jnp.zeros((rows, width), F32)
    for j in range(blocks):
        block = got_ref[j].astype(F32)
        total = total + block * block
    scale = lax.rsqrt(jnp.sum(total, axis=1, keepdims=True) / (blocks * width) + EPS)
    for j in range(blocks):
        at = slice(j * width, (j + 1) * width)
        out_ref[:, at] = (got_ref[j].astype(F32) * scale * gain_ref[:, at].astype(F32)).astype(BF16)


def share_kernel(owner_ref, x_ref, router_ref, slots_ref, rows_ref, out_ref):
    logits = lax.dot_general(x_ref[...], router_ref[...], (((1,), (1,)), ((), ())), preferred_element_type=F32)
    experts = router_ref.shape[0]
    rows = rows_ref.shape[0]
    label = lax.broadcasted_iota(jnp.int32, (rows, experts), 1)
    member = (rows_ref[:, 0:1] == label) | (rows_ref[:, 1:2] == label)
    both = dot(slots_ref[owner_ref[0]], member.astype(F32).astype(BF16))
    own = (lax.broadcasted_iota(jnp.int32, both.shape, 1) == owner_ref[0]).astype(F32) * both
    gap = jnp.sum(logits * (2.0 * own - both), axis=1, keepdims=True)
    out_ref[...] = jnp.broadcast_to(jax.nn.sigmoid(gap), out_ref.shape)


def fetched(sources, held, sem):
    copies = [pltpu.make_async_copy(a, b, sem.at[i]) for i, (a, b) in enumerate(zip(sources, held))]
    for copy in copies:
        copy.start()
    return copies


def sliced(source, target, sem, parts, axis):
    size = target.shape[axis] // parts
    at = lambda k: (slice(None),) * axis + (pl.ds(k * size, size),)
    return [pltpu.make_async_copy(source.at[at(k)], target.at[at(k)], sem.at[k]) for k in range(parts)]


def hidden_of(x_held, x_copies, weights, weight_copies, out_ref):
    parts = len(x_copies)
    size = x_held.shape[2] // parts
    totals = None
    for k in range(parts):
        x_copies[k].wait()
        for copies in weight_copies:
            copies[k].wait()
        x = x_held[:, :, k * size : (k + 1) * size].reshape(out_ref.shape[0], size)
        terms = [dot(x, w[k * size : (k + 1) * size, :]) for w in weights]
        totals = terms if totals is None else [a + b for a, b in zip(totals, terms)]
    width = weights[0].shape[1]
    for k in range(2):
        out_ref[:, k * width : (k + 1) * width] = (silu(totals[2 * k]) * totals[2 * k + 1]).astype(BF16)


def first_kernel(parity_ref, x_ref, g0_ref, u0_ref, g1_ref, u1_ref, out_ref, g0, u0, g1, u1, x_held, x_sem, sems):
    parts = x_sem.shape[0]
    x_copies = sliced(x_ref.at[:, 1 - parity_ref[0]], x_held, x_sem, parts, 2)
    held = (g0, u0, g1, u1)
    sources = (g0_ref, u0_ref, g1_ref, u1_ref)
    weight_copies = [sliced(a, b, sems.at[i], parts, 0) for i, (a, b) in enumerate(zip(sources, held))]
    for k in range(parts):
        x_copies[k].start()
        for copies in weight_copies:
            copies[k].start()
    hidden_of(x_held, x_copies, held, weight_copies, out_ref)


def second_kernel(parity_ref, x_ref, g0, u0, g1, u1, *refs):
    sources, out_ref, held, hidden, x_held, x_sem, sem = refs[:6], refs[6], refs[7:9], refs[9:12], refs[12], refs[13], refs[14]
    near, hidden = hidden[:2], hidden[2]
    x_copies = sliced(x_ref.at[:, parity_ref[0]], x_held, x_sem, x_sem.shape[0], 2)
    for copy in x_copies:
        copy.start()
    part = sources[2].shape[0]
    targets = near + tuple(d.at[pl.ds(k * part, part)] for d in held for k in range(2))
    copies = fetched(sources, targets, sem)
    hidden_of(x_held, x_copies, (g0, u0, g1, u1), (), hidden)
    copies[0].wait()
    copies[1].wait()
    width = near[0].shape[0]
    for j in range(0, out_ref.shape[1], 512):
        at = slice(j, j + 512)
        out_ref[:, at] = dot(hidden[:, :width], near[0][:, at]) + dot(hidden[:, width:], near[1][:, at])
    for copy in copies[2:]:
        copy.wait()


def down_kernel(sofar_ref, far_ref, d2, d3, out_ref):
    width = d2.shape[0]
    for j in range(0, out_ref.shape[1], 512):
        at = slice(j, j + 512)
        total = sofar_ref[:, at] + dot(far_ref[:, :width], d2[:, at]) + dot(far_ref[:, width:], d3[:, at])
        out_ref[:, at] = total.astype(BF16)


def weigh_kernel(got_ref, share_ref, out_ref):
    total = got_ref[0].astype(F32)
    for i in range(1, got_ref.shape[0]):
        total = total + got_ref[i].astype(F32)
    out_ref[0] = (total * share_ref[:, :1]).astype(BF16)


def combine_kernel(got_ref, slots_ref, out_ref):
    total = jnp.zeros(out_ref.shape, F32)
    for e in range(got_ref.shape[0]):
        total = total + lax.dot_general(
            slots_ref[e], got_ref[e], (((0,), (0,)), ((), ())), preferred_element_type=F32
        )
    out_ref[...] = total.astype(BF16)


def final_kernel(own_ref, got_ref, out_ref):
    width = got_ref.shape[2]
    for j in range(got_ref.shape[0]):
        total = own_ref[j] + got_ref[j].astype(F32)
        out_ref[:, :, j * width : (j + 1) * width] = total.reshape(out_ref.shape[0], out_ref.shape[1], width)


def shape(dims, dtype=F32):
    return jax.ShapeDtypeStruct(dims, dtype)


SCALAR = pl.BlockSpec(memory_space=pltpu.SMEM)
VM = pl.BlockSpec(memory_space=pltpu.VMEM)


def call(kernel, outs, specs, scratch=(), name=None):
    return pl.pallas_call(
        kernel, out_shape=outs, in_specs=specs, scratch_shapes=list(scratch), compiler_params=WIDE, name=name
    )


def shards(
    layer_input, x_branch, gate_branch, conv_weight, conv_bias, x_proj, dt_proj, dt_bias, a_log, d_skip, carry_state,
    carry_tail, out_proj, steering, refusal, norm_gain, router, specialist_switch_matrix, w_up, w_down, expert_ids,
):
    taps = conv_weight.shape[0]
    length, prompts, channels = x_branch.shape
    rows = length * prompts
    states = a_log.shape[1]
    rank = dt_proj.shape[0]
    d_model = out_proj.shape[1]
    experts = router.shape[1]
    top_count = expert_ids.shape[-1]
    capacity = rows * top_count * 5 // (4 * experts)
    n_seq = lax.axis_size("seq")
    groups = lax.axis_size("expert")
    width = d_model // groups
    own_rows = rows // groups
    place = lax.axis_index("seq").astype(jnp.int32)
    owner = lax.axis_index("expert").astype(jnp.int32)

    near, across = ([(i, i ^ d) for i in range(n_seq)] for d in (1, 2))
    weights = (specialist_switch_matrix[0], w_up[0], w_down[0])
    others = tuple(lax.ppermute(w, "seq", near) for w in weights)

    halo = (taps - 1) * prompts
    x_rows = x_branch.reshape(rows, channels)
    received = lax.ppermute(x_rows[rows - halo :], "seq", [(i, i + 1) for i in range(n_seq - 1)])
    here = (
        a_log.T, carry_state.transpose(0, 2, 1), gate_branch.reshape(rows, channels),
        layer_input.reshape(own_rows, d_model), jnp.stack([place, owner]),
    )

    activated, part = call(
        conv_kernel,
        (shape((rows, channels)), shape((rows, x_proj.shape[1]))),
        [SCALAR] + [VM] * 3 + [pl.BlockSpec(memory_space=pltpu.HBM), VM, pl.BlockSpec(memory_space=pltpu.HBM)],
        [
            pltpu.VMEM((rows + 8, channels), F32),
            pltpu.VMEM(conv_weight.shape, BF16),
            pltpu.VMEM(x_proj.shape[::-1], BF16),
            pltpu.SemaphoreType.DMA((2,)),
        ],
        name="conv",
    )(
        place[None], x_rows, received, carry_tail.reshape(halo, channels),
        pltpu.with_memory_space_constraint(conv_weight, pltpu.HBM), conv_bias[None],
        pltpu.with_memory_space_constraint(x_proj.T, pltpu.HBM),
    )
    part, activated, *here = fence(part, activated, *here)
    summed = exchanged(part, "expert").reshape(groups, own_rows, part.shape[1])
    summed = call(
        functools.partial(sum_kernel, rank),
        shape((groups, own_rows, -(-(rank + 6 * states) // 128) * 128), BF16),
        [VM],
        name="sum",
    )(summed)
    summed, activated, *here = fence(summed, activated, *here)
    projected = exchanged(summed, "expert").reshape(rows, -1)
    projected, activated, *rest = fence(projected, activated, *here, *others)
    (a_log_t, carry_t, gate_rows, own, spot), others = rest[:-3], rest[-3:]
    terms = [projected[:, rank + 2 * states * k : rank + 2 * states * (k + 1)].astype(F32) for k in range(3)]
    bc = (terms[0] + terms[1]) + terms[2]
    bc = jnp.broadcast_to(bc[:, :, None], (rows, 2 * states, 128))
    step, ends = call(
        functools.partial(local_kernel, prompts),
        (shape((rows, channels)), shape((prompts * states + 8, channels), BF16)),
        [VM] * 6,
        name="local",
    )(projected, dt_proj, dt_bias[None], activated, bc, a_log_t)
    ends, step, bc = fence(jnp.broadcast_to(ends[None], (n_seq,) + ends.shape), step, bc)
    every = exchanged(ends, "seq")
    every, step, bc, activated, a_log_t, carry_t, gate_rows, own, down_w = fence(
        every, step, bc, activated, a_log_t, carry_t, gate_rows, own, weights[2]
    )
    part = down_w.shape[0] // 2
    far_a, far_b = (lax.ppermute(down_w[k * part : (k + 1) * part], "seq", across) for k in range(2))
    mixed = call(
        functools.partial(scan_kernel, prompts),
        shape((groups, rows, width), BF16),
        [SCALAR] + [VM] * 9 + [pl.BlockSpec(memory_space=pl.ANY)],
        [pltpu.VMEM((rows, channels), F32), pltpu.VMEM((channels, d_model), BF16), pltpu.SemaphoreType.DMA],
        name="scan",
    )(spot, every, carry_t, step, activated, bc, a_log_t, d_skip[None], gate_rows, own, out_proj)
    mixed, steering, refusal, norm_gain, expert_ids = fence(mixed, steering, refusal, norm_gain, expert_ids)
    mixed = exchanged(mixed, "expert")
    clean = call(clean_kernel, shape((d_model // 128, 128)), [VM] * 2, name="clean")(
        steering.reshape(-1, 128), refusal.reshape(refusal.shape[0], -1, 128)
    )
    start = owner * width
    clean = lax.dynamic_slice_in_dim(clean.reshape(1, d_model), start, width, 1)
    ids = expert_ids.reshape(rows, top_count)

    residual, send, slots = call(
        dispatch_kernel,
        (
            shape((rows, width)),
            shape((experts, capacity, width), BF16),
            shape((experts, capacity, rows), BF16),
        ),
        [VM] * 3,
        name="dispatch",
    )(mixed, clean, ids.T)
    got = exchanged(send, "expert")
    normed = call(normed_kernel, shape((capacity, d_model), BF16), [VM] * 2, name="normed")(got, norm_gain[None])

    same_core = [[i for i in range(n_seq) if i % 2 == c] for c in range(2)]
    normed, far_a = fence(normed, far_a)
    corner_a = lax.ppermute(far_a, "seq", near)
    pieces = lax.all_gather(normed, "seq", axis=0, tiled=True, axis_index_groups=same_core)
    share = call(share_kernel, shape((capacity, 128)), [SCALAR] + [VM] * 4, name="share")(
        owner[None], normed, router.T, slots, ids
    )
    residual, share = fence(residual, share)
    own_residual = exchanged(residual, "expert").reshape(groups, own_rows, width)
    own_residual, share, far_b = fence(own_residual, share, far_b)
    corner_b = lax.ppermute(far_b, "seq", near)
    hbm = pl.BlockSpec(memory_space=pltpu.HBM)
    pieces, own_residual, share, corner_a, corner_b = fence(pieces, own_residual, share, corner_a, corner_b)
    pairs = n_seq // 4
    pieces = pieces.reshape(pairs, 2, capacity, d_model)
    ups = (weights[0], weights[1], others[0], others[1])
    downs = (down_w, others[2], far_a, far_b, corner_a, corner_b)
    half = pairs * capacity
    inner = 2 * ups[0].shape[1]
    dma = pltpu.SemaphoreType.DMA
    parity = ((place // 2) % 2)[None]
    pieces = pltpu.with_memory_space_constraint(pieces, pltpu.HBM)
    parts = 4
    held_rows = [pltpu.VMEM((pairs, capacity, d_model), BF16), dma((parts,))]
    theirs, *ups = pl.pallas_call(
        first_kernel,
        out_shape=(shape((half, inner), BF16),) + tuple(pltpu.VMEM(w.shape, BF16) for w in ups),
        in_specs=[SCALAR] + [hbm] * 5,
        out_specs=(VM,) * 5,
        scratch_shapes=held_rows + [dma((4, parts))],
        compiler_params=pltpu.CompilerParams(vmem_limit_bytes=16 * 1024 * 1024),
        name="first",
    )(parity, pieces, *(pltpu.with_memory_space_constraint(v, pltpu.HBM) for v in ups))
    given = lax.ppermute(theirs, "seq", across)
    sofar, *downs = pl.pallas_call(
        second_kernel,
        out_shape=(pltpu.VMEM((half, d_model), F32),) + (pltpu.VMEM(down_w.shape, BF16),) * 2,
        in_specs=[SCALAR, hbm] + [VM] * 4 + [hbm] * 6,
        out_specs=(VM,) * 3,
        scratch_shapes=[pltpu.VMEM(down_w.shape, BF16)] * 2 + [pltpu.VMEM((half, inner), BF16)] + held_rows + [dma((6,))],
        compiler_params=pltpu.CompilerParams(vmem_limit_bytes=16 * 1024 * 1024),
        cost_estimate=pl.CostEstimate(flops=4 * half * inner * d_model, bytes_accessed=1 << 24, transcendentals=0),
        name="second",
    )(parity, pieces, *ups, *(pltpu.with_memory_space_constraint(v, pltpu.HBM) for v in downs))
    partial = pl.pallas_call(
        down_kernel,
        out_shape=pltpu.VMEM((half, d_model), BF16),
        in_specs=[VM] * 4,
        out_specs=VM,
        compiler_params=pltpu.CompilerParams(vmem_limit_bytes=16 * 1024 * 1024),
        name="down",
    )(sofar, given, *downs)
    kinds = [[i for i in range(n_seq) if i % 4 == k] for k in range(4)]
    partial, share, slots, own_residual = fence(partial, share, slots, own_residual)
    partial = exchanged(partial, "seq", kinds).reshape(pairs, capacity, d_model)
    partial, share, slots, own_residual = fence(partial, share, slots, own_residual)
    weighted = pl.pallas_call(
        weigh_kernel,
        grid=(groups,),
        out_shape=shape((groups, capacity, width), BF16),
        in_specs=[
            pl.BlockSpec((pairs, capacity, width), lambda j: (0, 0, j)),
            pl.BlockSpec((capacity, 128), lambda j: (0, 0)),
        ],
        out_specs=pl.BlockSpec((1, capacity, width), lambda j: (j, 0, 0)),
        compiler_params=WIDE,
        name="weigh",
    )(partial, share)
    back = exchanged(weighted, "expert")
    total = call(combine_kernel, shape((rows, width), BF16), [VM] * 2, name="combine")(back, slots)
    out = exchanged(total, "expert").reshape(groups, own_rows, width)
    return call(final_kernel, shape((own_rows // prompts, prompts, d_model)), [VM] * 2, name="final")(own_residual, out)


def solution(mesh):
    return jax.shard_map(
        shards,
        mesh=mesh,
        in_specs=(
            P(("seq", "expert"), None, None),
            P("seq", None, "expert"),
            P("seq", None, "expert"),
            P(None, "expert"),
            P("expert"),
            P("expert", None),
            P(None, "expert"),
            P("expert"),
            P("expert", None),
            P("expert"),
            P(None, "expert", None),
            P(None, None, "expert"),
            P("expert", None),
            P(),
            P(),
            P(),
            P(),
            P("expert", None, "seq"),
            P("expert", None, "seq"),
            P("expert", "seq", None),
            P("seq", None, None),
        ),
        out_specs=P(("seq", "expert"), None, None),
        check_vma=False,
    )
```

```python
import functools

import jax
import jax.numpy as jnp
from jax import lax
from jax.experimental import pallas as pl
from jax.experimental.pallas import tpu as pltpu
from jax.sharding import PartitionSpec as P

EPS = 1e-06
LOG2E = 1.4426950408889634
F32 = jnp.float32
BF16 = jnp.bfloat16
WIDE = pltpu.CompilerParams(vmem_limit_bytes=40 * 1024 * 1024)


def silu(v):
    return v * jax.nn.sigmoid(v)


def dot(a, b):
    return jnp.dot(a, b, preferred_element_type=F32)


def fence(*values):
    return lax.optimization_barrier(values)


def exchanged(blocks, axis, groups=None):
    return lax.all_to_all(blocks, axis, 0, 0, tiled=True, axis_index_groups=groups)


def conv_kernel(
    lead_ref, x_ref, got_ref, carry_ref, taps_ref, b_ref, proj_ref, act_ref, part_ref, pad_ref, w_ref, xp_ref, sem
):
    copies = [pltpu.make_async_copy(a, b, sem.at[i]) for i, (a, b) in enumerate(((taps_ref, w_ref), (proj_ref, xp_ref)))]
    for copy in copies:
        copy.start()
    rows = x_ref.shape[0]
    taps = w_ref.shape[0]
    halo = got_ref.shape[0]
    step = halo // (taps - 1)
    first = lead_ref[0] == 0
    pad_ref[:halo, :] = jnp.where(first, carry_ref[...].astype(F32), got_ref[...].astype(F32))
    pad_ref[halo : halo + rows, :] = x_ref[...].astype(F32)
    total = b_ref[...].astype(F32)
    copies[0].wait()
    w = w_ref[...].astype(F32)
    for k in range(taps):
        total = total + w[k : k + 1, :] * pad_ref[k * step : k * step + rows, :]
    act = silu(total)
    act_ref[...] = act
    copies[1].wait()
    part_ref[...] = lax.dot_general(act.astype(BF16), xp_ref[...], (((1,), (1,)), ((), ())), preferred_element_type=F32)


def sum_kernel(rank, got_ref, out_ref):
    total = got_ref[0]
    for j in range(1, got_ref.shape[0]):
        total = total + got_ref[j]
    rest = total[:, rank:]
    high = rest.astype(BF16).astype(F32)
    middle = (rest - high).astype(BF16).astype(F32)
    out = [total[:, :rank], high, middle, rest - high - middle]
    pad = out_ref.shape[2] - rank - 3 * rest.shape[1]
    out = jnp.concatenate(out + [jnp.zeros((rest.shape[0], pad), F32)], axis=1).astype(BF16)
    for j in range(out_ref.shape[0]):
        out_ref[j] = out


def advance(state, rate, step, drive, b):
    return jnp.exp2(step * rate) * state + drive * b


def local_kernel(prompts, proj_ref, dtp_ref, dtb_ref, act_ref, bc_ref, alog_ref, step_ref, out_ref):
    rows, channels = act_ref.shape
    states = alog_ref.shape[0]
    rank = dtp_ref.shape[0]
    low = proj_ref[:, :rank]
    step_ref[...] = jax.nn.softplus(dot(low, dtp_ref[...]) + dtb_ref[...])
    rate = -jnp.exp(alog_ref[...]) * LOG2E

    def body(i, carried):
        carried = list(carried)
        at = pl.multiple_of(i * 8, 8)
        step = step_ref[pl.ds(at, 8), :]
        drive = step * act_ref[pl.ds(at, 8), :]
        for r in range(8):
            p = r % prompts
            b = jnp.tile(bc_ref[at + r, :states, :], (1, channels // 128))
            carried[p] = advance(carried[p], rate, step[r : r + 1, :], drive[r : r + 1, :], b)
        return tuple(carried)

    zero = jnp.zeros((states, channels), F32)
    ends = lax.fori_loop(0, rows // 8, body, (zero,) * prompts)
    for p in range(prompts):
        out_ref[p * states : (p + 1) * states, :] = ends[p].astype(BF16)
    step = step_ref[...].reshape(rows // 8, 8, channels).sum(axis=0)
    sums = [sum(step[r : r + 1, :] for r in range(p, 8, prompts)) for p in range(prompts)]
    high = [s.astype(BF16).astype(F32) for s in sums]
    low_part = [(s - h) for s, h in zip(sums, high)]
    rest = jnp.zeros((8 - 2 * prompts, channels), F32)
    out_ref[prompts * states :, :] = jnp.concatenate(high + low_part + [rest], axis=0).astype(BF16)


def scan_kernel(
    prompts, ids_ref, all_ref, carry_ref, step_ref, act_ref, bc_ref, alog_ref, skip_ref, gate_ref, own_ref,
    outp_ref, mixed_ref, y_ref, w_ref, sem,
):
    rows, channels = act_ref.shape
    states = alog_ref.shape[0]
    copy = pltpu.make_async_copy(outp_ref, w_ref, sem)
    copy.start()
    rate = -jnp.exp(alog_ref[...]) * LOG2E

    def earlier(j, carried):
        block = all_ref[j].astype(F32)
        at = prompts * states
        out = []
        for p in range(prompts):
            total = block[at + p : at + p + 1, :] + block[at + prompts + p : at + prompts + p + 1, :]
            out.append(jnp.exp2(total * rate) * carried[p] + block[p * states : (p + 1) * states, :])
        return tuple(out)

    entering = lax.fori_loop(0, ids_ref[0], earlier, tuple(carry_ref[p] for p in range(prompts)))

    def body(i, carried):
        carried = list(carried)
        at = pl.multiple_of(i * 8, 8)
        step = step_ref[pl.ds(at, 8), :]
        drive = step * act_ref[pl.ds(at, 8), :]
        outs = []
        for r in range(8):
            p = r % prompts
            bc = bc_ref[at + r]
            b = jnp.tile(bc[:states], (1, channels // 128))
            c = jnp.tile(bc[states:], (1, channels // 128))
            carried[p] = advance(carried[p], rate, step[r : r + 1, :], drive[r : r + 1, :], b)
            outs.append(jnp.sum(carried[p] * c, axis=0, keepdims=True))
        y_ref[pl.ds(at, 8), :] = jnp.concatenate(outs, axis=0)
        return tuple(carried)

    lax.fori_loop(0, rows // 8, body, entering)
    y = y_ref[...] + skip_ref[...] * act_ref[...]
    gated = (y * silu(gate_ref[...].astype(F32))).astype(BF16)
    copy.wait()
    blocks, _, width = mixed_ref.shape
    own_rows = own_ref.shape[0]
    row_group = lax.broadcasted_iota(jnp.int32, (rows, width), 0) // own_rows
    mine = row_group == ids_ref[1]
    for j in range(blocks):
        part = dot(gated, w_ref[:, j * width : (j + 1) * width])
        own = jnp.tile(own_ref[:, j * width : (j + 1) * width].astype(F32), (rows // own_rows, 1))
        mixed_ref[j] = (part + jnp.where(mine, own, 0.0)).astype(BF16)


def clean_kernel(steer_ref, refusal_ref, out_ref):
    vector = steer_ref[...].astype(F32)
    units = []
    for k in range(refusal_ref.shape[0]):
        r = refusal_ref[k].astype(F32)
        for q in units:
            r = r - jnp.sum(q * r) * q
        r = r * lax.rsqrt(jnp.sum(r * r) + EPS)
        units.append(r)
    for q in units:
        vector = vector - jnp.sum(q * vector) * q
    out_ref[...] = vector


def dispatch_kernel(mixed_ref, clean_ref, lanes_ref, res_ref, send_ref, slots_ref):
    experts, capacity, rows = slots_ref.shape
    width = res_ref.shape[1]
    residual = clean_ref[...]
    for j in range(mixed_ref.shape[0]):
        residual = residual + mixed_ref[j].astype(F32)
    res_ref[...] = residual
    payload = residual.astype(BF16)
    label = lax.broadcasted_iota(jnp.int32, (experts, rows), 0)
    member = (lanes_ref[0:1, :] == label) | (lanes_ref[1:2, :] == label)
    upper = lax.broadcasted_iota(jnp.int32, (rows, rows), 0) <= lax.broadcasted_iota(jnp.int32, (rows, rows), 1)
    order = dot(member.astype(F32).astype(BF16), upper.astype(F32).astype(BF16))
    place = jnp.where(member, order - 1.0, -1.0)
    slot = lax.broadcasted_iota(jnp.int32, (capacity, rows), 0).astype(F32)
    for e in range(experts):
        chosen = (place[e : e + 1, :] == slot).astype(F32).astype(BF16)
        slots_ref[e] = chosen
        send_ref[e] = dot(chosen, payload).astype(BF16)


def normed_kernel(got_ref, gain_ref, out_ref):
    blocks, rows, width = got_ref.shape
    total = jnp.zeros((rows, width), F32)
    for j in range(blocks):
        block = got_ref[j].astype(F32)
        total = total + block * block
    scale = lax.rsqrt(jnp.sum(total, axis=1, keepdims=True) / (blocks * width) + EPS)
    for j in range(blocks):
        at = slice(j * width, (j + 1) * width)
        out_ref[:, at] = (got_ref[j].astype(F32) * scale * gain_ref[:, at].astype(F32)).astype(BF16)


def share_kernel(owner_ref, x_ref, router_ref, slots_ref, rows_ref, out_ref):
    logits = lax.dot_general(x_ref[...], router_ref[...], (((1,), (1,)), ((), ())), preferred_element_type=F32)
    experts = router_ref.shape[0]
    rows = rows_ref.shape[0]
    label = lax.broadcasted_iota(jnp.int32, (rows, experts), 1)
    member = (rows_ref[:, 0:1] == label) | (rows_ref[:, 1:2] == label)
    both = dot(slots_ref[owner_ref[0]], member.astype(F32).astype(BF16))
    own = (lax.broadcasted_iota(jnp.int32, both.shape, 1) == owner_ref[0]).astype(F32) * both
    gap = jnp.sum(logits * (2.0 * own - both), axis=1, keepdims=True)
    out_ref[...] = jnp.broadcast_to(jax.nn.sigmoid(gap), out_ref.shape)


def fetched(sources, held, sem):
    copies = [pltpu.make_async_copy(a, b, sem.at[i]) for i, (a, b) in enumerate(zip(sources, held))]
    for copy in copies:
        copy.start()
    return copies


def sliced(source, target, sem, parts, axis):
    size = target.shape[axis] // parts
    at = lambda k: (slice(None),) * axis + (pl.ds(k * size, size),)
    return [pltpu.make_async_copy(source.at[at(k)], target.at[at(k)], sem.at[k]) for k in range(parts)]


def hidden_of(x_held, x_copies, weights, weight_copies, out_ref):
    parts = len(x_copies)
    size = x_held.shape[2] // parts
    totals = None
    for k in range(parts):
        x_copies[k].wait()
        for copies in weight_copies:
            copies[k].wait()
        x = x_held[:, :, k * size : (k + 1) * size].reshape(out_ref.shape[0], size)
        terms = [dot(x, w[k * size : (k + 1) * size, :]) for w in weights]
        totals = terms if totals is None else [a + b for a, b in zip(totals, terms)]
    width = weights[0].shape[1]
    for k in range(2):
        out_ref[:, k * width : (k + 1) * width] = (silu(totals[2 * k]) * totals[2 * k + 1]).astype(BF16)


def first_kernel(parity_ref, x_ref, g0_ref, u0_ref, g1_ref, u1_ref, out_ref, g0, u0, g1, u1, x_held, x_sem, sems):
    parts = x_sem.shape[0]
    x_copies = sliced(x_ref.at[:, 1 - parity_ref[0]], x_held, x_sem, parts, 2)
    held = (g0, u0, g1, u1)
    sources = (g0_ref, u0_ref, g1_ref, u1_ref)
    weight_copies = [sliced(a, b, sems.at[i], parts, 0) for i, (a, b) in enumerate(zip(sources, held))]
    for k in range(parts):
        x_copies[k].start()
        for copies in weight_copies:
            copies[k].start()
    hidden_of(x_held, x_copies, held, weight_copies, out_ref)


def second_kernel(parity_ref, x_ref, g0, u0, g1, u1, *refs):
    sources, out_ref, held, hidden, x_held, x_sem, sem = refs[:6], refs[6], refs[7:9], refs[9:12], refs[12], refs[13], refs[14]
    near, hidden = hidden[:2], hidden[2]
    x_copies = sliced(x_ref.at[:, parity_ref[0]], x_held, x_sem, x_sem.shape[0], 2)
    for copy in x_copies:
        copy.start()
    part = sources[2].shape[0]
    targets = near + tuple(d.at[pl.ds(k * part, part)] for d in held for k in range(2))
    copies = fetched(sources, targets, sem)
    hidden_of(x_held, x_copies, (g0, u0, g1, u1), (), hidden)
    copies[0].wait()
    copies[1].wait()
    width = near[0].shape[0]
    for j in range(0, out_ref.shape[1], 512):
        at = slice(j, j + 512)
        out_ref[:, at] = dot(hidden[:, :width], near[0][:, at]) + dot(hidden[:, width:], near[1][:, at])
    for copy in copies[2:]:
        copy.wait()


def down_kernel(sofar_ref, far_ref, d2, d3, out_ref):
    width = d2.shape[0]
    for j in range(0, out_ref.shape[1], 512):
        at = slice(j, j + 512)
        total = sofar_ref[:, at] + dot(far_ref[:, :width], d2[:, at]) + dot(far_ref[:, width:], d3[:, at])
        out_ref[:, at] = total.astype(BF16)


def weigh_kernel(got_ref, share_ref, out_ref):
    total = got_ref[0].astype(F32)
    for i in range(1, got_ref.shape[0]):
        total = total + got_ref[i].astype(F32)
    out_ref[0] = (total * share_ref[:, :1]).astype(BF16)


def combine_kernel(got_ref, slots_ref, out_ref):
    total = jnp.zeros(out_ref.shape, F32)
    for e in range(got_ref.shape[0]):
        total = total + lax.dot_general(
            slots_ref[e], got_ref[e], (((0,), (0,)), ((), ())), preferred_element_type=F32
        )
    out_ref[...] = total.astype(BF16)


def final_kernel(own_ref, got_ref, out_ref):
    width = got_ref.shape[2]
    for j in range(got_ref.shape[0]):
        total = own_ref[j] + got_ref[j].astype(F32)
        out_ref[:, :, j * width : (j + 1) * width] = total.reshape(out_ref.shape[0], out_ref.shape[1], width)


def shape(dims, dtype=F32):
    return jax.ShapeDtypeStruct(dims, dtype)


SCALAR = pl.BlockSpec(memory_space=pltpu.SMEM)
VM = pl.BlockSpec(memory_space=pltpu.VMEM)


def call(kernel, outs, specs, scratch=(), name=None):
    return pl.pallas_call(
        kernel, out_shape=outs, in_specs=specs, scratch_shapes=list(scratch), compiler_params=WIDE, name=name
    )


def shards(
    layer_input, x_branch, gate_branch, conv_weight, conv_bias, x_proj, dt_proj, dt_bias, a_log, d_skip, carry_state,
    carry_tail, out_proj, steering, refusal, norm_gain, router, specialist_switch_matrix, w_up, w_down, expert_ids,
):
    taps = conv_weight.shape[0]
    length, prompts, channels = x_branch.shape
    rows = length * prompts
    states = a_log.shape[1]
    rank = dt_proj.shape[0]
    d_model = out_proj.shape[1]
    experts = router.shape[1]
    top_count = expert_ids.shape[-1]
    capacity = rows * top_count * 5 // (4 * experts)
    n_seq = lax.axis_size("seq")
    groups = lax.axis_size("expert")
    width = d_model // groups
    own_rows = rows // groups
    place = lax.axis_index("seq").astype(jnp.int32)
    owner = lax.axis_index("expert").astype(jnp.int32)

    near, across = ([(i, i ^ d) for i in range(n_seq)] for d in (1, 2))
    weights = (specialist_switch_matrix[0], w_up[0], w_down[0])
    others = tuple(lax.ppermute(w, "seq", near) for w in weights)

    halo = (taps - 1) * prompts
    x_rows = x_branch.reshape(rows, channels)
    received = lax.ppermute(x_rows[rows - halo :], "seq", [(i, i + 1) for i in range(n_seq - 1)])
    here = (
        a_log.T, carry_state.transpose(0, 2, 1), gate_branch.reshape(rows, channels),
        layer_input.reshape(own_rows, d_model), jnp.stack([place, owner]),
    )

    activated, part = call(
        conv_kernel,
        (shape((rows, channels)), shape((rows, x_proj.shape[1]))),
        [SCALAR] + [VM] * 3 + [pl.BlockSpec(memory_space=pltpu.HBM), VM, pl.BlockSpec(memory_space=pltpu.HBM)],
        [
            pltpu.VMEM((rows + 8, channels), F32),
            pltpu.VMEM(conv_weight.shape, BF16),
            pltpu.VMEM(x_proj.shape[::-1], BF16),
            pltpu.SemaphoreType.DMA((2,)),
        ],
        name="conv",
    )(
        place[None], x_rows, received, carry_tail.reshape(halo, channels),
        pltpu.with_memory_space_constraint(conv_weight, pltpu.HBM), conv_bias[None],
        pltpu.with_memory_space_constraint(x_proj.T, pltpu.HBM),
    )
    part, activated, *here = fence(part, activated, *here)
    summed = exchanged(part, "expert").reshape(groups, own_rows, part.shape[1])
    summed = call(
        functools.partial(sum_kernel, rank),
        shape((groups, own_rows, -(-(rank + 6 * states) // 128) * 128), BF16),
        [VM],
        name="sum",
    )(summed)
    summed, activated, *here = fence(summed, activated, *here)
    projected = exchanged(summed, "expert").reshape(rows, -1)
    projected, activated, *rest = fence(projected, activated, *here, *others)
    (a_log_t, carry_t, gate_rows, own, spot), others = rest[:-3], rest[-3:]
    terms = [projected[:, rank + 2 * states * k : rank + 2 * states * (k + 1)].astype(F32) for k in range(3)]
    bc = (terms[0] + terms[1]) + terms[2]
    bc = jnp.broadcast_to(bc[:, :, None], (rows, 2 * states, 128))
    step, ends = call(
        functools.partial(local_kernel, prompts),
        (shape((rows, channels)), shape((prompts * states + 8, channels), BF16)),
        [VM] * 6,
        name="local",
    )(projected, dt_proj, dt_bias[None], activated, bc, a_log_t)
    ends, step, bc = fence(jnp.broadcast_to(ends[None], (n_seq,) + ends.shape), step, bc)
    every = exchanged(ends, "seq")
    every, step, bc, activated, a_log_t, carry_t, gate_rows, own, down_w = fence(
        every, step, bc, activated, a_log_t, carry_t, gate_rows, own, weights[2]
    )
    part = down_w.shape[0] // 2
    far_a, far_b = (lax.ppermute(down_w[k * part : (k + 1) * part], "seq", across) for k in range(2))
    mixed = call(
        functools.partial(scan_kernel, prompts),
        shape((groups, rows, width), BF16),
        [SCALAR] + [VM] * 9 + [pl.BlockSpec(memory_space=pl.ANY)],
        [pltpu.VMEM((rows, channels), F32), pltpu.VMEM((channels, d_model), BF16), pltpu.SemaphoreType.DMA],
        name="scan",
    )(spot, every, carry_t, step, activated, bc, a_log_t, d_skip[None], gate_rows, own, out_proj)
    mixed, steering, refusal, norm_gain, expert_ids = fence(mixed, steering, refusal, norm_gain, expert_ids)
    mixed = exchanged(mixed, "expert")
    clean = call(clean_kernel, shape((d_model // 128, 128)), [VM] * 2, name="clean")(
        steering.reshape(-1, 128), refusal.reshape(refusal.shape[0], -1, 128)
    )
    start = owner * width
    clean = lax.dynamic_slice_in_dim(clean.reshape(1, d_model), start, width, 1)
    ids = expert_ids.reshape(rows, top_count)
    gain = norm_gain[None]

    residual, send, slots = call(
        dispatch_kernel,
        (
            shape((rows, width)),
            shape((experts, capacity, width), BF16),
            shape((experts, capacity, rows), BF16),
        ),
        [VM] * 3,
        name="dispatch",
    )(mixed, clean, ids.T)
    send, gain = fence(send, gain)
    got = exchanged(send, "expert")
    normed = call(normed_kernel, shape((capacity, d_model), BF16), [VM] * 2, name="normed")(got, gain)

    same_core = [[i for i in range(n_seq) if i % 2 == c] for c in range(2)]
    normed, far_a = fence(normed, far_a)
    corner_a = lax.ppermute(far_a, "seq", near)
    pieces = lax.all_gather(normed, "seq", axis=0, tiled=True, axis_index_groups=same_core)
    share = call(share_kernel, shape((capacity, 128)), [SCALAR] + [VM] * 4, name="share")(
        owner[None], normed, router.T, slots, ids
    )
    residual, share = fence(residual, share)
    own_residual = exchanged(residual, "expert").reshape(groups, own_rows, width)
    own_residual, share, far_b = fence(own_residual, share, far_b)
    corner_b = lax.ppermute(far_b, "seq", near)
    hbm = pl.BlockSpec(memory_space=pltpu.HBM)
    pieces, own_residual, share, corner_a, corner_b = fence(pieces, own_residual, share, corner_a, corner_b)
    pairs = n_seq // 4
    pieces = pieces.reshape(pairs, 2, capacity, d_model)
    ups = (weights[0], weights[1], others[0], others[1])
    downs = (down_w, others[2], far_a, far_b, corner_a, corner_b)
    half = pairs * capacity
    inner = 2 * ups[0].shape[1]
    dma = pltpu.SemaphoreType.DMA
    parity = ((place // 2) % 2)[None]
    pieces = pltpu.with_memory_space_constraint(pieces, pltpu.HBM)
    parts = 4
    held_rows = [pltpu.VMEM((pairs, capacity, d_model), BF16), dma((parts,))]
    theirs, *ups = pl.pallas_call(
        first_kernel,
        out_shape=(shape((half, inner), BF16),) + tuple(pltpu.VMEM(w.shape, BF16) for w in ups),
        in_specs=[SCALAR] + [hbm] * 5,
        out_specs=(VM,) * 5,
        scratch_shapes=held_rows + [dma((4, parts))],
        compiler_params=pltpu.CompilerParams(vmem_limit_bytes=16 * 1024 * 1024),
        name="first",
    )(parity, pieces, *(pltpu.with_memory_space_constraint(v, pltpu.HBM) for v in ups))
    given = lax.ppermute(theirs, "seq", across)
    sofar, *downs = pl.pallas_call(
        second_kernel,
        out_shape=(pltpu.VMEM((half, d_model), F32),) + (pltpu.VMEM(down_w.shape, BF16),) * 2,
        in_specs=[SCALAR, hbm] + [VM] * 4 + [hbm] * 6,
        out_specs=(VM,) * 3,
        scratch_shapes=[pltpu.VMEM(down_w.shape, BF16)] * 2 + [pltpu.VMEM((half, inner), BF16)] + held_rows + [dma((6,))],
        compiler_params=pltpu.CompilerParams(vmem_limit_bytes=16 * 1024 * 1024),
        cost_estimate=pl.CostEstimate(flops=4 * half * inner * d_model, bytes_accessed=1 << 24, transcendentals=0),
        name="second",
    )(parity, pieces, *ups, *(pltpu.with_memory_space_constraint(v, pltpu.HBM) for v in downs))
    partial = pl.pallas_call(
        down_kernel,
        out_shape=pltpu.VMEM((half, d_model), BF16),
        in_specs=[VM] * 4,
        out_specs=VM,
        compiler_params=pltpu.CompilerParams(vmem_limit_bytes=16 * 1024 * 1024),
        name="down",
    )(sofar, given, *downs)
    kinds = [[i for i in range(n_seq) if i % 4 == k] for k in range(4)]
    partial, share, slots, own_residual = fence(partial, share, slots, own_residual)
    partial = exchanged(partial, "seq", kinds).reshape(pairs, capacity, d_model)
    partial, share, slots, own_residual = fence(partial, share, slots, own_residual)
    weighted = pl.pallas_call(
        weigh_kernel,
        grid=(groups,),
        out_shape=shape((groups, capacity, width), BF16),
        in_specs=[
            pl.BlockSpec((pairs, capacity, width), lambda j: (0, 0, j)),
            pl.BlockSpec((capacity, 128), lambda j: (0, 0)),
        ],
        out_specs=pl.BlockSpec((1, capacity, width), lambda j: (j, 0, 0)),
        compiler_params=WIDE,
        name="weigh",
    )(partial, share)
    back = exchanged(weighted, "expert")
    total = call(combine_kernel, shape((rows, width), BF16), [VM] * 2, name="combine")(back, slots)
    out = exchanged(total, "expert").reshape(groups, own_rows, width)
    return call(final_kernel, shape((own_rows // prompts, prompts, d_model)), [VM] * 2, name="final")(own_residual, out)


def solution(mesh):
    return jax.shard_map(
        shards,
        mesh=mesh,
        in_specs=(
            P(("seq", "expert"), None, None),
            P("seq", None, "expert"),
            P("seq", None, "expert"),
            P(None, "expert"),
            P("expert"),
            P("expert", None),
            P(None, "expert"),
            P("expert"),
            P("expert", None),
            P("expert"),
            P(None, "expert", None),
            P(None, None, "expert"),
            P("expert", None),
            P(),
            P(),
            P(),
            P(),
            P("expert", None, "seq"),
            P("expert", None, "seq"),
            P("expert", "seq", None),
            P("seq", None, None),
        ),
        out_specs=P(("seq", "expert"), None, None),
        check_vma=False,
    )
```

```python
import functools

import jax
import jax.numpy as jnp
from jax import lax
from jax.experimental import pallas as pl
from jax.experimental.pallas import tpu as pltpu
from jax.sharding import PartitionSpec as P

EPS = 1e-06
LOG2E = 1.4426950408889634
F32 = jnp.float32
BF16 = jnp.bfloat16
WIDE = pltpu.CompilerParams(vmem_limit_bytes=40 * 1024 * 1024)


def silu(v):
    return v * jax.nn.sigmoid(v)


def dot(a, b):
    return jnp.dot(a, b, preferred_element_type=F32)


def fence(*values):
    return lax.optimization_barrier(values)


def exchanged(blocks, axis, groups=None):
    return lax.all_to_all(blocks, axis, 0, 0, tiled=True, axis_index_groups=groups)


def conv_kernel(
    lead_ref, x_ref, got_ref, carry_ref, taps_ref, b_ref, proj_ref, act_ref, part_ref, pad_ref, w_ref, xp_ref, sem
):
    copies = [pltpu.make_async_copy(a, b, sem.at[i]) for i, (a, b) in enumerate(((taps_ref, w_ref), (proj_ref, xp_ref)))]
    for copy in copies:
        copy.start()
    rows = x_ref.shape[0]
    taps = w_ref.shape[0]
    halo = got_ref.shape[0]
    step = halo // (taps - 1)
    first = lead_ref[0] == 0
    pad_ref[:halo, :] = jnp.where(first, carry_ref[...].astype(F32), got_ref[...].astype(F32))
    pad_ref[halo : halo + rows, :] = x_ref[...].astype(F32)
    total = b_ref[...].astype(F32)
    copies[0].wait()
    w = w_ref[...].astype(F32)
    for k in range(taps):
        total = total + w[k : k + 1, :] * pad_ref[k * step : k * step + rows, :]
    act = silu(total)
    act_ref[...] = act
    copies[1].wait()
    part_ref[...] = lax.dot_general(act.astype(BF16), xp_ref[...], (((1,), (1,)), ((), ())), preferred_element_type=F32)


def sum_kernel(rank, got_ref, out_ref):
    total = got_ref[0]
    for j in range(1, got_ref.shape[0]):
        total = total + got_ref[j]
    rest = total[:, rank:]
    high = rest.astype(BF16).astype(F32)
    middle = (rest - high).astype(BF16).astype(F32)
    out = [total[:, :rank], high, middle, rest - high - middle]
    pad = out_ref.shape[2] - rank - 3 * rest.shape[1]
    out = jnp.concatenate(out + [jnp.zeros((rest.shape[0], pad), F32)], axis=1).astype(BF16)
    for j in range(out_ref.shape[0]):
        out_ref[j] = out


def advance(state, rate, step, drive, b):
    return jnp.exp2(step * rate) * state + drive * b


def local_kernel(prompts, proj_ref, dtp_ref, dtb_ref, act_ref, bc_ref, alog_ref, step_ref, out_ref):
    rows, channels = act_ref.shape
    states = alog_ref.shape[0]
    rank = dtp_ref.shape[0]
    low = proj_ref[:, :rank]
    step_ref[...] = jax.nn.softplus(dot(low, dtp_ref[...]) + dtb_ref[...])
    rate = -jnp.exp(alog_ref[...]) * LOG2E

    def body(i, carried):
        carried = list(carried)
        at = pl.multiple_of(i * 8, 8)
        step = step_ref[pl.ds(at, 8), :]
        drive = step * act_ref[pl.ds(at, 8), :]
        for r in range(8):
            p = r % prompts
            b = jnp.tile(bc_ref[at + r, :states, :], (1, channels // 128))
            carried[p] = advance(carried[p], rate, step[r : r + 1, :], drive[r : r + 1, :], b)
        return tuple(carried)

    zero = jnp.zeros((states, channels), F32)
    ends = lax.fori_loop(0, rows // 8, body, (zero,) * prompts)
    for p in range(prompts):
        out_ref[p * states : (p + 1) * states, :] = ends[p].astype(BF16)
    step = step_ref[...].reshape(rows // 8, 8, channels).sum(axis=0)
    sums = [sum(step[r : r + 1, :] for r in range(p, 8, prompts)) for p in range(prompts)]
    high = [s.astype(BF16).astype(F32) for s in sums]
    low_part = [(s - h) for s, h in zip(sums, high)]
    rest = jnp.zeros((8 - 2 * prompts, channels), F32)
    out_ref[prompts * states :, :] = jnp.concatenate(high + low_part + [rest], axis=0).astype(BF16)


def scan_kernel(
    prompts, ids_ref, all_ref, carry_ref, step_ref, act_ref, bc_ref, alog_ref, skip_ref, gate_ref, own_ref,
    outp_ref, mixed_ref, y_ref, w_ref, sem,
):
    rows, channels = act_ref.shape
    states = alog_ref.shape[0]
    copy = pltpu.make_async_copy(outp_ref, w_ref, sem)
    copy.start()
    rate = -jnp.exp(alog_ref[...]) * LOG2E

    def earlier(j, carried):
        block = all_ref[j].astype(F32)
        at = prompts * states
        out = []
        for p in range(prompts):
            total = block[at + p : at + p + 1, :] + block[at + prompts + p : at + prompts + p + 1, :]
            out.append(jnp.exp2(total * rate) * carried[p] + block[p * states : (p + 1) * states, :])
        return tuple(out)

    entering = lax.fori_loop(0, ids_ref[0], earlier, tuple(carry_ref[p] for p in range(prompts)))

    def body(i, carried):
        carried = list(carried)
        at = pl.multiple_of(i * 8, 8)
        step = step_ref[pl.ds(at, 8), :]
        drive = step * act_ref[pl.ds(at, 8), :]
        outs = []
        for r in range(8):
            p = r % prompts
            bc = bc_ref[at + r]
            b = jnp.tile(bc[:states], (1, channels // 128))
            c = jnp.tile(bc[states:], (1, channels // 128))
            carried[p] = advance(carried[p], rate, step[r : r + 1, :], drive[r : r + 1, :], b)
            outs.append(jnp.sum(carried[p] * c, axis=0, keepdims=True))
        y_ref[pl.ds(at, 8), :] = jnp.concatenate(outs, axis=0)
        return tuple(carried)

    lax.fori_loop(0, rows // 8, body, entering)
    y = y_ref[...] + skip_ref[...] * act_ref[...]
    gated = (y * silu(gate_ref[...].astype(F32))).astype(BF16)
    copy.wait()
    blocks, _, width = mixed_ref.shape
    own_rows = own_ref.shape[0]
    row_group = lax.broadcasted_iota(jnp.int32, (rows, width), 0) // own_rows
    mine = row_group == ids_ref[1]
    for j in range(blocks):
        part = dot(gated, w_ref[:, j * width : (j + 1) * width])
        own = jnp.tile(own_ref[:, j * width : (j + 1) * width].astype(F32), (rows // own_rows, 1))
        mixed_ref[j] = (part + jnp.where(mine, own, 0.0)).astype(BF16)


def clean_kernel(steer_ref, refusal_ref, out_ref):
    vector = steer_ref[...].astype(F32)
    units = []
    for k in range(refusal_ref.shape[0]):
        r = refusal_ref[k].astype(F32)
        for q in units:
            r = r - jnp.sum(q * r) * q
        r = r * lax.rsqrt(jnp.sum(r * r) + EPS)
        units.append(r)
    for q in units:
        vector = vector - jnp.sum(q * vector) * q
    out_ref[...] = vector


def dispatch_kernel(mixed_ref, clean_ref, lanes_ref, res_ref, send_ref, slots_ref):
    experts, capacity, rows = slots_ref.shape
    width = res_ref.shape[1]
    residual = clean_ref[...]
    for j in range(mixed_ref.shape[0]):
        residual = residual + mixed_ref[j].astype(F32)
    res_ref[...] = residual
    payload = residual.astype(BF16)
    label = lax.broadcasted_iota(jnp.int32, (experts, rows), 0)
    member = (lanes_ref[0:1, :] == label) | (lanes_ref[1:2, :] == label)
    upper = lax.broadcasted_iota(jnp.int32, (rows, rows), 0) <= lax.broadcasted_iota(jnp.int32, (rows, rows), 1)
    order = dot(member.astype(F32).astype(BF16), upper.astype(F32).astype(BF16))
    place = jnp.where(member, order - 1.0, -1.0)
    slot = lax.broadcasted_iota(jnp.int32, (capacity, rows), 0).astype(F32)
    for e in range(experts):
        chosen = (place[e : e + 1, :] == slot).astype(F32).astype(BF16)
        slots_ref[e] = chosen
        send_ref[e] = dot(chosen, payload).astype(BF16)


def normed_kernel(got_ref, gain_ref, out_ref):
    blocks, rows, width = got_ref.shape
    total = jnp.zeros((rows, width), F32)
    for j in range(blocks):
        block = got_ref[j].astype(F32)
        total = total + block * block
    scale = lax.rsqrt(jnp.sum(total, axis=1, keepdims=True) / (blocks * width) + EPS)
    for j in range(blocks):
        at = slice(j * width, (j + 1) * width)
        out_ref[:, at] = (got_ref[j].astype(F32) * scale * gain_ref[:, at].astype(F32)).astype(BF16)


def share_kernel(owner_ref, x_ref, router_ref, slots_ref, rows_ref, out_ref):
    logits = lax.dot_general(x_ref[...], router_ref[...], (((1,), (1,)), ((), ())), preferred_element_type=F32)
    experts = router_ref.shape[0]
    rows = rows_ref.shape[0]
    label = lax.broadcasted_iota(jnp.int32, (rows, experts), 1)
    member = (rows_ref[:, 0:1] == label) | (rows_ref[:, 1:2] == label)
    both = dot(slots_ref[owner_ref[0]], member.astype(F32).astype(BF16))
    own = (lax.broadcasted_iota(jnp.int32, both.shape, 1) == owner_ref[0]).astype(F32) * both
    gap = jnp.sum(logits * (2.0 * own - both), axis=1, keepdims=True)
    out_ref[...] = jnp.broadcast_to(jax.nn.sigmoid(gap), out_ref.shape)


def fetched(sources, held, sem):
    copies = [pltpu.make_async_copy(a, b, sem.at[i]) for i, (a, b) in enumerate(zip(sources, held))]
    for copy in copies:
        copy.start()
    return copies


def sliced(source, target, sem, parts, axis):
    size = target.shape[axis] // parts
    at = lambda k: (slice(None),) * axis + (pl.ds(k * size, size),)
    return [pltpu.make_async_copy(source.at[at(k)], target.at[at(k)], sem.at[k]) for k in range(parts)]


def hidden_of(x_held, x_copies, weights, weight_copies, out_ref):
    parts = len(x_copies)
    size = x_held.shape[2] // parts
    totals = None
    for k in range(parts):
        x_copies[k].wait()
        for copies in weight_copies:
            copies[k].wait()
        x = x_held[:, :, k * size : (k + 1) * size].reshape(out_ref.shape[0], size)
        terms = [dot(x, w[k * size : (k + 1) * size, :]) for w in weights]
        totals = terms if totals is None else [a + b for a, b in zip(totals, terms)]
    width = weights[0].shape[1]
    for k in range(2):
        out_ref[:, k * width : (k + 1) * width] = (silu(totals[2 * k]) * totals[2 * k + 1]).astype(BF16)


def first_kernel(parity_ref, x_ref, g0_ref, u0_ref, g1_ref, u1_ref, out_ref, g0, u0, g1, u1, x_held, x_sem, sems):
    parts = x_sem.shape[0]
    x_copies = sliced(x_ref.at[:, 1 - parity_ref[0]], x_held, x_sem, parts, 2)
    held = (g0, u0, g1, u1)
    sources = (g0_ref, u0_ref, g1_ref, u1_ref)
    weight_copies = [sliced(a, b, sems.at[i], parts, 0) for i, (a, b) in enumerate(zip(sources, held))]
    for k in range(parts):
        x_copies[k].start()
        for copies in weight_copies:
            copies[k].start()
    hidden_of(x_held, x_copies, held, weight_copies, out_ref)


def second_kernel(parity_ref, x_ref, g0, u0, g1, u1, *refs):
    sources, out_ref, held, hidden, x_held, x_sem, sem = refs[:6], refs[6], refs[7:9], refs[9:12], refs[12], refs[13], refs[14]
    near, hidden = hidden[:2], hidden[2]
    x_copies = sliced(x_ref.at[:, parity_ref[0]], x_held, x_sem, x_sem.shape[0], 2)
    for copy in x_copies:
        copy.start()
    part = sources[2].shape[0]
    targets = near + tuple(d.at[pl.ds(k * part, part)] for d in held for k in range(2))
    copies = fetched(sources, targets, sem)
    hidden_of(x_held, x_copies, (g0, u0, g1, u1), (), hidden)
    copies[0].wait()
    copies[1].wait()
    width = near[0].shape[0]
    for j in range(0, out_ref.shape[1], 512):
        at = slice(j, j + 512)
        out_ref[:, at] = dot(hidden[:, :width], near[0][:, at]) + dot(hidden[:, width:], near[1][:, at])
    for copy in copies[2:]:
        copy.wait()


def down_kernel(sofar_ref, far_ref, d2, d3, out_ref):
    width = d2.shape[0]
    for j in range(0, out_ref.shape[1], 512):
        at = slice(j, j + 512)
        total = sofar_ref[:, at] + dot(far_ref[:, :width], d2[:, at]) + dot(far_ref[:, width:], d3[:, at])
        out_ref[:, at] = total.astype(BF16)


def weigh_kernel(got_ref, share_ref, out_ref):
    total = got_ref[0].astype(F32)
    for i in range(1, got_ref.shape[0]):
        total = total + got_ref[i].astype(F32)
    out_ref[0] = (total * share_ref[:, :1]).astype(BF16)


def combine_kernel(got_ref, slots_ref, out_ref):
    total = jnp.zeros(out_ref.shape, F32)
    for e in range(got_ref.shape[0]):
        total = total + lax.dot_general(
            slots_ref[e], got_ref[e], (((0,), (0,)), ((), ())), preferred_element_type=F32
        )
    out_ref[...] = total.astype(BF16)


def final_kernel(own_ref, got_ref, out_ref):
    width = got_ref.shape[2]
    for j in range(got_ref.shape[0]):
        total = own_ref[j] + got_ref[j].astype(F32)
        out_ref[:, :, j * width : (j + 1) * width] = total.reshape(out_ref.shape[0], out_ref.shape[1], width)


def shape(dims, dtype=F32):
    return jax.ShapeDtypeStruct(dims, dtype)


SCALAR = pl.BlockSpec(memory_space=pltpu.SMEM)
VM = pl.BlockSpec(memory_space=pltpu.VMEM)


def call(kernel, outs, specs, scratch=(), name=None):
    return pl.pallas_call(
        kernel, out_shape=outs, in_specs=specs, scratch_shapes=list(scratch), compiler_params=WIDE, name=name
    )


def shards(
    layer_input, x_branch, gate_branch, conv_weight, conv_bias, x_proj, dt_proj, dt_bias, a_log, d_skip, carry_state,
    carry_tail, out_proj, steering, refusal, norm_gain, router, specialist_switch_matrix, w_up, w_down, expert_ids,
):
    taps = conv_weight.shape[0]
    length, prompts, channels = x_branch.shape
    rows = length * prompts
    states = a_log.shape[1]
    rank = dt_proj.shape[0]
    d_model = out_proj.shape[1]
    experts = router.shape[1]
    top_count = expert_ids.shape[-1]
    capacity = rows * top_count * 5 // (4 * experts)
    n_seq = lax.axis_size("seq")
    groups = lax.axis_size("expert")
    width = d_model // groups
    own_rows = rows // groups
    place = lax.axis_index("seq").astype(jnp.int32)
    owner = lax.axis_index("expert").astype(jnp.int32)

    near, across = ([(i, i ^ d) for i in range(n_seq)] for d in (1, 2))
    weights = (specialist_switch_matrix[0], w_up[0], w_down[0])
    others = tuple(lax.ppermute(w, "seq", near) for w in weights)

    halo = (taps - 1) * prompts
    x_rows = x_branch.reshape(rows, channels)
    received = lax.ppermute(x_rows[rows - halo :], "seq", [(i, i + 1) for i in range(n_seq - 1)])
    here = (
        a_log.T, carry_state.transpose(0, 2, 1), gate_branch.reshape(rows, channels),
        layer_input.reshape(own_rows, d_model), jnp.stack([place, owner]),
    )

    activated, part = call(
        conv_kernel,
        (shape((rows, channels)), shape((rows, x_proj.shape[1]))),
        [SCALAR] + [VM] * 3 + [pl.BlockSpec(memory_space=pltpu.HBM), VM, pl.BlockSpec(memory_space=pltpu.HBM)],
        [
            pltpu.VMEM((rows + 8, channels), F32),
            pltpu.VMEM(conv_weight.shape, BF16),
            pltpu.VMEM(x_proj.shape[::-1], BF16),
            pltpu.SemaphoreType.DMA((2,)),
        ],
        name="conv",
    )(
        place[None], x_rows, received, carry_tail.reshape(halo, channels),
        pltpu.with_memory_space_constraint(conv_weight, pltpu.HBM), conv_bias[None],
        pltpu.with_memory_space_constraint(x_proj.T, pltpu.HBM),
    )
    part, activated, *here = fence(part, activated, *here)
    summed = exchanged(part, "expert").reshape(groups, own_rows, part.shape[1])
    summed = call(
        functools.partial(sum_kernel, rank),
        shape((groups, own_rows, -(-(rank + 6 * states) // 128) * 128), BF16),
        [VM],
        name="sum",
    )(summed)
    summed, activated, *here = fence(summed, activated, *here)
    projected = exchanged(summed, "expert").reshape(rows, -1)
    projected, activated, *rest = fence(projected, activated, *here, *others)
    (a_log_t, carry_t, gate_rows, own, spot), others = rest[:-3], rest[-3:]
    terms = [projected[:, rank + 2 * states * k : rank + 2 * states * (k + 1)].astype(F32) for k in range(3)]
    bc = (terms[0] + terms[1]) + terms[2]
    bc = jnp.broadcast_to(bc[:, :, None], (rows, 2 * states, 128))
    step, ends = call(
        functools.partial(local_kernel, prompts),
        (shape((rows, channels)), shape((prompts * states + 8, channels), BF16)),
        [VM] * 6,
        name="local",
    )(projected, dt_proj, dt_bias[None], activated, bc, a_log_t)
    ends, step, bc = fence(jnp.broadcast_to(ends[None], (n_seq,) + ends.shape), step, bc)
    every = exchanged(ends, "seq")
    every, step, bc, activated, a_log_t, carry_t, gate_rows, own, down_w = fence(
        every, step, bc, activated, a_log_t, carry_t, gate_rows, own, weights[2]
    )
    part = down_w.shape[0] // 2
    far_a, far_b = (lax.ppermute(down_w[k * part : (k + 1) * part], "seq", across) for k in range(2))
    mixed = call(
        functools.partial(scan_kernel, prompts),
        shape((groups, rows, width), BF16),
        [SCALAR] + [VM] * 9 + [pl.BlockSpec(memory_space=pl.ANY)],
        [pltpu.VMEM((rows, channels), F32), pltpu.VMEM((channels, d_model), BF16), pltpu.SemaphoreType.DMA],
        name="scan",
    )(spot, every, carry_t, step, activated, bc, a_log_t, d_skip[None], gate_rows, own, out_proj)
    mixed, steering, refusal, norm_gain, expert_ids = fence(mixed, steering, refusal, norm_gain, expert_ids)
    mixed = exchanged(mixed, "expert")
    clean = call(clean_kernel, shape((d_model // 128, 128)), [VM] * 2, name="clean")(
        steering.reshape(-1, 128), refusal.reshape(refusal.shape[0], -1, 128)
    )
    start = owner * width
    clean = lax.dynamic_slice_in_dim(clean.reshape(1, d_model), start, width, 1)
    ids = expert_ids.reshape(rows, top_count)
    gain = norm_gain[None]

    residual, send, slots = call(
        dispatch_kernel,
        (
            shape((rows, width)),
            shape((experts, capacity, width), BF16),
            shape((experts, capacity, rows), BF16),
        ),
        [VM] * 3,
        name="dispatch",
    )(mixed, clean, ids.T)
    send, gain = fence(send, gain)
    got = exchanged(send, "expert")
    normed = call(normed_kernel, shape((capacity, d_model), BF16), [VM] * 2, name="normed")(got, gain)

    same_core = [[i for i in range(n_seq) if i % 2 == c] for c in range(2)]
    normed, far_a = fence(normed, far_a)
    corner_a = lax.ppermute(far_a, "seq", near)
    pieces = lax.all_gather(normed, "seq", axis=0, tiled=True, axis_index_groups=same_core)
    share = call(share_kernel, shape((capacity, 128)), [SCALAR] + [VM] * 4, name="share")(
        owner[None], normed, router.T, slots, ids
    )
    residual, share = fence(residual, share)
    own_residual = exchanged(residual, "expert").reshape(groups, own_rows, width)
    own_residual, share, far_b = fence(own_residual, share, far_b)
    corner_b = lax.ppermute(far_b, "seq", near)
    hbm = pl.BlockSpec(memory_space=pltpu.HBM)
    pieces, own_residual, share, corner_a, corner_b = fence(pieces, own_residual, share, corner_a, corner_b)
    pairs = n_seq // 4
    pieces = pieces.reshape(pairs, 2, capacity, d_model)
    ups = (weights[0], weights[1], others[0], others[1])
    downs = (down_w, others[2], far_a, far_b, corner_a, corner_b)
    half = pairs * capacity
    inner = 2 * ups[0].shape[1]
    dma = pltpu.SemaphoreType.DMA
    parity = ((place // 2) % 2)[None]
    pieces = pltpu.with_memory_space_constraint(pieces, pltpu.HBM)
    parts = 8
    held_rows = [pltpu.VMEM((pairs, capacity, d_model), BF16), dma((parts,))]
    theirs, *ups = pl.pallas_call(
        first_kernel,
        out_shape=(shape((half, inner), BF16),) + tuple(pltpu.VMEM(w.shape, BF16) for w in ups),
        in_specs=[SCALAR] + [hbm] * 5,
        out_specs=(VM,) * 5,
        scratch_shapes=held_rows + [dma((4, parts))],
        compiler_params=pltpu.CompilerParams(vmem_limit_bytes=16 * 1024 * 1024),
        name="first",
    )(parity, pieces, *(pltpu.with_memory_space_constraint(v, pltpu.HBM) for v in ups))
    given = lax.ppermute(theirs, "seq", across)
    sofar, *downs = pl.pallas_call(
        second_kernel,
        out_shape=(pltpu.VMEM((half, d_model), F32),) + (pltpu.VMEM(down_w.shape, BF16),) * 2,
        in_specs=[SCALAR, hbm] + [VM] * 4 + [hbm] * 6,
        out_specs=(VM,) * 3,
        scratch_shapes=[pltpu.VMEM(down_w.shape, BF16)] * 2 + [pltpu.VMEM((half, inner), BF16)] + held_rows + [dma((6,))],
        compiler_params=pltpu.CompilerParams(vmem_limit_bytes=16 * 1024 * 1024),
        cost_estimate=pl.CostEstimate(flops=4 * half * inner * d_model, bytes_accessed=1 << 24, transcendentals=0),
        name="second",
    )(parity, pieces, *ups, *(pltpu.with_memory_space_constraint(v, pltpu.HBM) for v in downs))
    partial = pl.pallas_call(
        down_kernel,
        out_shape=pltpu.VMEM((half, d_model), BF16),
        in_specs=[VM] * 4,
        out_specs=VM,
        compiler_params=pltpu.CompilerParams(vmem_limit_bytes=16 * 1024 * 1024),
        name="down",
    )(sofar, given, *downs)
    kinds = [[i for i in range(n_seq) if i % 4 == k] for k in range(4)]
    partial, share, slots, own_residual = fence(partial, share, slots, own_residual)
    partial = exchanged(partial, "seq", kinds).reshape(pairs, capacity, d_model)
    partial, share, slots, own_residual = fence(partial, share, slots, own_residual)
    weighted = pl.pallas_call(
        weigh_kernel,
        grid=(groups,),
        out_shape=shape((groups, capacity, width), BF16),
        in_specs=[
            pl.BlockSpec((pairs, capacity, width), lambda j: (0, 0, j)),
            pl.BlockSpec((capacity, 128), lambda j: (0, 0)),
        ],
        out_specs=pl.BlockSpec((1, capacity, width), lambda j: (j, 0, 0)),
        compiler_params=WIDE,
        name="weigh",
    )(partial, share)
    back = exchanged(weighted, "expert")
    total = call(combine_kernel, shape((rows, width), BF16), [VM] * 2, name="combine")(back, slots)
    out = exchanged(total, "expert").reshape(groups, own_rows, width)
    return call(final_kernel, shape((own_rows // prompts, prompts, d_model)), [VM] * 2, name="final")(own_residual, out)


def solution(mesh):
    return jax.shard_map(
        shards,
        mesh=mesh,
        in_specs=(
            P(("seq", "expert"), None, None),
            P("seq", None, "expert"),
            P("seq", None, "expert"),
            P(None, "expert"),
            P("expert"),
            P("expert", None),
            P(None, "expert"),
            P("expert"),
            P("expert", None),
            P("expert"),
            P(None, "expert", None),
            P(None, None, "expert"),
            P("expert", None),
            P(),
            P(),
            P(),
            P(),
            P("expert", None, "seq"),
            P("expert", None, "seq"),
            P("expert", "seq", None),
            P("seq", None, None),
        ),
        out_specs=P(("seq", "expert"), None, None),
        check_vma=False,
    )
```
